32 devices in a mesh: dp: 2 (over x), rows: 4 (over z), heads: 4 (over y, core).
Axes of the slice: x: 2, y: 2, z: 4, core: 2. Of those that a mesh axis runs over, the one named last changes fastest.
Arguments:
- pixels: float32 [64, 2, 64, 512], P(('rows', 'heads'), 'dp'), may hold values from -6 to 6
- crop_slot: int32 [64, 2], P(None, 'dp'), may hold values from 0 to 1, as said below
- embedding: float32 [2, 2, 2048], P('dp'), may hold values from -6 to 6
- context: bfloat16 [2, 2, 81, 2048], P('dp'), may hold values from -6 to 6
- first_gain: float32 [512], replicated, may hold values from 0.1 to 1.9
- first_offset: float32 [512], replicated, may hold values from -1.75 to 1.75
- first_kernel: bfloat16 [3, 3, 512, 512], replicated, may hold values from -0.09375 to 0.09375
- first_bias: float32 [512], replicated, may hold values from -1.75 to 1.75
- embed_weight: bfloat16 [2048, 1024], replicated, may hold values from -0.125 to 0.125
- embed_bias: float32 [1024], replicated, may hold values from -1.75 to 1.75
- second_gain: float32 [512], replicated, may hold values from 0.1 to 1.9
- second_offset: float32 [512], replicated, may hold values from -1.75 to 1.75
- second_kernel: bfloat16 [3, 3, 512, 512], replicated, may hold values from -0.09375 to 0.09375
- second_bias: float32 [512], replicated, may hold values from -1.75 to 1.75
- attend_gain: float32 [512], replicated, may hold values from 0.1 to 1.9
- attend_offset: float32 [512], replicated, may hold values from -1.75 to 1.75
- inner_weight: bfloat16 [512, 3, 8, 64], P(None, None, 'heads'), may hold values from -0.25 to 0.25
- inner_bias: float32 [2, 8, 64], P(None, 'heads'), may hold values from -1.75 to 1.75
- context_weight: bfloat16 [2048, 2, 8, 64], P(None, None, 'heads'), may hold values from -0.125 to 0.125
- context_bias: float32 [8, 64], P('heads'), may hold values from -1.75 to 1.75
- outer_weight: bfloat16 [8, 64, 512], P('heads'), may hold values from -2 to 2
- outer_bias: float32 [512], replicated, may hold values from -1.75 to 1.75
- cotangent: float32 [64, 2, 64, 512], P(('rows', 'heads'), 'dp'), may hold values from -6 to 6
Outputs:
- output: float32 [64, 2, 64, 512], P(('rows', 'heads'), 'dp')
- pixels_grad: float32 [64, 2, 64, 512], P(('rows', 'heads'), 'dp')
- first_gain_grad: float32 [512], replicated
- first_offset_grad: float32 [512], replicated
- first_kernel_grad: float32 [3, 3, 512, 512], P(None, None, ('rows', 'heads'), 'dp')
- first_bias_grad: float32 [512], replicated
- embed_weight_grad: float32 [2048, 1024], P(('rows', 'heads'), 'dp')
- embed_bias_grad: float32 [1024], replicated
- second_gain_grad: float32 [512], replicated
- second_offset_grad: float32 [512], replicated
- second_kernel_grad: float32 [3, 3, 512, 512], P(None, None, ('rows', 'heads'), 'dp')
- second_bias_grad: float32 [512], replicated
- attend_gain_grad: float32 [512], replicated
- attend_offset_grad: float32 [512], replicated
- inner_weight_grad: float32 [512, 3, 8, 64], P(None, None, 'heads')
- inner_bias_grad: float32 [2, 8, 64], P(None, 'heads')
- context_weight_grad: float32 [2048, 2, 8, 64], P(None, None, 'heads')
- context_bias_grad: float32 [8, 64], P('heads')
- outer_weight_grad: float32 [8, 64, 512], P('heads')
- outer_bias_grad: float32 [512], replicated
The draws below stay inside these ranges and needn't reach their ends.
Inputs may be any that keep to these rules, and one draw needn't show every extreme that they name: `crop_slot`: column s holds 0 for rows below a split and 1 from the split on; the split is 16, 32, 48 or 64, and below 64 in every even-numbered column.
All inputs are finite; a program needn't handle non-finite values.
Results may differ from the reference program's by a relative error of at most 0.00035.
Values sent between devices are 32-bit elements; how exact they have to be, the bound alone decides.
No kernel may reach another device: no remote copies, remote signals or barrier semaphores. Data moves between devices by JAX's collectives and lax.ppermute only.
A program may use at most 192 MiB of HBM per device.

```python
import jax
import jax.numpy as jnp
from jax import lax

C = 512
NH = 8
HD = 64
E = 2048
GROUPS = 32
CTX_TOK = 81
WID = 64
ROWS_SEQ = 64
SLOTS = 2
SEQS = 2


def draw_crop_slot(key, part):
    first_pick = jax.random.randint(jax.random.fold_in(key, 11), (SEQS,), 1, 4)
    second_pick = jax.random.randint(jax.random.fold_in(key, 12), (SEQS,), 1, 5)
    order = jnp.arange(SEQS, dtype=jnp.int32)
    quarters = jnp.where(order % 2 == 0, first_pick, second_pick)
    splits = quarters * (ROWS_SEQ // 4)
    row_index = jnp.arange(ROWS_SEQ, dtype=jnp.int32)
    return (row_index[:, None] >= splits[None, :]).astype(jnp.int32)


def shard_levels(own_key, extent, split, smallest, largest):
    factor_of, own = 1.0, jax.random.fold_in(own_key, 6)
    for position, parts in split:
        draws = jnp.exp(jax.random.uniform(jax.random.fold_in(own, position), (parts,), jnp.float32, smallest / len(split), largest / len(split)))
        factor_of = factor_of * jnp.repeat(draws, extent[position] // parts).reshape([-1 if axis == position else 1 for axis in range(len(extent))])
    return factor_of


def centred(own_key, dims, scale, reach, cuts=(), kind=jnp.bfloat16):
    values = jax.random.normal(own_key, dims, jnp.float32) * scale
    if len(cuts) > 0:
        values = shard_levels(own_key, dims, cuts, -0.22, 0.18) * values
    return jnp.clip(values, min=-reach, max=reach).astype(kind)


def setup_inputs(seed: int = 0) -> dict:
    keys = jax.random.split(jax.random.key(seed), 24)
    pixels = centred(keys[0], (ROWS_SEQ, SEQS, WID, C), 1.0, 6.0, ((0, 16), (1, 2)), jnp.float32)
    crop_slot = draw_crop_slot(jax.random.fold_in(keys[23], 71), 0)
    embedding = centred(keys[2], (SEQS, SLOTS, E), 1.0, 6.0, ((0, 2),), jnp.float32)
    context = centred(keys[3], (SEQS, SLOTS, CTX_TOK, E), 1.0, 6.0, ((0, 2),))
    first_gain = jnp.clip(1.0 + 0.18 * jax.random.normal(keys[4], (C,), jnp.float32), 0.1, 1.9)
    first_offset = centred(keys[5], (C,), 0.3, 1.75, (), jnp.float32)
    first_kernel = centred(keys[6], (3, 3, C, C), (9 * C) ** -0.5, 0.09375)
    first_bias = centred(keys[7], (C,), 0.3, 1.75, (), jnp.float32)
    embed_weight = centred(keys[8], (E, 2 * C), E ** -0.5, 0.125)
    embed_bias = centred(keys[9], (2 * C,), 0.3, 1.75, (), jnp.float32)
    second_gain = jnp.clip(1.0 + 0.18 * jax.random.normal(keys[10], (C,), jnp.float32), 0.1, 1.9)
    second_offset = centred(keys[11], (C,), 0.3, 1.75, (), jnp.float32)
    second_kernel = centred(keys[12], (3, 3, C, C), (9 * C) ** -0.5, 0.09375)
    second_bias = centred(keys[13], (C,), 0.3, 1.75, (), jnp.float32)
    attend_gain = jnp.clip(1.0 + 0.18 * jax.random.normal(keys[14], (C,), jnp.float32), 0.1, 1.9)
    attend_offset = centred(keys[15], (C,), 0.3, 1.75, (), jnp.float32)
    inner_weight = centred(keys[16], (C, 3, NH, HD), C ** -0.5, 0.25, ((2, 4),))
    inner_bias = centred(keys[17], (2, NH, HD), 0.3, 1.75, ((1, 4),), jnp.float32)
    context_weight = centred(keys[18], (E, 2, NH, HD), E ** -0.5, 0.125, ((2, 4),))
    context_bias = centred(keys[19], (NH, HD), 0.3, 1.75, ((0, 4),), jnp.float32)
    outer_weight = centred(keys[20], (NH, HD, C), 8 ** -0.5, 2.0, ((0, 4),))
    outer_bias = centred(keys[21], (C,), 0.3, 1.75, (), jnp.float32)
    cotangent = centred(keys[22], (ROWS_SEQ, SEQS, WID, C), 1.0, 6.0, ((0, 16), (1, 2)), jnp.float32)
    return dict(pixels=pixels, crop_slot=crop_slot, embedding=embedding, context=context, first_gain=first_gain, first_offset=first_offset, first_kernel=first_kernel, first_bias=first_bias, embed_weight=embed_weight, embed_bias=embed_bias, second_gain=second_gain, second_offset=second_offset, second_kernel=second_kernel, second_bias=second_bias, attend_gain=attend_gain, attend_offset=attend_offset, inner_weight=inner_weight, inner_bias=inner_bias, context_weight=context_weight, context_bias=context_bias, outer_weight=outer_weight, outer_bias=outer_bias, cotangent=cotangent)


HIGH = lax.Precision.HIGHEST
eps_norm = 1e-05

@jax.custom_vjp
def low(v):
    return lax.optimization_barrier(v.astype(jnp.bfloat16)).astype(jnp.float32)

@jax.custom_vjp
def low_back(v):
    return v

def low_keep(v):
    return (low(v), None)

def low_pass(kept, grad):
    return (grad,)

def back_keep(v):
    return (v, None)

def back_low(kept, grad):
    return (low(grad),)
low.defvjp(low_keep, low_pass)
low_back.defvjp(back_keep, back_low)

def slot_table(slots):
    return (slots[:, :, None] == jnp.arange(SLOTS, dtype=jnp.int32)[None, None, :]).astype(jnp.float32)

def expand(table, stat):
    return jnp.einsum('rsk,skg->rsg', table, stat, precision=HIGH)[:, :, None, :, None]

def normalize(values, table, count):
    grouped = values.reshape(values.shape[:3] + (GROUPS, values.shape[3] // GROUPS))
    totals = jnp.einsum('rswgc,rsk->skg', grouped, table, precision=HIGH)
    centered = grouped - expand(table, totals / count[:, :, None])
    spread = jnp.einsum('rswgc,rsk->skg', centered * centered, table, precision=HIGH) / count[:, :, None]
    return (centered * expand(table, lax.rsqrt(spread + eps_norm))).reshape(values.shape)

def conv_masks(slot_rows):
    middle = slot_rows[1:-1]
    row_count = middle.shape[0]
    return jnp.stack([(slot_rows[row_tap:row_tap + row_count] == middle).astype(jnp.float32) for row_tap in range(3)])

def conv_taps(padded, kernel, masks):
    row_count = masks.shape[1]
    col_count = padded.shape[2]
    wide_pad = jnp.pad(padded, ((0, 0), (0, 0), (1, 1), (0, 0)))
    result = None
    for row_tap in range(3):
        shifted = wide_pad[row_tap:row_tap + row_count] * masks[row_tap][:, :, None, None]
        stacked = jnp.concatenate([shifted[:, :, col_tap:col_tap + col_count] for col_tap in range(3)], axis=3)
        product = jnp.dot(stacked, kernel[row_tap].reshape(3 * kernel.shape[2], kernel.shape[3]), precision=HIGH)
        result = product if result is None else result + product
    return result

def forward(pixels, first_gain, first_offset, first_kernel, first_bias, embed_weight, embed_bias, second_gain, second_offset, second_kernel, second_bias, attend_gain, attend_offset, inner_weight, inner_bias, context_weight, context_bias, outer_weight, outer_bias, crop_slot, embedding, context):
    table = slot_table(crop_slot)
    count = jnp.maximum(lax.optimization_barrier(jnp.sum(table, axis=0)) * (WID * (C // GROUPS)), 1.0)
    masks = conv_masks(jnp.pad(crop_slot, ((1, 1), (0, 0)), constant_values=-1))
    row_pad = ((1, 1), (0, 0), (0, 0), (0, 0))
    first_act = jax.nn.silu(normalize(pixels, table, count) * first_gain + first_offset)
    first_conv = conv_taps(jnp.pad(first_act, row_pad), first_kernel, masks) + first_bias
    modulation = jnp.dot(jax.nn.silu(embedding), embed_weight, precision=HIGH) + embed_bias
    mod_pixel = jnp.einsum('rsk,skc->rsc', table, modulation, precision=HIGH)[:, :, None, :]
    hidden = (normalize(first_conv, table, count) * second_gain + second_offset) * (1.0 + mod_pixel[..., :C]) + mod_pixel[..., C:]
    second_conv = conv_taps(jnp.pad(jax.nn.silu(hidden), row_pad), second_kernel, masks) + second_bias
    residual = pixels + second_conv
    normed = normalize(residual, table, count) * attend_gain + attend_offset
    inner = jnp.einsum('rswc,cjhd->rswjhd', normed, inner_weight, precision=HIGH)
    row_count, seq_count = (pixels.shape[0], pixels.shape[1])

    def to_seq(member):
        return member.transpose(1, 0, 2, 3, 4).reshape(seq_count, row_count * WID, NH, HD)
    queries = to_seq(inner[:, :, :, 0] + inner_bias[0])
    keys_px = to_seq(inner[:, :, :, 1])
    values_px = to_seq(inner[:, :, :, 2] + inner_bias[1])
    ctx_pair = jnp.einsum('skte,ejhd->sktjhd', context, context_weight, precision=HIGH)
    ctx_keys = ctx_pair[:, :, :, 0].reshape(seq_count, SLOTS * CTX_TOK, NH, HD)
    ctx_values = ctx_pair[:, :, :, 1].reshape(seq_count, SLOTS * CTX_TOK, NH, HD) + context_bias
    ctx_slots = jnp.repeat(jnp.arange(SLOTS, dtype=jnp.int32), CTX_TOK)
    query_slots = jnp.repeat(crop_slot.T, WID, axis=1)

    def attend_sequence(members):
        seq_query, seq_key, seq_value, seq_ckey, seq_cvalue, seq_slot = members
        all_keys = jnp.concatenate([seq_key, seq_ckey], axis=0)
        all_values = jnp.concatenate([seq_value, seq_cvalue], axis=0)
        keep = seq_slot[:, None] == jnp.concatenate([seq_slot, ctx_slots])[None, :]

        def one_head(head_members):
            head_query, head_key, head_value = head_members
            scores = jnp.dot(head_query, head_key.T, precision=HIGH) * HD ** (-0.5)
            scores = jnp.where(keep, scores, -1e+30)
            weights = jnp.where(keep, jnp.exp(scores - lax.optimization_barrier(jnp.max(scores, axis=1, keepdims=True))), 0.0)
            return jnp.dot(weights / lax.optimization_barrier(jnp.sum(weights, axis=1, keepdims=True)), head_value, precision=HIGH)
        heads_out = lax.map(jax.checkpoint(one_head), (jnp.moveaxis(seq_query, 1, 0), jnp.moveaxis(all_keys, 1, 0), jnp.moveaxis(all_values, 1, 0)))
        return jnp.moveaxis(heads_out, 0, 1)
    attended = lax.map(jax.checkpoint(attend_sequence), (queries, keys_px, values_px, ctx_keys, ctx_values, query_slots))
    attended = attended.reshape(seq_count, row_count, WID, NH, HD).transpose(1, 0, 2, 3, 4)
    return residual + jnp.einsum('rswhd,hdc->rswc', attended, outer_weight, precision=HIGH) + outer_bias

def reference(pixels, crop_slot, embedding, context, first_gain, first_offset, first_kernel, first_bias, embed_weight, embed_bias, second_gain, second_offset, second_kernel, second_bias, attend_gain, attend_offset, inner_weight, inner_bias, context_weight, context_bias, outer_weight, outer_bias, cotangent):
    params = tuple((member.astype(jnp.float32) for member in (pixels, first_gain, first_offset, first_kernel, first_bias, embed_weight, embed_bias, second_gain, second_offset, second_kernel, second_bias, attend_gain, attend_offset, inner_weight, inner_bias, context_weight, context_bias, outer_weight, outer_bias)))
    context_full = context.astype(jnp.float32)
    embed_full = embedding.astype(jnp.float32)

    def closed(*members):
        return forward(*members, crop_slot, embed_full, context_full)
    output, pullback = jax.vjp(closed, *params)
    grads = pullback(cotangent.astype(jnp.float32))
    return (output, grads[0], grads[1], grads[2], grads[3], grads[4], grads[5], grads[6], grads[7], grads[8], grads[9], grads[10], grads[11], grads[12], grads[13], grads[14], grads[15], grads[16], grads[17], grads[18])
```

```python
import functools

import jax
import jax.numpy as jnp
from jax import lax
from jax.experimental import pallas as pl
from jax.experimental.pallas import tpu as pltpu
from jax.sharding import PartitionSpec as P

C = 512
NH = 8
HD = 64
GROUPS = 32
GROUP_C = C // GROUPS
CTX_TOK = 81
CTX_PAD = 128
WID = 64
SLOTS = 2
ROWS_SEQ = 64
GRAN = 4
EPS = 1e-05
LOG2E = 1.4426950408889634
F32 = jnp.float32
BF = jnp.bfloat16
SEQ = ("rows", "heads")
HIGH = lax.Precision.HIGHEST
VMEM_LIMIT = 56 << 20


def hilo(values):
    high = values.astype(BF)
    return high, (values - high.astype(F32)).astype(BF)


def dot(left, right):
    return jnp.dot(left, right, preferred_element_type=F32)


def dot_nt(left, right):
    return lax.dot_general(left, right, (((1,), (1,)), ((), ())), preferred_element_type=F32)


def dot_tn(left, right):
    return lax.dot_general(left, right, (((0,), (0,)), ((), ())), preferred_element_type=F32)


def group_mean(values):
    lane = lax.broadcasted_iota(jnp.int32, values.shape, 1)
    for step in (1, 2, 4, 8):
        up = pltpu.roll(values, step, 1)
        down = pltpu.roll(values, C - step, 1)
        values = values + jnp.where((lane & step) != 0, up, down)
    return values * (1.0 / GROUP_C)


def wide(row):
    return jnp.broadcast_to(row, (8, C))


def norm_stats(pays, scal, band_px):
    count = sum(scal[i] for i in range(len(pays)))
    mean = sum(scal[i] * wide(pay[0:1, :]) for i, pay in enumerate(pays)) / count
    spread = sum(
        scal[i] * (wide(pay[1:2, :]) + band_px * jnp.square(wide(pay[0:1, :]) - mean))
        for i, pay in enumerate(pays)
    )
    total = count * band_px
    center = group_mean(mean)
    variance = group_mean(spread + total * jnp.square(mean - center)) / total
    return center[0:1], (1.0 / jnp.sqrt(variance + EPS))[0:1]


def back_means(pays, scal, gain, band_px):
    count = sum(scal[i] for i in range(len(pays))) * band_px
    first = sum(scal[i] * wide(pay[0:1, :]) for i, pay in enumerate(pays))
    second = sum(scal[i] * wide(pay[1:2, :]) for i, pay in enumerate(pays))
    return (group_mean(first * gain) / count)[0:1], (group_mean(second * gain) / count)[0:1]


def local_stats(values):
    mean = jnp.mean(values, axis=0, keepdims=True)
    return mean, jnp.sum(jnp.square(values - mean), axis=0, keepdims=True)


def row_sum(values):
    return jnp.sum(values, axis=0, keepdims=True)


def shifted(values, tap):
    if tap == 1:
        return values
    column = lax.broadcasted_iota(jnp.int32, values.shape, 0) % WID
    rows = values.shape[0]
    if tap == 0:
        return jnp.where(column == 0, 0.0, pltpu.roll(values, 1, 0))
    return jnp.where(column == WID - 1, 0.0, pltpu.roll(values, rows - 1, 0))


def fill_taps(values, high_ref, low_ref, row, width):
    for tap in range(3):
        high, low = hilo(shifted(values, tap))
        high_ref[row : row + values.shape[0], tap * width : (tap + 1) * width] = high
        low_ref[row : row + values.shape[0], tap * width : (tap + 1) * width] = low


def conv_forward_kernel(*refs, ranks, band_px, px, ways, has_skip):
    scal, x_ref, top_ref, low_ref = refs[:4]
    pays = refs[4 : 4 + ranks]
    rest = refs[4 + ranks :]
    scale_ref, shift_ref, w_ref, bias_ref = rest[:4]
    rest = rest[4:]
    if has_skip:
        skip_ref, rest = rest[0], rest[1:]
    out_ref, act_ref, stat_ref, vec_ref, high_sc, low_sc, acc = rest
    tap = pl.program_id(0)
    block = C // ways

    @pl.when(tap == 0)
    def _():
        mean, inverse = norm_stats(pays, scal, band_px)
        vec_ref[...] = jnp.concatenate([mean, inverse], axis=0)
        scale = scale_ref[...]
        shift = shift_ref[...]
        heads_count = act_ref.shape[0]

        def activate(values, weight, row):
            pre = (values - mean) * inverse * scale + shift
            act = pre / (1.0 + jnp.exp(-pre))
            if weight is not None:
                act = act * weight
            size = values.shape[0]
            fill_taps(act, high_sc, low_sc, row, C)
            for head in range(heads_count):
                act_ref[head, row : row + size, :] = jnp.concatenate(
                    [
                        act[:, (r * heads_count + head) * block : (r * heads_count + head + 1) * block]
                        for r in range(ways // heads_count)
                    ],
                    axis=1,
                )

        activate(top_ref[...], scal[ranks], 0)
        for row in range(px // WID):
            activate(x_ref[row * WID : (row + 1) * WID, :], None, (row + 1) * WID)
        activate(low_ref[...], scal[ranks + 1], px + WID)

    base = pl.multiple_of(tap * WID, WID)
    part = dot(high_sc[pl.ds(base, px), :], w_ref[0]) + dot(low_sc[pl.ds(base, px), :], w_ref[0])

    @pl.when(tap == 0)
    def _():
        acc[...] = part

    @pl.when(tap == 1)
    def _():
        acc[...] += part

    @pl.when(tap == 2)
    def _():
        out = acc[...] + part + bias_ref[...]
        if has_skip:
            out = out + skip_ref[...]
        out_ref[...] = out
        stat_ref[...] = jnp.concatenate(local_stats(out), axis=0)


def whole_block(shape):
    return pl.BlockSpec(shape, lambda *_: (0,) * len(shape), pipeline_mode=pl.Buffered(1))


def conv_forward(scal, x, halo, pays, scale, shift, kernel, bias, skip, dims):
    px, ranks, band_px, ways, head_ways = dims
    quarter = C // head_ways
    operands = [scal, x, halo[0], halo[1], *pays, scale, shift, kernel, bias]
    specs = (
        [pl.BlockSpec(memory_space=pltpu.SMEM), whole_block((px, C))]
        + [whole_block((WID, C))] * 2
        + [whole_block(pays[0].shape)] * ranks
        + [whole_block((1, C))] * 2
        + [pl.BlockSpec((1, 3 * C, C), lambda i: (i, 0, 0)), whole_block((1, C))]
    )
    if skip is not None:
        operands.append(skip)
        specs.append(whole_block((px, C)))
    ext = px + 2 * WID
    return pl.pallas_call(
        functools.partial(
            conv_forward_kernel,
            ranks=ranks,
            band_px=band_px,
            px=px,
            ways=ways,
            has_skip=skip is not None,
        ),
        grid=(3,),
        in_specs=specs,
        out_specs=[
            whole_block((px, C)),
            whole_block((head_ways, ext, quarter)),
            whole_block((2, C)),
            whole_block((2, C)),
        ],
        out_shape=[
            jax.ShapeDtypeStruct((px, C), F32),
            jax.ShapeDtypeStruct((head_ways, ext, quarter), F32),
            jax.ShapeDtypeStruct((2, C), F32),
            jax.ShapeDtypeStruct((2, C), F32),
        ],
        scratch_shapes=[
            pltpu.VMEM((ext, 3 * C), BF),
            pltpu.VMEM((ext, 3 * C), BF),
            pltpu.VMEM((px, C), F32),
        ],
        compiler_params=pltpu.CompilerParams(vmem_limit_bytes=VMEM_LIMIT),
        name="conv_forward",
    )(*operands)


def conv_backward_kernel(*refs, ranks, band_px, px, has_add):
    scal, yg_ref, yg_top, yg_low, x_ref, x_top, x_low, vec_ref, gain_ref = refs[:9]
    pays = refs[9 : 9 + ranks]
    rest = refs[9 + ranks :]
    if has_add:
        adds, rest = rest[:3], rest[3:]
    w_ref, in_ref, in_vec, in_scale, in_shift = rest[:5]
    g_ref, h_ref, sum_ref, high_sc, low_sc, acc = rest[5:]
    tap = pl.program_id(0)

    @pl.when(tap == 0)
    def _():
        gain = gain_ref[...]
        mean, inverse = vec_ref[0:1, :], vec_ref[1:2, :]
        first, second = back_means(pays, scal, gain, band_px)

        def gradient(yg, x, extra, weight, row):
            grad = (yg * gain - first - (x - mean) * inverse * second) * inverse
            if extra is not None:
                grad = grad + extra
            if weight is not None:
                grad = grad * weight
            fill_taps(grad, high_sc, low_sc, row, C)
            return grad

        gradient(yg_top[...], x_top[...], adds[1][...] if has_add else None, scal[ranks], 0)
        total = jnp.zeros((1, C), F32)
        for row in range(px // WID):
            at = slice(row * WID, (row + 1) * WID)
            grad = gradient(
                yg_ref[at, :],
                x_ref[at, :],
                adds[0][at, :] if has_add else None,
                None,
                (row + 1) * WID,
            )
            g_ref[at, :] = grad
            total = total + row_sum(grad)
        gradient(
            yg_low[...], x_low[...], adds[2][...] if has_add else None, scal[ranks + 1], px + WID
        )
        sum_ref[2:3, :] = total
        acc[...] = jnp.zeros_like(acc)

    base = pl.multiple_of(tap * WID, WID)
    part = acc[...]
    for col in range(3):
        weight = w_ref[0, (2 - col) * C : (3 - col) * C, :]
        at = (pl.ds(base, px), slice(col * C, (col + 1) * C))
        part = part + dot_nt(high_sc[at], weight) + dot_nt(low_sc[at], weight)
    acc[...] = part

    @pl.when(tap == 2)
    def _():
        hat = (in_ref[...] - in_vec[0:1, :]) * in_vec[1:2, :]
        pre = hat * in_scale[...] + in_shift[...]
        sigmoid = 1.0 / (1.0 + jnp.exp(-pre))
        h = acc[...] * (sigmoid * (1.0 + pre * (1.0 - sigmoid)))
        h_ref[...] = h
        sum_ref[0:1, :] = row_sum(h)
        sum_ref[1:2, :] = row_sum(h * hat)


def conv_backward(scal, yg, yg_halo, x, x_halo, vec, gain, pays, adds, kernel, inner, dims):
    px, ranks, band_px, _, _ = dims
    in_x, in_vec, in_scale, in_shift = inner
    rows3 = [whole_block((px, C)), whole_block((WID, C)), whole_block((WID, C))]
    operands = [scal, yg, *yg_halo, x, *x_halo, vec, gain, *pays]
    specs = (
        [pl.BlockSpec(memory_space=pltpu.SMEM)]
        + rows3
        + rows3
        + [whole_block((2, C)), whole_block((1, C))]
        + [whole_block(pays[0].shape)] * ranks
    )
    if adds is not None:
        operands += adds
        specs += rows3
    operands += [kernel, in_x, in_vec, in_scale, in_shift]
    specs += [
        pl.BlockSpec((1, 3 * C, C), lambda i: (2 - i, 0, 0)),
        whole_block((px, C)),
        whole_block((2, C)),
        whole_block((1, C)),
        whole_block((1, C)),
    ]
    ext = px + 2 * WID
    return pl.pallas_call(
        functools.partial(
            conv_backward_kernel, ranks=ranks, band_px=band_px, px=px, has_add=adds is not None
        ),
        grid=(3,),
        in_specs=specs,
        out_specs=[whole_block((px, C)), whole_block((px, C)), whole_block((3, C))],
        out_shape=[
            jax.ShapeDtypeStruct((px, C), F32),
            jax.ShapeDtypeStruct((px, C), F32),
            jax.ShapeDtypeStruct((3, C), F32),
        ],
        scratch_shapes=[
            pltpu.VMEM((ext, 3 * C), BF),
            pltpu.VMEM((ext, 3 * C), BF),
            pltpu.VMEM((px, C), F32),
        ],
        compiler_params=pltpu.CompilerParams(vmem_limit_bytes=VMEM_LIMIT),
        name="conv_backward",
    )(*operands)


def kernel_grad_kernel(act_ref, grad_ref, out_ref, taps, g_high, g_low):
    tap = pl.program_id(0)
    parts, ext, quarter = act_ref.shape
    px = ext - 2 * WID

    @pl.when(tap == 0)
    def _():
        for part in range(parts):
            act = act_ref[part]
            for col in range(3):
                high, low = hilo(shifted(act, col))
                taps[part, :, col * quarter : (col + 1) * quarter] = high
                taps[part, :, (3 + col) * quarter : (4 + col) * quarter] = low
            high, low = hilo(grad_ref[part * px : (part + 1) * px, :])
            g_high[part * px : (part + 1) * px, :] = high
            g_low[part * px : (part + 1) * px, :] = low

    base = pl.multiple_of(tap * WID, WID)
    left = jnp.concatenate([taps[part, pl.ds(base, px), :] for part in range(parts)], axis=0)
    both = dot_tn(left, g_high[...])
    rest = dot_tn(left[:, : 3 * quarter], g_low[...])
    out_ref[0] = both[: 3 * quarter] + both[3 * quarter :] + rest


def kernel_grad(act, grad):
    parts, ext, quarter = act.shape
    px = ext - 2 * WID
    return pl.pallas_call(
        kernel_grad_kernel,
        grid=(3,),
        in_specs=[whole_block(act.shape), whole_block(grad.shape)],
        out_specs=pl.BlockSpec((1, 3 * quarter, C), lambda i: (i, 0, 0)),
        out_shape=jax.ShapeDtypeStruct((3, 3 * quarter, C), F32),
        scratch_shapes=[
            pltpu.VMEM((parts, ext, 6 * quarter), BF),
            pltpu.VMEM((parts * px, C), BF),
            pltpu.VMEM((parts * px, C), BF),
        ],
        compiler_params=pltpu.CompilerParams(vmem_limit_bytes=VMEM_LIMIT),
        name="kernel_grad",
    )(act, grad)


def final_kernel(*refs, ranks, band_px):
    scal, yg_ref, x_ref, vec_ref, gain_ref, add_ref = refs[:6]
    pays = refs[6 : 6 + ranks]
    out_ref = refs[6 + ranks]
    gain = gain_ref[...]
    mean, inverse = vec_ref[0:1, :], vec_ref[1:2, :]
    first, second = back_means(pays, scal, gain, band_px)
    hat = (x_ref[...] - mean) * inverse
    out_ref[...] = add_ref[...] + (yg_ref[...] * gain - first - hat * second) * inverse


def final_norm(scal, yg, x, vec, gain, add, pays, dims):
    px, ranks, band_px, _, _ = dims
    return pl.pallas_call(
        functools.partial(final_kernel, ranks=ranks, band_px=band_px),
        in_specs=[pl.BlockSpec(memory_space=pltpu.SMEM)]
        + [pl.BlockSpec(memory_space=pltpu.VMEM)] * (5 + ranks),
        out_specs=pl.BlockSpec(memory_space=pltpu.VMEM),
        out_shape=jax.ShapeDtypeStruct((px, C), F32),
        compiler_params=pltpu.CompilerParams(vmem_limit_bytes=VMEM_LIMIT),
        name="final_norm",
    )(scal, yg, x, vec, gain, add, *pays)


def split_halves(packed):
    return jnp.concatenate([packed[:, :HD], packed[:, HD:]], axis=0)


def join_halves(values):
    half = values.shape[0] // 2
    return jnp.concatenate([values[:half], values[half:]], axis=1)


def project_kernel(*refs, ranks, band_px, px, group, shards, shard_heads):
    scal, x_ref = refs[:2]
    pays = refs[2 : 2 + ranks]
    scale_ref, shift_ref, w_ref, out_ref, vec_ref = refs[2 + ranks :]
    mean, inverse = norm_stats(pays, scal, band_px)
    vec_ref[...] = jnp.concatenate([mean, inverse], axis=0)
    high, low = hilo((x_ref[...] - mean) * inverse * scale_ref[...] + shift_ref[...])
    portion = px // group
    span = shard_heads * HD
    for shard in range(shards):
        weight = w_ref[shard, :C, :].astype(BF)
        inner = dot(high, weight) + dot(low, weight) + w_ref[shard, C : C + 1, :]
        for head in range(shard_heads):
            at = head * HD
            query = inner[:, at : at + HD]
            pair = jnp.concatenate(
                [inner[:, span + at : span + at + HD], inner[:, 2 * span + at : 2 * span + at + HD]],
                axis=1,
            )
            for part in range(group):
                slot = (shard * shard_heads + head) * group + part
                rows = slice(part * portion, (part + 1) * portion)
                out_ref[slot, :portion, :] = pair[rows]
                out_ref[slot, portion:, :] = join_halves(query[rows])


def project(scal, x, pays, scale, shift, weights, dims, group):
    px, ranks, band_px, ways, _ = dims
    portion = px // group
    shards = weights.shape[0]
    return pl.pallas_call(
        functools.partial(
            project_kernel,
            ranks=ranks,
            band_px=band_px,
            px=px,
            group=group,
            shards=shards,
            shard_heads=NH // shards,
        ),
        in_specs=[pl.BlockSpec(memory_space=pltpu.SMEM)]
        + [pl.BlockSpec(memory_space=pltpu.VMEM)] * (4 + ranks),
        out_specs=[pl.BlockSpec(memory_space=pltpu.VMEM)] * 2,
        out_shape=[
            jax.ShapeDtypeStruct((ways, portion + portion // 2, 2 * HD), F32),
            jax.ShapeDtypeStruct((2, C), F32),
        ],
        compiler_params=pltpu.CompilerParams(vmem_limit_bytes=VMEM_LIMIT),
        name="project",
    )(scal, x, *pays, scale, shift, weights)


def project_back_kernel(
    grad_ref, x_ref, vec_ref, scale_ref, shift_ref, w_ref, ng_ref, wg_ref, sum_ref, *, px, group, shards, shard_heads
):
    hat = (x_ref[...] - vec_ref[0:1, :]) * vec_ref[1:2, :]
    normed_high, normed_low = hilo(hat * scale_ref[...] + shift_ref[...])
    portion = px // group
    grad = jnp.zeros((px, C), F32)
    for shard in range(shards):
        columns = [[], [], []]
        for head in range(shard_heads):
            slots = [(shard * shard_heads + head) * group + part for part in range(group)]
            pair = jnp.concatenate([grad_ref[slot, :portion, :] for slot in slots], axis=0)
            query = jnp.concatenate(
                [split_halves(grad_ref[slot, portion:, :]) for slot in slots], axis=0
            )
            columns[0].append(query)
            columns[1].append(pair[:, :HD])
            columns[2].append(pair[:, HD:])
        inner = jnp.concatenate(columns[0] + columns[1] + columns[2], axis=1)
        high, low = hilo(inner)
        weight = w_ref[shard, :C, :].astype(BF)
        grad = grad + dot_nt(high, weight) + dot_nt(low, weight)
        wg_ref[shard, :C, :] = (
            dot_tn(normed_high, high) + dot_tn(normed_high, low) + dot_tn(normed_low, high)
        )
        wg_ref[shard, C:, :] = jnp.broadcast_to(row_sum(inner), (8, inner.shape[1]))
    ng_ref[...] = grad
    sum_ref[0:1, :] = row_sum(grad)
    sum_ref[1:2, :] = row_sum(grad * hat)


def project_back(grad, x, vec, scale, shift, weights, dims, group):
    px = dims[0]
    shards = weights.shape[0]
    return pl.pallas_call(
        functools.partial(
            project_back_kernel, px=px, group=group, shards=shards, shard_heads=NH // shards
        ),
        in_specs=[pl.BlockSpec(memory_space=pltpu.VMEM)] * 6,
        out_specs=[pl.BlockSpec(memory_space=pltpu.VMEM)] * 3,
        out_shape=[
            jax.ShapeDtypeStruct((px, C), F32),
            jax.ShapeDtypeStruct(weights.shape, F32),
            jax.ShapeDtypeStruct((2, C), F32),
        ],
        compiler_params=pltpu.CompilerParams(vmem_limit_bytes=VMEM_LIMIT),
        name="project_back",
    )(grad, x, vec, scale, shift, weights)


def attended_grad_kernel(cot_ref, w_ref, out_ref, sum_ref, *, group):
    cot = cot_ref[...]
    high, low = hilo(cot)
    weight = w_ref[...].astype(BF)
    grad = dot_nt(high, weight) + dot_nt(low, weight)
    portion = cot.shape[0] // group
    for head in range(NH):
        for part in range(group):
            rows = slice(part * portion, (part + 1) * portion)
            out_ref[head * group + part] = join_halves(grad[rows, head * HD : (head + 1) * HD])
    sum_ref[...] = row_sum(cot)


def attended_gradient(cot, weight, ways, group):
    px = cot.shape[0]
    return pl.pallas_call(
        functools.partial(attended_grad_kernel, group=group),
        out_shape=[
            jax.ShapeDtypeStruct((ways, px // group // 2, 2 * HD), F32),
            jax.ShapeDtypeStruct((1, C), F32),
        ],
        compiler_params=pltpu.CompilerParams(vmem_limit_bytes=VMEM_LIMIT),
        name="attended_gradient",
    )(cot, weight)


def output_kernel(att_ref, res_ref, cot_ref, w_ref, bias_ref, out_ref, wg_ref, *, group):
    att = jnp.concatenate(
        [
            jnp.concatenate(
                [split_halves(att_ref[head * group + part]) for part in range(group)], axis=0
            )
            for head in range(NH)
        ],
        axis=1,
    )
    high, low = hilo(att)
    weight = w_ref[...].astype(BF)
    out_ref[...] = res_ref[...] + (dot(high, weight) + dot(low, weight)) + bias_ref[...]
    cot_high, cot_low = hilo(cot_ref[...])
    wg_ref[...] = dot_tn(high, cot_high) + dot_tn(high, cot_low) + dot_tn(low, cot_high)


def output_step(att, residual, cot, weight, bias, group):
    return pl.pallas_call(
        functools.partial(output_kernel, group=group),
        out_shape=[
            jax.ShapeDtypeStruct(residual.shape, F32),
            jax.ShapeDtypeStruct((NH * HD, C), F32),
        ],
        compiler_params=pltpu.CompilerParams(vmem_limit_bytes=VMEM_LIMIT),
        name="output_step",
    )(att, residual, cot, weight, bias)


def attention_kernel(*refs, group, sources, portion):
    n0_ref, q_ref, do_ref = refs[:3]
    kv_refs = refs[3 : 3 + group]
    ctx_ref, o_ref, dq_ref = refs[3 + group : 6 + group]
    dkv_refs = refs[6 + group : 6 + 2 * group]
    dctx_ref = refs[6 + 2 * group]
    k4, v4, kt, vt, ck4, cv4, ckt, cvt, s_sc, dk_acc, dv_acc, cdk, cdv = refs[7 + 2 * group :]
    step = pl.program_id(0)
    own = sources * portion
    chunk = own // GRAN
    piece = 512 if own % 512 == 0 else own

    def prepare(kv, k4_at, v4_at):
        kh, kl = hilo(kv[:, :HD])
        vh, vl = hilo(kv[:, HD:])
        k4_at[...] = jnp.concatenate([kh, kl, kh, kl], axis=1)
        v4_at[...] = jnp.concatenate([vh, vl, vh, vl], axis=1)
        high, low = hilo(kv.T)
        return (
            jnp.concatenate([high[:HD], low[:HD]], axis=0),
            jnp.concatenate([high[HD:], low[HD:]], axis=0),
        )

    @pl.when(step == 0)
    def _():
        for way in range(group):
            for start in range(0, own, piece):
                kv = kv_refs[way][start // portion : (start + piece) // portion]
                at = slice(way * own + start, way * own + start + piece)
                kt[:, at], vt[:, at] = prepare(kv.reshape(piece, 2 * HD), k4.at[at], v4.at[at])
        for slot in range(SLOTS):
            ckt[slot], cvt[slot] = prepare(ctx_ref[slot], ck4.at[slot], cv4.at[slot])
        dk_acc[...] = jnp.zeros_like(dk_acc)
        dv_acc[...] = jnp.zeros_like(dv_acc)
        cdk[...] = jnp.zeros_like(cdk)
        cdv[...] = jnp.zeros_like(cdv)

    boundary = n0_ref[0]
    gran = step // (pl.num_programs(0) // GRAN)
    slot = (gran >= boundary).astype(jnp.int32)
    first = jnp.where(slot == 0, 0, boundary)
    last = jnp.where(slot == 0, boundary, GRAN)
    packed = q_ref[...].reshape(2 * HD, 2 * HD)
    turned = packed.T
    turned = jnp.concatenate([turned[:HD], turned[HD:]], axis=1)
    high, low = hilo(turned * (HD**-0.5 * LOG2E))
    q4 = jnp.concatenate([high, high, low, low], axis=0)
    q2 = jnp.concatenate(hilo(split_halves(packed) * HD**-0.5), axis=1)
    do_turned = do_ref[...].reshape(2 * HD, 2 * HD).T
    do_turned = jnp.concatenate([do_turned[:HD], do_turned[HD:]], axis=1)

    def pack_back(values):
        half = values.shape[1] // 2
        return jnp.concatenate([values[:, :half], values[:, half:]], axis=0).T

    def take(high, low, turned_pair):
        both = dot(turned_pair, high)
        return both[:HD] + both[HD:] + dot(turned_pair[:HD], low)

    def places(g):
        return [
            pl.ds(pl.multiple_of(way * own + g * chunk, chunk), chunk) for way in range(group)
        ]

    ctx_scores = dot(ck4[slot], q4)
    token = lax.broadcasted_iota(jnp.int32, ctx_scores.shape, 0)
    ctx_scores = jnp.where(token < CTX_TOK, ctx_scores, -1e30)

    def score_pass(g, top):
        for at in places(g):
            scores = dot(k4[at, :], q4)
            s_sc[at, :] = scores
            top = jnp.maximum(top, jnp.max(scores, axis=0, keepdims=True))
        return top

    top = lax.fori_loop(first, last, score_pass, jnp.max(ctx_scores, axis=0, keepdims=True))
    ctx_p = jnp.exp2(ctx_scores - top)

    def value_pass(g, carry):
        total, out = carry
        for at in places(g):
            p = jnp.exp2(s_sc[at, :] - top)
            s_sc[at, :] = p
            total = total + row_sum(p)
            out = out + take(*hilo(p), vt[:, at])
        return total, out

    total, out = lax.fori_loop(
        first, last, value_pass, (row_sum(ctx_p), take(*hilo(ctx_p), cvt[slot]))
    )
    inverse = 1.0 / total
    out = out * inverse
    o_ref[...] = pack_back(out).reshape(o_ref.shape)
    do_scaled = do_turned * inverse
    diagonal = row_sum(do_scaled * out)
    high, low = hilo(do_scaled)
    d4 = jnp.concatenate([high, high, low, low], axis=0)
    d2 = jnp.concatenate(hilo(split_halves(pack_back(do_scaled))), axis=1)

    def back(p, values, keys_turned):
        ds = p * (dot(values, d4) - diagonal)
        ds_high, ds_low = hilo(ds)
        p_high, p_low = hilo(p)
        dv = dot(p_high, d2) + dot(p_low, d2)
        dk = dot(ds_high, q2) + dot(ds_low, q2)
        return dk, dv, take(ds_high, ds_low, keys_turned)

    dk, dv, dq = back(ctx_p, cv4[slot], ckt[slot])
    cdk[slot] += dk
    cdv[slot] += dv

    def gradient_pass(g, dq):
        for at in places(g):
            dk, dv, part = back(s_sc[at, :], v4[at, :], kt[:, at])
            dk_acc[at, :] += dk
            dv_acc[at, :] += dv
            dq = dq + part
        return dq

    dq = lax.fori_loop(first, last, gradient_pass, dq) * HD**-0.5
    dq_ref[...] = pack_back(dq).reshape(dq_ref.shape)

    def fold(pair):
        return pair[:, :HD] + pair[:, HD:]

    @pl.when(step == pl.num_programs(0) - 1)
    def _():
        for way in range(group):
            for start in range(0, own, piece):
                at = slice(way * own + start, way * own + start + piece)
                joined = jnp.concatenate([fold(dk_acc[at, :]), fold(dv_acc[at, :])], axis=1)
                dkv_refs[way][start // portion : (start + piece) // portion] = joined.reshape(
                    piece // portion, portion, 2 * HD
                )
        for slot in range(SLOTS):
            dctx_ref[slot] = jnp.concatenate([fold(cdk[slot]), fold(cdv[slot])], axis=1)


def attention(boundary, traded, do, others, ctx, group):
    sources = traded.shape[0]
    half = do.shape[1]
    portion = 2 * half
    own = sources * portion
    keys = group * own
    per_step = 2 * HD // half
    steps = sources // per_step
    q_block = pl.BlockSpec((per_step, half, 2 * HD), lambda i: (i, 2, 0))
    side_block = pl.BlockSpec((per_step, half, 2 * HD), lambda i: (i, 0, 0))
    kv_shape = (sources, portion, 2 * HD)
    pair_shape = (SLOTS, CTX_PAD, 2 * HD)
    return pl.pallas_call(
        functools.partial(attention_kernel, group=group, sources=sources, portion=portion),
        grid=(steps,),
        in_specs=[pl.BlockSpec(memory_space=pltpu.SMEM), q_block, side_block]
        + [whole_block(kv_shape)] * group
        + [whole_block(pair_shape)],
        out_specs=[side_block, side_block] + [whole_block(kv_shape)] * group + [whole_block(pair_shape)],
        out_shape=[jax.ShapeDtypeStruct((sources, half, 2 * HD), F32)] * 2
        + [jax.ShapeDtypeStruct(kv_shape, F32)] * group
        + [jax.ShapeDtypeStruct(pair_shape, F32)],
        scratch_shapes=[
            pltpu.VMEM((keys, 4 * HD), BF),
            pltpu.VMEM((keys, 4 * HD), BF),
            pltpu.VMEM((2 * HD, keys), BF),
            pltpu.VMEM((2 * HD, keys), BF),
            pltpu.VMEM((SLOTS, CTX_PAD, 4 * HD), BF),
            pltpu.VMEM((SLOTS, CTX_PAD, 4 * HD), BF),
            pltpu.VMEM((SLOTS, 2 * HD, CTX_PAD), BF),
            pltpu.VMEM((SLOTS, 2 * HD, CTX_PAD), BF),
            pltpu.VMEM((keys, 4 * HD), F32),
            pltpu.VMEM((keys, 2 * HD), F32),
            pltpu.VMEM((keys, 2 * HD), F32),
            pltpu.VMEM(pair_shape, F32),
            pltpu.VMEM(pair_shape, F32),
        ],
        compiler_params=pltpu.CompilerParams(vmem_limit_bytes=VMEM_LIMIT),
        name="attention",
    )(boundary, traded, do, traded, *others, ctx)


def rotated(values, axis):
    size = lax.axis_size(axis)
    return [values] + [
        lax.ppermute(values, axis, [(i, (i + d) % size) for i in range(size)])
        for d in range(1, size)
    ]


def shared_stats(stat, px):
    parts = jnp.stack(rotated(stat, "heads"))
    mean = jnp.mean(parts[:, 0], axis=0)
    spread = jnp.sum(parts[:, 1] + px * jnp.square(parts[:, 0] - mean), axis=0)
    return rotated(jnp.stack([mean, spread]), "rows")


def shared_sums(sums):
    return rotated(sum(rotated(sums, "heads")), "rows")


def halo(edge_low, edge_high):
    size = lax.axis_size("rows") * lax.axis_size("heads")
    forward = [(i, i + 1) for i in range(size - 1)]
    backward = [(i + 1, i) for i in range(size - 1)]
    return lax.ppermute(edge_high, SEQ, forward), lax.ppermute(edge_low, SEQ, backward)


def edges(values):
    return halo(values[:WID], values[-WID:])


def trade(values):
    return lax.all_to_all(values, SEQ, split_axis=0, concat_axis=0, tiled=True)


def per_device(
    pixels,
    crop_slot,
    embedding,
    context,
    first_gain,
    first_offset,
    first_kernel,
    first_bias,
    embed_weight,
    embed_bias,
    second_gain,
    second_offset,
    second_kernel,
    second_bias,
    attend_gain,
    attend_offset,
    inner_weight,
    inner_bias,
    context_weight,
    context_bias,
    outer_weight,
    outer_bias,
    cotangent,
):
    row_count = pixels.shape[0]
    assert pixels.shape[1] == 1
    ranks = lax.axis_size("rows")
    head_ways = lax.axis_size("heads")
    ways = ranks * head_ways
    group = ways // NH
    px = row_count * WID
    band_rows = row_count * head_ways
    band_px = band_rows * WID
    dims = (px, ranks, float(band_px), ways, head_ways)
    rank = lax.axis_index("rows")
    head_rank = lax.axis_index("heads")
    joint = rank * head_ways + head_rank
    shard_heads = NH // head_ways

    slots = crop_slot[:, 0]
    own_slot = slots[joint * row_count]
    band_slots = slots[::band_rows]
    weights = [
        (band_slots[(rank - d) % ranks] == own_slot).astype(F32) for d in range(ranks)
    ]
    slot_of = [band_slots[(rank - d) % ranks] for d in range(ranks)]
    above = slots[jnp.maximum(joint * row_count - 1, 0)]
    below = slots[jnp.minimum((joint + 1) * row_count, ROWS_SEQ - 1)]
    top_ok = ((joint > 0) & (above == own_slot)).astype(F32)
    low_ok = ((joint < ways - 1) & (below == own_slot)).astype(F32)
    scal = jnp.stack(weights + [top_ok, low_ok])
    boundary = (GRAN - jnp.sum(slots[:: ROWS_SEQ // GRAN])).reshape(1).astype(jnp.int32)

    x = pixels.reshape(px, C)
    cot = cotangent.reshape(px, C)

    def row(vector):
        return vector.reshape(1, C)

    mean = jnp.mean(x, axis=0)
    x_stat = jnp.stack([mean, jnp.sum(jnp.square(x - mean), axis=0)])
    x_halo = edges(x)
    x_pays = shared_stats(x_stat, px)
    first_k = first_kernel.reshape(3, 3 * C, C)
    second_k = second_kernel.reshape(3, 3 * C, C)
    conv1, act1, stat1, x_vec = conv_forward(
        scal, x, x_halo, x_pays, row(first_gain), row(first_offset), first_k, row(first_bias), None, dims
    )

    embed_act = jax.nn.silu(embedding[0])
    modulation = jnp.dot(embed_act, embed_weight.astype(F32), precision=HIGH) + embed_bias
    own_mod = lax.dynamic_index_in_dim(modulation, own_slot, 0, keepdims=True)
    lift = 1.0 + own_mod[:, :C]
    second_scale = row(second_gain) * lift
    second_shift = row(second_offset) * lift + own_mod[:, C:]
    span = shard_heads * HD
    bias_row = jnp.concatenate(
        [inner_bias[0].reshape(1, span), jnp.zeros((1, span), F32), inner_bias[1].reshape(1, span)],
        axis=1,
    )
    inner_own = jnp.concatenate(
        [
            inner_weight.astype(F32).reshape(C, 3 * span),
            jnp.pad(bias_row, ((0, 7), (0, 0))),
        ],
        axis=0,
    )
    inner_w = lax.all_gather(inner_own, "heads", axis=0, tiled=False)
    outer_w = lax.all_gather(
        outer_weight.astype(F32).reshape(span, C), "heads", axis=0, tiled=True
    )
    ctx_flat = context[0].reshape(SLOTS * CTX_TOK, context.shape[-1])
    ctx_pair = jnp.dot(
        ctx_flat,
        context_weight.reshape(context.shape[-1], 2 * span),
        preferred_element_type=F32,
    ).reshape(SLOTS * CTX_TOK, 2, shard_heads, HD)
    ctx_pair = ctx_pair + jnp.stack([jnp.zeros_like(context_bias), context_bias])
    ctx_pair = ctx_pair.transpose(2, 0, 1, 3).reshape(shard_heads, SLOTS * CTX_TOK, 2 * HD)
    ctx_all = lax.all_gather(ctx_pair, "heads", axis=0, tiled=True)
    ctx_own = lax.dynamic_index_in_dim(ctx_all, joint // group, 0, keepdims=False)
    ctx_own = jnp.pad(
        ctx_own.reshape(SLOTS, CTX_TOK, 2 * HD), ((0, 0), (0, CTX_PAD - CTX_TOK), (0, 0))
    )
    do_blocks, cot_sum = attended_gradient(cot, outer_w, ways, group)
    do_own = trade(do_blocks)
    cot_halo = edges(cot)
    act1_parts = lax.all_to_all(act1, "heads", split_axis=0, concat_axis=0, tiled=True)
    ctx_seqs = rotated(ctx_flat.astype(F32), "dp")
    act_seqs = rotated(embed_act, "dp")

    conv1_halo = edges(conv1)
    pays1 = shared_stats(stat1, px)
    residual, act2, stat2, vec1 = conv_forward(
        scal, conv1, conv1_halo, pays1, second_scale, second_shift, second_k, row(second_bias), x, dims
    )
    act2_parts = lax.all_to_all(act2, "heads", split_axis=0, concat_axis=0, tiled=True)

    pays2 = shared_stats(stat2, px)
    res_halo = edges(residual)
    blocks, vec2 = project(
        scal, residual, pays2, row(attend_gain), row(attend_offset), inner_w, dims, group
    )
    traded = trade(blocks)
    portion = px // group
    own_kv = traded[:, :portion]

    def mates(d):
        return [(i, i // group * group + (i % group + d) % group) for i in range(ways)]

    others = [lax.ppermute(own_kv, SEQ, mates(group - d)) for d in range(1, group)]
    results = attention(boundary, traded, do_own, others, ctx_own, group)
    att_own, dq_own = results[:2]
    dkv_parts = results[2 : 2 + group]
    ctx_grad = results[2 + group]
    dkv = dkv_parts[0]
    for d in range(1, group):
        dkv = dkv + lax.ppermute(dkv_parts[d], SEQ, mates(d))
    grads = trade(jnp.concatenate([dkv, dq_own], axis=1))
    attended = trade(att_own)
    output, outer_part = output_step(attended, residual, cot, outer_w, row(outer_bias), group)
    normed_grad, inner_part, sums2 = project_back(
        grads, residual, vec2, row(attend_gain), row(attend_offset), inner_w, dims, group
    )

    ng_halo = edges(normed_grad)
    pays3 = shared_sums(jnp.concatenate([sums2, cot_sum], axis=0))
    residual_grad, hidden_grad, sums1 = conv_backward(
        scal,
        normed_grad,
        ng_halo,
        residual,
        res_halo,
        vec2,
        row(attend_gain),
        pays3,
        [cot, *cot_halo],
        second_k,
        (conv1, vec1, second_scale, second_shift),
        dims,
    )
    hg_halo = edges(hidden_grad)
    pays4 = shared_sums(sums1)
    conv1_grad, pre_grad, sums0 = conv_backward(
        scal,
        hidden_grad,
        hg_halo,
        conv1,
        conv1_halo,
        vec1,
        second_scale,
        pays4,
        None,
        first_k,
        (x, x_vec, row(first_gain), row(first_offset)),
        dims,
    )
    pays5 = shared_sums(sums0)
    pixels_grad = final_norm(scal, pre_grad, x, x_vec, row(first_gain), residual_grad, pays5, dims)

    def kernel_sum(parts, grad):
        band = lax.all_gather(grad, "heads", axis=0, tiled=True)
        part = kernel_grad(parts, band).reshape(3, 3, C // head_ways, C)
        part = lax.psum_scatter(part, "dp", scatter_dimension=3, tiled=True)
        return lax.psum_scatter(part, "rows", scatter_dimension=2, tiled=True)

    second_kernel_grad = kernel_sum(act2_parts, residual_grad)
    first_kernel_grad = kernel_sum(act1_parts, conv1_grad)

    inner_sum = lax.psum_scatter(inner_part, "heads", scatter_dimension=0, tiled=True)
    outer_sum = lax.psum_scatter(outer_part, "heads", scatter_dimension=0, tiled=True)
    inner_sum, outer_sum = lax.psum((inner_sum, outer_sum), ("dp", "rows"))
    inner_sum = inner_sum.reshape(C + 8, 3 * span)
    inner_weight_grad = inner_sum[:C].reshape(C, 3, shard_heads, HD)
    bias_sum = inner_sum[C].reshape(3, shard_heads, HD)
    inner_bias_grad = jnp.stack([bias_sum[0], bias_sum[2]])
    outer_weight_grad = outer_sum.reshape(shard_heads, HD, C)

    ctx_grad = ctx_grad[:, :CTX_TOK].reshape(SLOTS * CTX_TOK, 2 * HD)
    ctx_grads = lax.all_gather(ctx_grad, SEQ, axis=0, tiled=False)
    ctx_grads = jnp.sum(
        ctx_grads.reshape(NH, group, SLOTS * CTX_TOK, 2 * HD), axis=1
    )
    ctx_mine = lax.dynamic_slice_in_dim(ctx_grads, head_rank * shard_heads, shard_heads, 0)
    ctx_mine = (
        ctx_mine.reshape(shard_heads, SLOTS * CTX_TOK, 2, HD)
        .transpose(1, 2, 0, 3)
        .reshape(SLOTS * CTX_TOK, 2 * span)
    )
    mine_seqs = rotated(ctx_mine, "dp")
    context_weight_grad = jnp.dot(
        jnp.concatenate(ctx_seqs, axis=0).T, jnp.concatenate(mine_seqs, axis=0), precision=lax.Precision.HIGH
    ).reshape(context.shape[-1], 2, shard_heads, HD)
    context_bias_grad = jnp.sum(sum(mine_seqs), axis=0).reshape(2, shard_heads, HD)[1]

    def per_slot(pays, at):
        return jnp.stack(
            [
                sum(jnp.where(slot_of[d] == slot, pays[d][at], 0.0) for d in range(ranks))
                for slot in range(SLOTS)
            ]
        )

    attend_sums = sum(pays3)
    shift_grad = per_slot(pays4, 0)
    hat_grad = per_slot(pays4, 1)
    mod_lift = 1.0 + modulation[:, :C]
    scale_grad = hat_grad * second_gain + shift_grad * second_offset
    pack = jnp.concatenate(
        [
            attend_sums,
            jnp.stack(
                [
                    jnp.sum(hat_grad * mod_lift, axis=0),
                    jnp.sum(shift_grad * mod_lift, axis=0),
                    sum(pay[2] for pay in pays4),
                ]
            ),
            scale_grad,
            shift_grad,
        ],
        axis=0,
    )
    packs = rotated(pack, "dp")
    vectors = sum(packs)
    mod_grads = jnp.concatenate(
        [jnp.concatenate([p[6 : 6 + SLOTS], p[6 + SLOTS :]], axis=1) for p in packs], axis=0
    )
    embed_bias_grad = jnp.sum(mod_grads, axis=0)
    embed_rows = embed_weight.shape[0] // ways
    embed_cols = 2 * C // lax.axis_size("dp")
    embed_weight_grad = jnp.einsum(
        "ke,kc->ec",
        lax.dynamic_slice_in_dim(jnp.concatenate(act_seqs, axis=0), joint * embed_rows, embed_rows, 1),
        lax.dynamic_slice_in_dim(mod_grads, lax.axis_index("dp") * embed_cols, embed_cols, 1),
        precision=HIGH,
    )
    first_sums = sum(rotated(sum(pays5), "dp"))

    shape = pixels.shape
    return (
        output.reshape(shape),
        pixels_grad.reshape(shape),
        first_sums[1],
        first_sums[0],
        first_kernel_grad,
        first_sums[2],
        embed_weight_grad,
        embed_bias_grad,
        vectors[3],
        vectors[4],
        second_kernel_grad,
        vectors[5],
        vectors[1],
        vectors[0],
        inner_weight_grad,
        inner_bias_grad,
        context_weight_grad,
        context_bias_grad,
        outer_weight_grad,
        vectors[2],
    )


def solution(mesh):
    band = P(SEQ, "dp", None, None)
    kernel_out = P(None, None, SEQ, "dp")
    return jax.shard_map(
        per_device,
        mesh=mesh,
        in_specs=(
            band,
            P(None, "dp"),
            P("dp", None, None),
            P("dp", None, None, None),
            P(),
            P(),
            P(),
            P(),
            P(),
            P(),
            P(),
            P(),
            P(),
            P(),
            P(),
            P(),
            P(None, None, "heads", None),
            P(None, "heads", None),
            P(None, None, "heads", None),
            P("heads", None),
            P("heads", None, None),
            P(),
            band,
        ),
        out_specs=(
            band,
            band,
            P(),
            P(),
            kernel_out,
            P(),
            P(SEQ, "dp"),
            P(),
            P(),
            P(),
            kernel_out,
            P(),
            P(),
            P(),
            P(None, None, "heads", None),
            P(None, "heads", None),
            P(None, None, "heads", None),
            P("heads", None),
            P("heads", None, None),
            P(),
        ),
        check_vma=False,
    )
```

```python
import functools

import jax
import jax.numpy as jnp
from jax import lax
from jax.experimental import pallas as pl
from jax.experimental.pallas import tpu as pltpu
from jax.sharding import PartitionSpec as P

C = 512
NH = 8
HD = 64
GROUPS = 32
GROUP_C = C // GROUPS
CTX_TOK = 81
CTX_PAD = 128
WID = 64
SLOTS = 2
ROWS_SEQ = 64
GRAN = 4
EPS = 1e-05
LOG2E = 1.4426950408889634
F32 = jnp.float32
BF = jnp.bfloat16
SEQ = ("rows", "heads")
HIGH = lax.Precision.HIGHEST
VMEM_LIMIT = 56 << 20


def hilo(values):
    high = values.astype(BF)
    return high, (values - high.astype(F32)).astype(BF)


def dot(left, right):
    return jnp.dot(left, right, preferred_element_type=F32)


def dot_nt(left, right):
    return lax.dot_general(left, right, (((1,), (1,)), ((), ())), preferred_element_type=F32)


def dot_tn(left, right):
    return lax.dot_general(left, right, (((0,), (0,)), ((), ())), preferred_element_type=F32)


def group_mean(values):
    lane = lax.broadcasted_iota(jnp.int32, values.shape, 1)
    for step in (1, 2, 4, 8):
        up = pltpu.roll(values, step, 1)
        down = pltpu.roll(values, C - step, 1)
        values = values + jnp.where((lane & step) != 0, up, down)
    return values * (1.0 / GROUP_C)


def wide(row):
    return jnp.broadcast_to(row, (8, C))


def norm_stats(pays, scal, px):
    ways = pays.shape[0]
    count = sum(scal[i] for i in range(ways))
    mean = sum(scal[i] * wide(pays[i, 0:1, :]) for i in range(ways)) / count
    spread = sum(
        scal[i] * (wide(pays[i, 1:2, :]) + px * jnp.square(wide(pays[i, 0:1, :]) - mean))
        for i in range(ways)
    )
    total = count * px
    center = group_mean(mean)
    variance = group_mean(spread + total * jnp.square(mean - center)) / total
    return center[0:1], (1.0 / jnp.sqrt(variance + EPS))[0:1]


def back_means(pays, scal, gain, px):
    ways = pays.shape[0]
    count = sum(scal[i] for i in range(ways)) * px
    first = sum(scal[i] * wide(pays[i, 0:1, :]) for i in range(ways))
    second = sum(scal[i] * wide(pays[i, 1:2, :]) for i in range(ways))
    return (group_mean(first * gain) / count)[0:1], (group_mean(second * gain) / count)[0:1]


def spread_out(rows, ref):
    ref[...] = jnp.broadcast_to(jnp.concatenate(rows, axis=0)[None], ref.shape)


def local_stats(values):
    mean = jnp.mean(values, axis=0, keepdims=True)
    return mean, jnp.sum(jnp.square(values - mean), axis=0, keepdims=True)


def row_sum(values):
    return jnp.sum(values, axis=0, keepdims=True)


def shifted(values, tap):
    if tap == 1:
        return values
    column = lax.broadcasted_iota(jnp.int32, values.shape, 0) % WID
    rows = values.shape[0]
    if tap == 0:
        return jnp.where(column == 0, 0.0, pltpu.roll(values, 1, 0))
    return jnp.where(column == WID - 1, 0.0, pltpu.roll(values, rows - 1, 0))


def fill_taps(values, high_ref, low_ref, row, width):
    for tap in range(3):
        high, low = hilo(shifted(values, tap))
        high_ref[row : row + values.shape[0], tap * width : (tap + 1) * width] = high
        low_ref[row : row + values.shape[0], tap * width : (tap + 1) * width] = low


def conv_forward_kernel(*refs, px, ways, has_skip):
    scal, x_ref, top_ref, low_ref, pays, scale_ref, shift_ref, w_ref, bias_ref = refs[:9]
    rest = refs[9:]
    if has_skip:
        skip_ref, rest = rest[0], rest[1:]
    out_ref, act_ref, stat_ref, vec_ref, high_sc, low_sc, acc = rest
    tap = pl.program_id(0)
    block = C // ways

    @pl.when(tap == 0)
    def _():
        mean, inverse = norm_stats(pays, scal, float(px))
        vec_ref[...] = jnp.concatenate([mean, inverse], axis=0)
        scale = scale_ref[...]
        shift = shift_ref[...]
        heads_count = act_ref.shape[0]

        def activate(values, weight, row):
            pre = (values - mean) * inverse * scale + shift
            act = pre / (1.0 + jnp.exp(-pre))
            if weight is not None:
                act = act * weight
            size = values.shape[0]
            fill_taps(act, high_sc, low_sc, row, C)
            for head in range(heads_count):
                act_ref[head, row : row + size, :] = jnp.concatenate(
                    [
                        act[:, (r * heads_count + head) * block : (r * heads_count + head + 1) * block]
                        for r in range(ways // heads_count)
                    ],
                    axis=1,
                )

        activate(top_ref[...], scal[ways], 0)
        for row in range(px // WID):
            activate(x_ref[row * WID : (row + 1) * WID, :], None, (row + 1) * WID)
        activate(low_ref[...], scal[ways + 1], px + WID)

    base = pl.multiple_of(tap * WID, WID)
    part = dot(
        jnp.concatenate([high_sc[pl.ds(base, px), :], low_sc[pl.ds(base, px), :]], axis=0), w_ref[0]
    )
    part = part[:px] + part[px:]

    @pl.when(tap == 0)
    def _():
        acc[...] = part

    @pl.when(tap == 1)
    def _():
        acc[...] += part

    @pl.when(tap == 2)
    def _():
        out = acc[...] + part + bias_ref[...]
        if has_skip:
            out = out + skip_ref[...]
        out_ref[...] = out
        spread_out(local_stats(out), stat_ref)


def cost(flops):
    return pl.CostEstimate(flops=int(flops), transcendentals=0, bytes_accessed=0)


def whole_block(shape):
    return pl.BlockSpec(shape, lambda *_: (0,) * len(shape), pipeline_mode=pl.Buffered(1))


def conv_forward(scal, x, halo, pays, scale, shift, kernel, bias, skip, dims):
    px, ways, head_ways = dims
    quarter = C // head_ways
    operands = [scal, x, halo[0], halo[1], pays, scale, shift, kernel, bias]
    specs = (
        [pl.BlockSpec(memory_space=pltpu.SMEM), whole_block((px, C))]
        + [whole_block((WID, C))] * 2
        + [whole_block(pays.shape)]
        + [whole_block((1, C))] * 2
        + [pl.BlockSpec((1, 3 * C, C), lambda i: (i, 0, 0)), whole_block((1, C))]
    )
    if skip is not None:
        operands.append(skip)
        specs.append(whole_block((px, C)))
    ext = px + 2 * WID
    return pl.pallas_call(
        functools.partial(
            conv_forward_kernel,
            px=px,
            ways=ways,
            has_skip=skip is not None,
        ),
        grid=(3,),
        in_specs=specs,
        out_specs=[
            whole_block((px, C)),
            whole_block((head_ways, ext, quarter)),
            whole_block((ways, 2, C)),
            whole_block((2, C)),
        ],
        out_shape=[
            jax.ShapeDtypeStruct((px, C), F32),
            jax.ShapeDtypeStruct((head_ways, ext, quarter), F32),
            jax.ShapeDtypeStruct((ways, 2, C), F32),
            jax.ShapeDtypeStruct((2, C), F32),
        ],
        scratch_shapes=[
            pltpu.VMEM((ext, 3 * C), BF),
            pltpu.VMEM((ext, 3 * C), BF),
            pltpu.VMEM((px, C), F32),
        ],
        compiler_params=pltpu.CompilerParams(vmem_limit_bytes=VMEM_LIMIT),
        cost_estimate=cost(7e9),
        name="conv_forward",
    )(*operands)


def conv_backward_kernel(*refs, px, ways, has_add):
    scal, yg_ref, yg_top, yg_low, x_ref, x_top, x_low, vec_ref, gain_ref, pays = refs[:10]
    rest = refs[10:]
    if has_add:
        adds, rest = rest[:3], rest[3:]
    w_ref, in_ref, in_vec, in_scale, in_shift = rest[:5]
    g_ref, h_ref, sum_ref, high_sc, low_sc, acc, bias_sum = rest[5:]
    tap = pl.program_id(0)

    @pl.when(tap == 0)
    def _():
        gain = gain_ref[...]
        mean, inverse = vec_ref[0:1, :], vec_ref[1:2, :]
        first, second = back_means(pays, scal, gain, float(px))

        def gradient(yg, x, extra, weight, row):
            grad = (yg * gain - first - (x - mean) * inverse * second) * inverse
            if extra is not None:
                grad = grad + extra
            if weight is not None:
                grad = grad * weight
            fill_taps(grad, high_sc, low_sc, row, C)
            return grad

        gradient(yg_top[...], x_top[...], adds[1][...] if has_add else None, scal[ways], 0)
        total = jnp.zeros((1, C), F32)
        for row in range(px // WID):
            at = slice(row * WID, (row + 1) * WID)
            grad = gradient(
                yg_ref[at, :],
                x_ref[at, :],
                adds[0][at, :] if has_add else None,
                None,
                (row + 1) * WID,
            )
            g_ref[at, :] = grad
            total = total + row_sum(grad)
        gradient(
            yg_low[...], x_low[...], adds[2][...] if has_add else None, scal[ways + 1], px + WID
        )
        bias_sum[...] = total
        acc[...] = jnp.zeros_like(acc)

    base = pl.multiple_of(tap * WID, WID)
    part = acc[...]
    for col in range(3):
        weight = w_ref[0, (2 - col) * C : (3 - col) * C, :]
        at = (pl.ds(base, px), slice(col * C, (col + 1) * C))
        both = dot_nt(jnp.concatenate([high_sc[at], low_sc[at]], axis=0), weight)
        part = part + both[:px] + both[px:]
    acc[...] = part

    @pl.when(tap == 2)
    def _():
        hat = (in_ref[...] - in_vec[0:1, :]) * in_vec[1:2, :]
        pre = hat * in_scale[...] + in_shift[...]
        sigmoid = 1.0 / (1.0 + jnp.exp(-pre))
        h = acc[...] * (sigmoid * (1.0 + pre * (1.0 - sigmoid)))
        h_ref[...] = h
        spread_out([row_sum(h), row_sum(h * hat), bias_sum[...]], sum_ref)


def conv_backward(scal, yg, yg_halo, x, x_halo, vec, gain, pays, adds, kernel, inner, dims):
    px, ways, _ = dims
    in_x, in_vec, in_scale, in_shift = inner
    rows3 = [whole_block((px, C)), whole_block((WID, C)), whole_block((WID, C))]
    operands = [scal, yg, *yg_halo, x, *x_halo, vec, gain, pays]
    specs = (
        [pl.BlockSpec(memory_space=pltpu.SMEM)]
        + rows3
        + rows3
        + [whole_block((2, C)), whole_block((1, C)), whole_block(pays.shape)]
    )
    if adds is not None:
        operands += adds
        specs += rows3
    operands += [kernel, in_x, in_vec, in_scale, in_shift]
    specs += [
        pl.BlockSpec((1, 3 * C, C), lambda i: (2 - i, 0, 0)),
        whole_block((px, C)),
        whole_block((2, C)),
        whole_block((1, C)),
        whole_block((1, C)),
    ]
    ext = px + 2 * WID
    return pl.pallas_call(
        functools.partial(
            conv_backward_kernel, px=px, ways=ways, has_add=adds is not None
        ),
        grid=(3,),
        in_specs=specs,
        out_specs=[whole_block((px, C)), whole_block((px, C)), whole_block((ways, 3, C))],
        out_shape=[
            jax.ShapeDtypeStruct((px, C), F32),
            jax.ShapeDtypeStruct((px, C), F32),
            jax.ShapeDtypeStruct((ways, 3, C), F32),
        ],
        scratch_shapes=[
            pltpu.VMEM((ext, 3 * C), BF),
            pltpu.VMEM((ext, 3 * C), BF),
            pltpu.VMEM((px, C), F32),
            pltpu.VMEM((1, C), F32),
        ],
        compiler_params=pltpu.CompilerParams(vmem_limit_bytes=VMEM_LIMIT),
        cost_estimate=cost(7e9),
        name="conv_backward",
    )(*operands)


def kernel_grad_kernel(side_ref, act_ref, grad_ref, *refs, ranks, split):
    outs, (taps, g_high, g_low) = refs[:-3], refs[-3:]
    tap = pl.program_id(0)
    parts, ext, quarter = act_ref.shape
    px = ext - 2 * WID
    block = quarter // ranks

    @pl.when(tap == 0)
    def _():
        for part in range(parts):
            act = act_ref[part]
            for col in range(3):
                high, low = hilo(shifted(act, col))
                taps[part, :, col * quarter : (col + 1) * quarter] = high
                taps[part, :, (3 + col) * quarter : (4 + col) * quarter] = low
            high, low = hilo(grad_ref[part * px : (part + 1) * px, :])
            g_high[part * px : (part + 1) * px, :] = high
            g_low[part * px : (part + 1) * px, :] = low

    base = pl.multiple_of(tap * WID, WID)
    left = jnp.concatenate([taps[part, pl.ds(base, px), :] for part in range(parts)], axis=0)
    both = dot_tn(left, g_high[...])
    rest = dot_tn(left[:, : 3 * quarter], g_low[...])
    total = both[: 3 * quarter] + both[3 * quarter :] + rest
    if split:
        even = side_ref[0] == 0
        pieces = [
            jnp.where(even, total[:, : C // 2], total[:, C // 2 :]),
            jnp.where(even, total[:, C // 2 :], total[:, : C // 2]),
        ]
    else:
        pieces = [total]
    for row in range(3):

        @pl.when(tap == row)
        def _():
            for index, piece in enumerate(pieces):
                ref = outs[row * len(pieces) + index]
                for rank in range(ranks):
                    for col in range(3):
                        start = col * quarter + rank * block
                        ref[rank, col * block : (col + 1) * block, :] = piece[start : start + block]


def kernel_grad(side, act, grad, ranks, split):
    parts, ext, quarter = act.shape
    px = ext - 2 * WID
    wide_out = C // 2 if split else C
    shape = (ranks, 3 * quarter // ranks, wide_out)
    count = 6 if split else 3
    return pl.pallas_call(
        functools.partial(kernel_grad_kernel, ranks=ranks, split=split),
        grid=(3,),
        in_specs=[
            pl.BlockSpec(memory_space=pltpu.SMEM),
            whole_block(act.shape),
            whole_block(grad.shape),
        ],
        out_specs=[whole_block(shape)] * count,
        out_shape=[jax.ShapeDtypeStruct(shape, F32)] * count,
        scratch_shapes=[
            pltpu.VMEM((parts, ext, 6 * quarter), BF),
            pltpu.VMEM((parts * px, C), BF),
            pltpu.VMEM((parts * px, C), BF),
        ],
        compiler_params=pltpu.CompilerParams(vmem_limit_bytes=VMEM_LIMIT),
        cost_estimate=cost(6e9),
        name="kernel_grad",
    )(side, act, grad)


def final_kernel(scal, yg_ref, x_ref, vec_ref, gain_ref, add_ref, pays, out_ref):
    gain = gain_ref[...]
    mean, inverse = vec_ref[0:1, :], vec_ref[1:2, :]
    first, second = back_means(pays, scal, gain, float(x_ref.shape[0]))
    hat = (x_ref[...] - mean) * inverse
    out_ref[...] = add_ref[...] + (yg_ref[...] * gain - first - hat * second) * inverse


def final_norm(scal, yg, x, vec, gain, add, pays):
    return pl.pallas_call(
        final_kernel,
        in_specs=[pl.BlockSpec(memory_space=pltpu.SMEM)]
        + [pl.BlockSpec(memory_space=pltpu.VMEM)] * 6,
        out_specs=pl.BlockSpec(memory_space=pltpu.VMEM),
        out_shape=jax.ShapeDtypeStruct(x.shape, F32),
        compiler_params=pltpu.CompilerParams(vmem_limit_bytes=VMEM_LIMIT),
        cost_estimate=cost(2e9),
        name="final_norm",
    )(scal, yg, x, vec, gain, add, pays)


def split_halves(packed):
    return jnp.concatenate([packed[:, :HD], packed[:, HD:]], axis=0)


def join_halves(values):
    half = values.shape[0] // 2
    return jnp.concatenate([values[:half], values[half:]], axis=1)


def inner_weight_of(w_ref, shard, span):
    rows = C + 8
    weight = jnp.concatenate(
        [w_ref[shard, part * rows : part * rows + C, :].astype(BF) for part in range(3)], axis=1
    )
    bias = jnp.concatenate(
        [w_ref[shard, part * rows + C : part * rows + C + 1, :] for part in range(3)], axis=1
    )
    return weight, bias


def outer_weight_of(w_ref, span):
    rows = 3 * (C + 8)
    return jnp.concatenate(
        [
            jnp.concatenate(
                [
                    w_ref[shard, rows + part * span : rows + (part + 1) * span, :].astype(BF)
                    for part in range(C // span)
                ],
                axis=1,
            )
            for shard in range(w_ref.shape[0])
        ],
        axis=0,
    )


def project_kernel(scal, x_ref, pays, scale_ref, shift_ref, w_ref, out_ref, vec_ref, *, group, shard_heads):
    px = x_ref.shape[0]
    mean, inverse = norm_stats(pays, scal, float(px))
    vec_ref[...] = jnp.concatenate([mean, inverse], axis=0)
    high, low = hilo((x_ref[...] - mean) * inverse * scale_ref[...] + shift_ref[...])
    both = jnp.concatenate([high, low], axis=0)
    portion = px // group
    span = shard_heads * HD
    for shard in range(w_ref.shape[0]):
        weight, bias = inner_weight_of(w_ref, shard, span)
        inner = dot(both, weight)
        inner = inner[:px] + inner[px:] + bias
        for head in range(shard_heads):
            at = head * HD
            query = inner[:, at : at + HD]
            pair = jnp.concatenate(
                [inner[:, span + at : span + at + HD], inner[:, 2 * span + at : 2 * span + at + HD]],
                axis=1,
            )
            for part in range(group):
                slot = (shard * shard_heads + head) * group + part
                rows = slice(part * portion, (part + 1) * portion)
                out_ref[slot, :portion, :] = pair[rows]
                out_ref[slot, portion:, :] = join_halves(query[rows])


def project(scal, x, pays, scale, shift, weights, dims, group):
    px, ways, _ = dims
    portion = px // group
    return pl.pallas_call(
        functools.partial(project_kernel, group=group, shard_heads=NH // weights.shape[0]),
        in_specs=[pl.BlockSpec(memory_space=pltpu.SMEM)]
        + [pl.BlockSpec(memory_space=pltpu.VMEM)] * 5,
        out_specs=[pl.BlockSpec(memory_space=pltpu.VMEM)] * 2,
        out_shape=[
            jax.ShapeDtypeStruct((ways, portion + portion // 2, 2 * HD), F32),
            jax.ShapeDtypeStruct((2, C), F32),
        ],
        compiler_params=pltpu.CompilerParams(vmem_limit_bytes=VMEM_LIMIT),
        cost_estimate=cost(5e9),
        name="project",
    )(scal, x, pays, scale, shift, weights)


def project_back_kernel(
    grad_ref, x_ref, vec_ref, scale_ref, shift_ref, w_ref, cot_sum, ng_ref, wg_ref, sum_ref, *, group, shard_heads
):
    px = x_ref.shape[0]
    hat = (x_ref[...] - vec_ref[0:1, :]) * vec_ref[1:2, :]
    normed_high, normed_low = hilo(hat * scale_ref[...] + shift_ref[...])
    portion = px // group
    span = shard_heads * HD
    grad = jnp.zeros((px, C), F32)
    for shard in range(w_ref.shape[0]):
        columns = [[], [], []]
        for head in range(shard_heads):
            slots = [(shard * shard_heads + head) * group + part for part in range(group)]
            pair = jnp.concatenate([grad_ref[slot, :portion, :] for slot in slots], axis=0)
            query = jnp.concatenate(
                [split_halves(grad_ref[slot, portion:, :]) for slot in slots], axis=0
            )
            columns[0].append(query)
            columns[1].append(pair[:, :HD])
            columns[2].append(pair[:, HD:])
        inner = jnp.concatenate(columns[0] + columns[1] + columns[2], axis=1)
        high, low = hilo(inner)
        weight, _ = inner_weight_of(w_ref, shard, span)
        part = dot_nt(jnp.concatenate([high, low], axis=0), weight)
        grad = grad + part[:px] + part[px:]
        weight_grad = (
            dot_tn(normed_high, high) + dot_tn(normed_high, low) + dot_tn(normed_low, high)
        )
        wg_ref[shard, :C, :] = weight_grad
        wg_ref[shard, C:, :] = jnp.broadcast_to(row_sum(inner), (8, inner.shape[1]))
    ng_ref[...] = grad
    spread_out([row_sum(grad), row_sum(grad * hat), cot_sum[...]], sum_ref)


def project_back(grad, x, vec, scale, shift, weights, cot_sum, dims, group):
    px, ways, _ = dims
    shards = weights.shape[0]
    return pl.pallas_call(
        functools.partial(project_back_kernel, group=group, shard_heads=NH // shards),
        in_specs=[pl.BlockSpec(memory_space=pltpu.VMEM)] * 7,
        out_specs=[pl.BlockSpec(memory_space=pltpu.VMEM)] * 3,
        out_shape=[
            jax.ShapeDtypeStruct((px, C), F32),
            jax.ShapeDtypeStruct((shards, C + 8, 3 * C // shards), F32),
            jax.ShapeDtypeStruct((ways, 3, C), F32),
        ],
        compiler_params=pltpu.CompilerParams(vmem_limit_bytes=VMEM_LIMIT),
        cost_estimate=cost(7e9),
        name="project_back",
    )(grad, x, vec, scale, shift, weights, cot_sum)


def attended_grad_kernel(cot_ref, w_ref, out_ref, sum_ref, *, group):
    cot = cot_ref[...]
    px = cot.shape[0]
    weight = outer_weight_of(w_ref, C // w_ref.shape[0])
    grad = dot_nt(jnp.concatenate(hilo(cot), axis=0), weight)
    grad = grad[:px] + grad[px:]
    portion = px // group
    for head in range(NH):
        for part in range(group):
            rows = slice(part * portion, (part + 1) * portion)
            out_ref[head * group + part] = join_halves(grad[rows, head * HD : (head + 1) * HD])
    sum_ref[...] = row_sum(cot)


def attended_gradient(cot, weights, ways, group):
    px = cot.shape[0]
    return pl.pallas_call(
        functools.partial(attended_grad_kernel, group=group),
        out_shape=[
            jax.ShapeDtypeStruct((ways, px // group // 2, 2 * HD), F32),
            jax.ShapeDtypeStruct((1, C), F32),
        ],
        compiler_params=pltpu.CompilerParams(vmem_limit_bytes=VMEM_LIMIT),
        cost_estimate=cost(3e9),
        name="attended_gradient",
    )(cot, weights)


def output_kernel(att_ref, res_ref, cot_ref, w_ref, bias_ref, out_ref, wg_ref, *, group):
    att = jnp.concatenate(
        [
            jnp.concatenate(
                [split_halves(att_ref[head * group + part]) for part in range(group)], axis=0
            )
            for head in range(NH)
        ],
        axis=1,
    )
    px = att.shape[0]
    high, low = hilo(att)
    weight = outer_weight_of(w_ref, C // w_ref.shape[0])
    out = dot(jnp.concatenate([high, low], axis=0), weight)
    out_ref[...] = res_ref[...] + out[:px] + out[px:] + bias_ref[...]
    cot_high, cot_low = hilo(cot_ref[...])
    wg_ref[...] = dot_tn(high, cot_high) + dot_tn(high, cot_low) + dot_tn(low, cot_high)


def output_step(att, residual, cot, weights, bias, group):
    return pl.pallas_call(
        functools.partial(output_kernel, group=group),
        out_shape=[
            jax.ShapeDtypeStruct(residual.shape, F32),
            jax.ShapeDtypeStruct((NH * HD, C), F32),
        ],
        compiler_params=pltpu.CompilerParams(vmem_limit_bytes=VMEM_LIMIT),
        cost_estimate=cost(4e9),
        name="output_step",
    )(att, residual, cot, weights, bias)


def attention_kernel(*refs, group, sources, portion):
    n0_ref, q_ref, do_ref = refs[:3]
    kv_refs = refs[3 : 3 + group]
    ctx_ref, o_ref, dq_ref = refs[3 + group : 6 + group]
    dkv_refs = refs[6 + group : 6 + 2 * group]
    dctx_ref = refs[6 + 2 * group]
    k4, v4, kt, vt, ck4, cv4, ckt, cvt, s_sc, dk_acc, dv_acc, cdk, cdv = refs[7 + 2 * group :]
    step = pl.program_id(0)
    own = sources * portion
    chunk = own // GRAN
    piece = 512 if own % 512 == 0 else own

    def prepare(kv, k4_at, v4_at):
        kh, kl = hilo(kv[:, :HD])
        vh, vl = hilo(kv[:, HD:])
        k4_at[...] = jnp.concatenate([kh, kl, kh, kl], axis=1)
        v4_at[...] = jnp.concatenate([vh, vl, vh, vl], axis=1)
        high, low = hilo(kv.T)
        return (
            jnp.concatenate([high[:HD], low[:HD]], axis=0),
            jnp.concatenate([high[HD:], low[HD:]], axis=0),
        )

    @pl.when(step == 0)
    def _():
        for way in range(group):
            for start in range(0, own, piece):
                kv = kv_refs[way][start // portion : (start + piece) // portion]
                at = slice(way * own + start, way * own + start + piece)
                kt[:, at], vt[:, at] = prepare(kv.reshape(piece, 2 * HD), k4.at[at], v4.at[at])
        for slot in range(SLOTS):
            ckt[slot], cvt[slot] = prepare(ctx_ref[slot], ck4.at[slot], cv4.at[slot])
        dk_acc[...] = jnp.zeros_like(dk_acc)
        dv_acc[...] = jnp.zeros_like(dv_acc)
        cdk[...] = jnp.zeros_like(cdk)
        cdv[...] = jnp.zeros_like(cdv)

    boundary = n0_ref[0]
    gran = step // (pl.num_programs(0) // GRAN)
    slot = (gran >= boundary).astype(jnp.int32)
    first = jnp.where(slot == 0, 0, boundary)
    last = jnp.where(slot == 0, boundary, GRAN)
    packed = q_ref[...].reshape(2 * HD, 2 * HD)
    turned = packed.T
    turned = jnp.concatenate([turned[:HD], turned[HD:]], axis=1)
    high, low = hilo(turned * (HD**-0.5 * LOG2E))
    q4 = jnp.concatenate([high, high, low, low], axis=0)
    q2 = jnp.concatenate(hilo(split_halves(packed) * HD**-0.5), axis=1)
    do_turned = do_ref[...].reshape(2 * HD, 2 * HD).T
    do_turned = jnp.concatenate([do_turned[:HD], do_turned[HD:]], axis=1)

    def pack_back(values):
        half = values.shape[1] // 2
        return jnp.concatenate([values[:, :half], values[:, half:]], axis=0).T

    def take(high, low, turned_pair):
        both = dot(turned_pair, high)
        return both[:HD] + both[HD:] + dot(turned_pair[:HD], low)

    def places(g):
        return [
            pl.ds(pl.multiple_of(way * own + g * chunk, chunk), chunk) for way in range(group)
        ]

    ctx_scores = dot(ck4[slot], q4)
    token = lax.broadcasted_iota(jnp.int32, ctx_scores.shape, 0)
    ctx_scores = jnp.where(token < CTX_TOK, ctx_scores, -1e30)

    def score_pass(g, top):
        for at in places(g):
            scores = dot(k4[at, :], q4)
            s_sc[at, :] = scores
            top = jnp.maximum(top, jnp.max(scores, axis=0, keepdims=True))
        return top

    top = lax.fori_loop(first, last, score_pass, jnp.max(ctx_scores, axis=0, keepdims=True))
    ctx_p = jnp.exp2(ctx_scores - top)

    def value_pass(g, carry):
        total, out = carry
        for at in places(g):
            p = jnp.exp2(s_sc[at, :] - top)
            s_sc[at, :] = p
            total = total + row_sum(p)
            out = out + take(*hilo(p), vt[:, at])
        return total, out

    total, out = lax.fori_loop(
        first, last, value_pass, (row_sum(ctx_p), take(*hilo(ctx_p), cvt[slot]))
    )
    inverse = 1.0 / total
    out = out * inverse
    o_ref[...] = pack_back(out).reshape(o_ref.shape)
    do_scaled = do_turned * inverse
    diagonal = row_sum(do_scaled * out)
    high, low = hilo(do_scaled)
    d4 = jnp.concatenate([high, high, low, low], axis=0)
    d2 = jnp.concatenate(hilo(split_halves(pack_back(do_scaled))), axis=1)

    def back(p, values, keys_turned):
        ds = p * (dot(values, d4) - diagonal)
        ds_high, ds_low = hilo(ds)
        p_high, p_low = hilo(p)
        dv = dot(p_high, d2) + dot(p_low, d2)
        dk = dot(ds_high, q2) + dot(ds_low, q2)
        return dk, dv, take(ds_high, ds_low, keys_turned)

    dk, dv, dq = back(ctx_p, cv4[slot], ckt[slot])
    cdk[slot] += dk
    cdv[slot] += dv

    def gradient_pass(g, dq):
        for at in places(g):
            dk, dv, part = back(s_sc[at, :], v4[at, :], kt[:, at])
            dk_acc[at, :] += dk
            dv_acc[at, :] += dv
            dq = dq + part
        return dq

    dq = lax.fori_loop(first, last, gradient_pass, dq) * HD**-0.5
    dq_ref[...] = pack_back(dq).reshape(dq_ref.shape)

    def fold(pair):
        return pair[:, :HD] + pair[:, HD:]

    @pl.when(step == pl.num_programs(0) - 1)
    def _():
        for way in range(group):
            for start in range(0, own, piece):
                at = slice(way * own + start, way * own + start + piece)
                joined = jnp.concatenate([fold(dk_acc[at, :]), fold(dv_acc[at, :])], axis=1)
                dkv_refs[way][start // portion : (start + piece) // portion] = joined.reshape(
                    piece // portion, portion, 2 * HD
                )
        for slot in range(SLOTS):
            dctx_ref[slot] = jnp.concatenate([fold(cdk[slot]), fold(cdv[slot])], axis=1)


def attention(boundary, traded, do, others, ctx, group):
    sources = traded.shape[0]
    half = do.shape[1]
    portion = 2 * half
    own = sources * portion
    keys = group * own
    per_step = 2 * HD // half
    steps = sources // per_step
    q_block = pl.BlockSpec((per_step, half, 2 * HD), lambda i: (i, 2, 0))
    side_block = pl.BlockSpec((per_step, half, 2 * HD), lambda i: (i, 0, 0))
    kv_shape = (sources, portion, 2 * HD)
    pair_shape = (SLOTS, CTX_PAD, 2 * HD)
    return pl.pallas_call(
        functools.partial(attention_kernel, group=group, sources=sources, portion=portion),
        grid=(steps,),
        in_specs=[pl.BlockSpec(memory_space=pltpu.SMEM), q_block, side_block]
        + [whole_block(kv_shape)] * group
        + [whole_block(pair_shape)],
        out_specs=[side_block, side_block] + [whole_block(kv_shape)] * group + [whole_block(pair_shape)],
        out_shape=[jax.ShapeDtypeStruct((sources, half, 2 * HD), F32)] * 2
        + [jax.ShapeDtypeStruct(kv_shape, F32)] * group
        + [jax.ShapeDtypeStruct(pair_shape, F32)],
        scratch_shapes=[
            pltpu.VMEM((keys, 4 * HD), BF),
            pltpu.VMEM((keys, 4 * HD), BF),
            pltpu.VMEM((2 * HD, keys), BF),
            pltpu.VMEM((2 * HD, keys), BF),
            pltpu.VMEM((SLOTS, CTX_PAD, 4 * HD), BF),
            pltpu.VMEM((SLOTS, CTX_PAD, 4 * HD), BF),
            pltpu.VMEM((SLOTS, 2 * HD, CTX_PAD), BF),
            pltpu.VMEM((SLOTS, 2 * HD, CTX_PAD), BF),
            pltpu.VMEM((keys, 4 * HD), F32),
            pltpu.VMEM((keys, 2 * HD), F32),
            pltpu.VMEM((keys, 2 * HD), F32),
            pltpu.VMEM(pair_shape, F32),
            pltpu.VMEM(pair_shape, F32),
        ],
        compiler_params=pltpu.CompilerParams(vmem_limit_bytes=VMEM_LIMIT),
        cost_estimate=cost(6e10),
        name="attention",
    )(boundary, traded, do, traded, *others, ctx)


def rotated(values, axis):
    size = lax.axis_size(axis)
    return [values] + [
        lax.ppermute(values, axis, [(i, (i + d) % size) for i in range(size)])
        for d in range(1, size)
    ]


def shared(rows):
    return lax.all_to_all(rows, SEQ, split_axis=0, concat_axis=0, tiled=True)


def turned(values):
    size = lax.axis_size("heads")
    return lax.ppermute(
        values, SEQ, [(r * size + h, h * size + r) for r in range(size) for h in range(size)]
    )


def after(values, *others):
    return lax.optimization_barrier((values, *others))[0]


def halo(edge_low, edge_high):
    size = lax.axis_size("rows") * lax.axis_size("heads")
    forward = [(i, i + 1) for i in range(size - 1)]
    backward = [(i + 1, i) for i in range(size - 1)]
    return lax.ppermute(edge_high, SEQ, forward), lax.ppermute(edge_low, SEQ, backward)


def edges(values):
    return halo(values[:WID], values[-WID:])


def trade(values):
    return lax.all_to_all(values, SEQ, split_axis=0, concat_axis=0, tiled=True)


def per_device(
    pixels,
    crop_slot,
    embedding,
    context,
    first_gain,
    first_offset,
    first_kernel,
    first_bias,
    embed_weight,
    embed_bias,
    second_gain,
    second_offset,
    second_kernel,
    second_bias,
    attend_gain,
    attend_offset,
    inner_weight,
    inner_bias,
    context_weight,
    context_bias,
    outer_weight,
    outer_bias,
    cotangent,
):
    row_count = pixels.shape[0]
    assert pixels.shape[1] == 1
    ranks = lax.axis_size("rows")
    head_ways = lax.axis_size("heads")
    halves = lax.axis_size("dp")
    ways = ranks * head_ways
    group = ways // NH
    px = row_count * WID
    dims = (px, ways, head_ways)
    rank = lax.axis_index("rows")
    head_rank = lax.axis_index("heads")
    joint = rank * head_ways + head_rank
    shard_heads = NH // head_ways
    span = shard_heads * HD
    square = ranks == head_ways and NH // ranks == shard_heads

    slots = crop_slot[:, 0]
    source_slots = slots[::row_count]
    own_slot = slots[joint * row_count]
    above = slots[jnp.maximum(joint * row_count - 1, 0)]
    below = slots[jnp.minimum((joint + 1) * row_count, ROWS_SEQ - 1)]
    top_ok = ((joint > 0) & (above == own_slot)).astype(F32)
    low_ok = ((joint < ways - 1) & (below == own_slot)).astype(F32)
    scal = jnp.concatenate([(source_slots == own_slot).astype(F32), jnp.stack([top_ok, low_ok])])
    slot_rows = (source_slots[None, :] == jnp.arange(SLOTS)[:, None]).astype(F32)
    boundary = (GRAN - jnp.sum(slots[:: ROWS_SEQ // GRAN])).reshape(1).astype(jnp.int32)
    side = lax.axis_index("dp").reshape(1).astype(jnp.int32)

    x = pixels.reshape(px, C)
    cot = cotangent.reshape(px, C)

    def row(vector):
        return vector.reshape(1, C)

    bias_rows = jnp.stack(
        [inner_bias[0].reshape(span), jnp.zeros((span,), F32), inner_bias[1].reshape(span)]
    )
    own_w = jnp.concatenate(
        [
            jnp.concatenate(
                [
                    inner_weight.astype(F32).transpose(1, 0, 2, 3).reshape(3, C, span),
                    jnp.pad(bias_rows[:, None], ((0, 0), (0, 7), (0, 0))),
                ],
                axis=1,
            ).reshape(3 * (C + 8), span),
            outer_weight.astype(F32)
            .reshape(span, C // span, span)
            .transpose(1, 0, 2)
            .reshape(C, span),
        ],
        axis=0,
    )
    head_w = lax.all_gather(own_w, "heads", axis=0, tiled=False)

    mean = jnp.mean(x, axis=0)
    x_stat = jnp.stack([mean, jnp.sum(jnp.square(x - mean), axis=0)])
    pays0 = shared(jnp.broadcast_to(x_stat[None], (ways, 2, C)))
    x_halo = edges(x)
    first_k = first_kernel.reshape(3, 3 * C, C)
    second_k = second_kernel.reshape(3, 3 * C, C)
    conv1, act1, stat1, x_vec = conv_forward(
        scal, x, x_halo, pays0, row(first_gain), row(first_offset), first_k, row(first_bias), None, dims
    )

    embed_act = jax.nn.silu(embedding[0])
    modulation = jnp.dot(embed_act, embed_weight.astype(F32), precision=HIGH) + embed_bias
    own_mod = lax.dynamic_index_in_dim(modulation, own_slot, 0, keepdims=True)
    lift = 1.0 + own_mod[:, :C]
    second_scale = row(second_gain) * lift
    second_shift = row(second_offset) * lift + own_mod[:, C:]
    ctx_flat = context[0].reshape(SLOTS * CTX_TOK, context.shape[-1])
    ctx_pair = jnp.dot(
        ctx_flat,
        context_weight.reshape(context.shape[-1], 2 * span),
        preferred_element_type=F32,
    ).reshape(SLOTS * CTX_TOK, 2, shard_heads, HD)
    ctx_pair = ctx_pair + jnp.stack([jnp.zeros_like(context_bias), context_bias])
    ctx_pair = ctx_pair.transpose(2, 0, 1, 3).reshape(shard_heads, SLOTS * CTX_TOK, 2 * HD)
    own_head = joint // group
    if square:
        ctx_all, at = turned(ctx_pair), own_head % shard_heads
    else:
        ctx_all, at = lax.all_gather(ctx_pair, "heads", axis=0, tiled=True), own_head
    ctx_own = lax.dynamic_index_in_dim(ctx_all, at, 0, keepdims=False)
    ctx_own = jnp.pad(
        ctx_own.reshape(SLOTS, CTX_TOK, 2 * HD), ((0, 0), (0, CTX_PAD - CTX_TOK), (0, 0))
    )

    pays1 = shared(stat1)
    conv1_halo = edges(conv1)
    do_blocks, cot_sum = attended_gradient(cot, head_w, ways, group)
    pays1 = after(pays1, do_blocks, ctx_own)
    residual, act2, stat2, vec1 = conv_forward(
        scal, conv1, conv1_halo, pays1, second_scale, second_shift, second_k, row(second_bias), x, dims
    )
    do_own = trade(do_blocks)

    pays2 = shared(stat2)
    res_halo = edges(residual)
    pays2 = after(pays2, do_own)
    blocks, vec2 = project(
        scal, residual, pays2, row(attend_gain), row(attend_offset), head_w, dims, group
    )
    traded = trade(blocks)
    portion = px // group
    own_kv = traded[:, :portion]

    def mates(d):
        return [(i, i // group * group + (i % group + d) % group) for i in range(ways)]

    def by_heads(values):
        return lax.all_to_all(values, "heads", split_axis=0, concat_axis=0, tiled=True)

    others = [lax.ppermute(own_kv, SEQ, mates(group - d)) for d in range(1, group)]
    act1_parts = by_heads(after(act1, traded))
    act2_parts = by_heads(after(act2, traded))
    cot_halo = edges(after(cot, traded))
    ctx_seqs = rotated(after(ctx_flat.astype(F32), traded), "dp")
    act_seqs = rotated(after(embed_act, traded), "dp")
    results = attention(boundary, traded, do_own, others, ctx_own, group)
    att_own, dq_own = results[:2]
    dkv_parts = list(results[2 : 2 + group])
    ctx_grad = results[2 + group]
    dkv_parts[0] = after(
        dkv_parts[0], act1_parts, act2_parts, cot_halo, tuple(ctx_seqs), tuple(act_seqs)
    )
    dkv = dkv_parts[0]
    for d in range(1, group):
        dkv = dkv + lax.ppermute(dkv_parts[d], SEQ, mates(d))
    grads = trade(jnp.concatenate([dkv, dq_own], axis=1))
    normed_grad, inner_part, sums2 = project_back(
        grads, residual, vec2, row(attend_gain), row(attend_offset), head_w, cot_sum, dims, group
    )

    pays3 = shared(sums2)
    ng_halo = edges(normed_grad)
    attended = trade(after(att_own, grads))
    pays3 = after(pays3, attended)
    residual_grad, hidden_grad, sums1 = conv_backward(
        scal,
        normed_grad,
        ng_halo,
        residual,
        res_halo,
        vec2,
        row(attend_gain),
        pays3,
        [cot, *cot_halo],
        second_k,
        (conv1, vec1, second_scale, second_shift),
        dims,
    )
    pays4 = shared(sums1)
    hg_halo = edges(hidden_grad)
    output, outer_part = output_step(attended, residual, cot, head_w, row(outer_bias), group)
    pays4 = after(pays4, outer_part)
    conv1_grad, pre_grad, sums0 = conv_backward(
        scal,
        hidden_grad,
        hg_halo,
        conv1,
        conv1_halo,
        vec1,
        second_scale,
        pays4,
        None,
        first_k,
        (x, x_vec, row(first_gain), row(first_offset)),
        dims,
    )
    pays5 = shared(sums0)

    def band_of(grad):
        if head_ways != 4:
            return lax.all_gather(grad, "heads", axis=0, tiled=True)
        far = lax.ppermute(grad, "heads", [(i, i ^ 2) for i in range(4)])
        near, diagonal = (
            lax.ppermute(v, "heads", [(i, i ^ 1) for i in range(4)]) for v in (grad, far)
        )
        return jnp.concatenate([grad, near, far, diagonal], axis=0)

    def band_parts(parts):
        if head_ways != 4:
            return parts
        return jnp.concatenate(
            [lax.dynamic_index_in_dim(parts, head_rank ^ d, 0) for d in range(4)], axis=0
        )

    def kernel_parts(parts, band):
        return kernel_grad(side, band_parts(parts), band, ranks, halves == 2)

    def kernel_total(parts):
        taps = []
        for tap in range(3):
            if halves == 2:
                mine, other = parts[2 * tap : 2 * tap + 2]
                total = mine + lax.ppermute(other, "dp", [(0, 1), (1, 0)])
            else:
                total = lax.psum_scatter(parts[tap], "dp", scatter_dimension=2, tiled=True)
            taps.append(
                jnp.sum(lax.all_to_all(total, "rows", split_axis=0, concat_axis=0), axis=0)
            )
        return jnp.stack(taps).reshape(3, 3, C // ways, C // halves)

    second_parts = kernel_parts(act2_parts, band_of(residual_grad))
    pays5 = after(pays5, second_parts[0])
    pixels_grad = final_norm(scal, pre_grad, x, x_vec, row(first_gain), residual_grad, pays5)
    second_kernel_grad = kernel_total(second_parts)
    first_kernel_grad = kernel_total(kernel_parts(act1_parts, band_of(conv1_grad)))

    outer_sum = lax.psum_scatter(outer_part, "heads", scatter_dimension=0, tiled=True)
    inner_sum = lax.psum_scatter(inner_part, "heads", scatter_dimension=0, tiled=True)
    inner_sum, outer_sum = lax.psum((inner_sum, outer_sum), ("dp", "rows"))
    inner_sum = inner_sum.reshape(C + 8, 3 * span)
    inner_weight_grad = inner_sum[:C].reshape(C, 3, shard_heads, HD)
    bias_sum = inner_sum[C].reshape(3, shard_heads, HD)
    inner_bias_grad = jnp.stack([bias_sum[0], bias_sum[2]])
    outer_weight_grad = outer_sum.reshape(shard_heads, HD, C)

    ctx_grad = ctx_grad[:, :CTX_TOK].reshape(SLOTS * CTX_TOK, 2 * HD)
    if square:
        ctx_grads = jnp.stack(rotated(ctx_grad, "heads"))
        ctx_order = (head_rank - jnp.arange(head_ways)) % head_ways // group
        ctx_row = jnp.stack(
            [
                jnp.sum(jnp.where((ctx_order == head)[:, None, None], ctx_grads, 0.0), axis=0)
                for head in range(shard_heads)
            ]
        )
        ctx_mine = turned(ctx_row)
    else:
        ctx_grads = lax.all_gather(ctx_grad, SEQ, axis=0, tiled=False)
        ctx_grads = jnp.sum(ctx_grads.reshape(NH, group, SLOTS * CTX_TOK, 2 * HD), axis=1)
        ctx_mine = lax.dynamic_slice_in_dim(ctx_grads, head_rank * shard_heads, shard_heads, 0)
    ctx_mine = (
        ctx_mine.reshape(shard_heads, SLOTS * CTX_TOK, 2, HD)
        .transpose(1, 2, 0, 3)
        .reshape(SLOTS * CTX_TOK, 2 * span)
    )
    mine_seqs = rotated(ctx_mine, "dp")
    context_weight_grad = jnp.dot(
        jnp.concatenate(ctx_seqs, axis=0).T, jnp.concatenate(mine_seqs, axis=0), precision=HIGH
    ).reshape(context.shape[-1], 2, shard_heads, HD)
    context_bias_grad = jnp.sum(sum(mine_seqs), axis=0).reshape(2, shard_heads, HD)[1]

    attend_sums = jnp.sum(pays3, axis=0)
    by_slot = jnp.einsum("ks,src->krc", slot_rows, pays4, precision=HIGH)
    shift_grad, hat_grad = by_slot[:, 0], by_slot[:, 1]
    mod_lift = 1.0 + modulation[:, :C]
    scale_grad = hat_grad * second_gain + shift_grad * second_offset
    pack = jnp.concatenate(
        [
            attend_sums,
            jnp.stack(
                [
                    jnp.sum(hat_grad * mod_lift, axis=0),
                    jnp.sum(shift_grad * mod_lift, axis=0),
                    jnp.sum(by_slot[:, 2], axis=0),
                ]
            ),
            scale_grad,
            shift_grad,
        ],
        axis=0,
    )
    packs = rotated(pack, "dp")
    vectors = sum(packs)
    mod_grads = jnp.concatenate(
        [jnp.concatenate([p[6 : 6 + SLOTS], p[6 + SLOTS :]], axis=1) for p in packs], axis=0
    )
    embed_bias_grad = jnp.sum(mod_grads, axis=0)
    embed_rows = embed_weight.shape[0] // ways
    embed_cols = 2 * C // halves
    embed_weight_grad = jnp.einsum(
        "ke,kc->ec",
        lax.dynamic_slice_in_dim(jnp.concatenate(act_seqs, axis=0), joint * embed_rows, embed_rows, 1),
        lax.dynamic_slice_in_dim(mod_grads, lax.axis_index("dp") * embed_cols, embed_cols, 1),
        precision=HIGH,
    )
    first_sums = sum(rotated(jnp.sum(pays5, axis=0), "dp"))

    shape = pixels.shape
    return (
        output.reshape(shape),
        pixels_grad.reshape(shape),
        first_sums[1],
        first_sums[0],
        first_kernel_grad,
        first_sums[2],
        embed_weight_grad,
        embed_bias_grad,
        vectors[3],
        vectors[4],
        second_kernel_grad,
        vectors[5],
        vectors[1],
        vectors[0],
        inner_weight_grad,
        inner_bias_grad,
        context_weight_grad,
        context_bias_grad,
        outer_weight_grad,
        vectors[2],
    )


def solution(mesh):
    band = P(SEQ, "dp", None, None)
    kernel_out = P(None, None, SEQ, "dp")
    return jax.shard_map(
        per_device,
        mesh=mesh,
        in_specs=(
            band,
            P(None, "dp"),
            P("dp", None, None),
            P("dp", None, None, None),
            P(),
            P(),
            P(),
            P(),
            P(),
            P(),
            P(),
            P(),
            P(),
            P(),
            P(),
            P(),
            P(None, None, "heads", None),
            P(None, "heads", None),
            P(None, None, "heads", None),
            P("heads", None),
            P("heads", None, None),
            P(),
            band,
        ),
        out_specs=(
            band,
            band,
            P(),
            P(),
            kernel_out,
            P(),
            P(SEQ, "dp"),
            P(),
            P(),
            P(),
            kernel_out,
            P(),
            P(),
            P(),
            P(None, None, "heads", None),
            P(None, "heads", None),
            P(None, None, "heads", None),
            P("heads", None),
            P("heads", None, None),
            P(),
        ),
        check_vma=False,
    )
```

```python
import functools

import jax
import jax.numpy as jnp
from jax import lax
from jax.experimental import pallas as pl
from jax.experimental.pallas import tpu as pltpu
from jax.sharding import PartitionSpec as P

C = 512
NH = 8
HD = 64
GROUPS = 32
GROUP_C = C // GROUPS
CTX_TOK = 81
CTX_PAD = 128
GRAD_ROWS = 576
WID = 64
SLOTS = 2
ROWS_SEQ = 64
GRAN = 4
EPS = 1e-05
LOG2E = 1.4426950408889634
F32 = jnp.float32
BF = jnp.bfloat16
SEQ = ("rows", "heads")
HIGH = lax.Precision.HIGHEST
VMEM_LIMIT = 56 << 20


def hilo(values):
    high = values.astype(BF)
    return high, (values - high.astype(F32)).astype(BF)


def dot(left, right):
    return jnp.dot(left, right, preferred_element_type=F32)


def dot_nt(left, right):
    return lax.dot_general(left, right, (((1,), (1,)), ((), ())), preferred_element_type=F32)


def dot_tn(left, right):
    return lax.dot_general(left, right, (((0,), (0,)), ((), ())), preferred_element_type=F32)


def group_mean(values):
    lane = lax.broadcasted_iota(jnp.int32, values.shape, 1)
    for step in (1, 2, 4, 8):
        up = pltpu.roll(values, step, 1)
        down = pltpu.roll(values, C - step, 1)
        values = values + jnp.where((lane & step) != 0, up, down)
    return values * (1.0 / GROUP_C)


def wide(row):
    return jnp.broadcast_to(row, (8, C))


def scalars(info, ranks, rows):
    rank, joint = info[ROWS_SEQ], info[ROWS_SEQ + 1]
    band = ROWS_SEQ // ranks
    own = info[joint * rows]
    found = []
    for step in range(ranks):
        other = rank - step
        other = jnp.where(other < 0, other + ranks, other)
        found.append(info[other * band] == own)
    first, last = joint * rows, joint * rows + rows
    found.append((first > 0) & (info[jnp.maximum(first - 1, 0)] == own))
    found.append((last < ROWS_SEQ) & (info[jnp.minimum(last, ROWS_SEQ - 1)] == own))
    return [jnp.where(item, 1.0, 0.0).astype(F32) for item in found]


def norm_stats(pays, scal, px):
    count = sum(scal[i] for i in range(len(pays)))
    mean = sum(scal[i] * wide(pay[0:1, :]) for i, pay in enumerate(pays)) / count
    spread = sum(
        scal[i] * (wide(pay[1:2, :]) + px * jnp.square(wide(pay[0:1, :]) - mean))
        for i, pay in enumerate(pays)
    )
    total = count * px
    center = group_mean(mean)
    variance = group_mean(spread + total * jnp.square(mean - center)) / total
    return center[0:1], (1.0 / jnp.sqrt(variance + EPS))[0:1]


def back_means(pays, scal, gain, px):
    count = sum(scal[i] for i in range(len(pays))) * px
    first = sum(scal[i] * wide(pay[0:1, :]) for i, pay in enumerate(pays))
    second = sum(scal[i] * wide(pay[1:2, :]) for i, pay in enumerate(pays))
    return (group_mean(first * gain) / count)[0:1], (group_mean(second * gain) / count)[0:1]


def local_stats(values):
    mean = jnp.mean(values, axis=0, keepdims=True)
    return mean, jnp.sum(jnp.square(values - mean), axis=0, keepdims=True)


def row_sum(values):
    return jnp.sum(values, axis=0, keepdims=True)


def shifted(values, tap):
    if tap == 1:
        return values
    column = lax.broadcasted_iota(jnp.int32, values.shape, 0) % WID
    rows = values.shape[0]
    if tap == 0:
        return jnp.where(column == 0, 0.0, pltpu.roll(values, 1, 0))
    return jnp.where(column == WID - 1, 0.0, pltpu.roll(values, rows - 1, 0))


def fill_taps(values, high_ref, low_ref, row, width):
    for tap in range(3):
        high, low = hilo(shifted(values, tap))
        high_ref[row : row + values.shape[0], tap * width : (tap + 1) * width] = high
        low_ref[row : row + values.shape[0], tap * width : (tap + 1) * width] = low


def conv_forward_kernel(*refs, px, ways, ranks, has_skip):
    info, x_ref, top_ref, low_ref = refs[:4]
    pays = refs[4 : 4 + ranks]
    scale_ref, shift_ref, w_ref, bias_ref = refs[4 + ranks : 8 + ranks]
    rest = refs[8 + ranks :]
    band_px = float(px * (ways // ranks))
    if has_skip:
        skip_ref, rest = rest[0], rest[1:]
    out_ref, act_ref, stat_ref, vec_ref, high_sc, low_sc, acc = rest
    tap = pl.program_id(0)
    block = C // ways

    @pl.when(tap == 0)
    def _():
        scal = scalars(info, ranks, px // WID)
        mean, inverse = norm_stats(pays, scal, band_px)
        vec_ref[...] = jnp.concatenate([mean, inverse], axis=0)
        scale = scale_ref[...]
        shift = shift_ref[...]
        heads_count = act_ref.shape[0]

        def activate(values, weight, row):
            pre = (values - mean) * inverse * scale + shift
            act = pre / (1.0 + jnp.exp(-pre))
            if weight is not None:
                act = act * weight
            size = values.shape[0]
            fill_taps(act, high_sc, low_sc, row, C)
            for head in range(heads_count):
                act_ref[head, row : row + size, :] = jnp.concatenate(
                    [
                        act[:, (r * heads_count + head) * block : (r * heads_count + head + 1) * block]
                        for r in range(ways // heads_count)
                    ],
                    axis=1,
                )

        activate(top_ref[...], scal[ranks], 0)
        for row in range(px // WID):
            activate(x_ref[row * WID : (row + 1) * WID, :], None, (row + 1) * WID)
        activate(low_ref[...], scal[ranks + 1], px + WID)

    base = pl.multiple_of(tap * WID, WID)
    part = dot(
        jnp.concatenate([high_sc[pl.ds(base, px), :], low_sc[pl.ds(base, px), :]], axis=0), w_ref[0]
    )
    part = part[:px] + part[px:]

    @pl.when(tap == 0)
    def _():
        acc[...] = part

    @pl.when(tap == 1)
    def _():
        acc[...] += part

    @pl.when(tap == 2)
    def _():
        out = acc[...] + part + bias_ref[...]
        if has_skip:
            out = out + skip_ref[...]
        out_ref[...] = out
        stat_ref[...] = jnp.concatenate(local_stats(out), axis=0)


def cost(flops):
    return pl.CostEstimate(flops=int(flops), transcendentals=0, bytes_accessed=0)


def whole_block(shape):
    return pl.BlockSpec(shape, lambda *_: (0,) * len(shape), pipeline_mode=pl.Buffered(1))


def conv_forward(info, x, halo, pays, scale, shift, kernel, bias, skip, dims):
    px, ways, head_ways = dims
    ranks = len(pays)
    quarter = C // head_ways
    operands = [info, x, halo[0], halo[1], *pays, scale, shift, kernel, bias]
    specs = (
        [pl.BlockSpec(memory_space=pltpu.SMEM), whole_block((px, C))]
        + [whole_block((WID, C))] * 2
        + [whole_block(pays[0].shape)] * ranks
        + [whole_block((1, C))] * 2
        + [pl.BlockSpec((1, 3 * C, C), lambda i: (i, 0, 0)), whole_block((1, C))]
    )
    if skip is not None:
        operands.append(skip)
        specs.append(whole_block((px, C)))
    ext = px + 2 * WID
    return pl.pallas_call(
        functools.partial(
            conv_forward_kernel,
            px=px,
            ways=ways,
            ranks=ranks,
            has_skip=skip is not None,
        ),
        grid=(3,),
        in_specs=specs,
        out_specs=[
            whole_block((px, C)),
            whole_block((head_ways, ext, quarter)),
            whole_block((2, C)),
            whole_block((2, C)),
        ],
        out_shape=[
            jax.ShapeDtypeStruct((px, C), F32),
            jax.ShapeDtypeStruct((head_ways, ext, quarter), F32),
            jax.ShapeDtypeStruct((2, C), F32),
            jax.ShapeDtypeStruct((2, C), F32),
        ],
        scratch_shapes=[
            pltpu.VMEM((ext, 3 * C), BF),
            pltpu.VMEM((ext, 3 * C), BF),
            pltpu.VMEM((px, C), F32),
        ],
        compiler_params=pltpu.CompilerParams(vmem_limit_bytes=VMEM_LIMIT),
        cost_estimate=cost(7e9),
        name="conv_forward",
    )(*operands)


def halves_of(info, values, split):
    if not split:
        return [values]
    even = info[ROWS_SEQ + 2] == 0
    left, right = values[:, : C // 2], values[:, C // 2 :]
    return [jnp.where(even, left, right), jnp.where(even, right, left)]


def conv_backward_kernel(*refs, px, ways, ranks, has_add, split):
    info, yg_ref, yg_top, yg_low, x_ref, x_top, x_low, vec_ref, gain_ref = refs[:9]
    pays = refs[9 : 9 + ranks]
    rest = refs[9 + ranks :]
    band_px = float(px * (ways // ranks))
    if has_add:
        adds, rest = rest[:3], rest[3:]
    w_ref, in_ref, in_vec, in_scale, in_shift = rest[:5]
    g_refs = rest[5 : 7 if split else 6]
    h_ref, sum_ref, high_sc, low_sc, acc, bias_sum = rest[7 if split else 6 :]
    tap = pl.program_id(0)

    @pl.when(tap == 0)
    def _():
        scal = scalars(info, ranks, px // WID)
        gain = gain_ref[...]
        mean, inverse = vec_ref[0:1, :], vec_ref[1:2, :]
        first, second = back_means(pays, scal, gain, band_px)

        def gradient(yg, x, extra, weight, row):
            grad = (yg * gain - first - (x - mean) * inverse * second) * inverse
            if extra is not None:
                grad = grad + extra
            if weight is not None:
                grad = grad * weight
            fill_taps(grad, high_sc, low_sc, row, C)
            return grad

        gradient(yg_top[...], x_top[...], adds[1][...] if has_add else None, scal[ranks], 0)
        total = jnp.zeros((1, C), F32)
        for row in range(px // WID):
            at = slice(row * WID, (row + 1) * WID)
            grad = gradient(
                yg_ref[at, :],
                x_ref[at, :],
                adds[0][at, :] if has_add else None,
                None,
                (row + 1) * WID,
            )
            for ref, piece in zip(g_refs, halves_of(info, grad, split)):
                ref[at, :] = piece
            total = total + row_sum(grad)
        gradient(
            yg_low[...], x_low[...], adds[2][...] if has_add else None, scal[ranks + 1], px + WID
        )
        bias_sum[...] = total
        acc[...] = jnp.zeros_like(acc)

    base = pl.multiple_of(tap * WID, WID)
    part = acc[...]
    for col in range(3):
        weight = w_ref[0, (2 - col) * C : (3 - col) * C, :]
        at = (pl.ds(base, px), slice(col * C, (col + 1) * C))
        both = dot_nt(jnp.concatenate([high_sc[at], low_sc[at]], axis=0), weight)
        part = part + both[:px] + both[px:]
    acc[...] = part

    @pl.when(tap == 2)
    def _():
        hat = (in_ref[...] - in_vec[0:1, :]) * in_vec[1:2, :]
        pre = hat * in_scale[...] + in_shift[...]
        sigmoid = 1.0 / (1.0 + jnp.exp(-pre))
        h = acc[...] * (sigmoid * (1.0 + pre * (1.0 - sigmoid)))
        h_ref[...] = h
        sum_ref[...] = jnp.concatenate([row_sum(h), row_sum(h * hat), bias_sum[...]], axis=0)


def conv_backward(info, yg, yg_halo, x, x_halo, vec, gain, pays, adds, kernel, inner, dims, split):
    px, ways, _ = dims
    ranks = len(pays)
    in_x, in_vec, in_scale, in_shift = inner
    rows3 = [whole_block((px, C)), whole_block((WID, C)), whole_block((WID, C))]
    operands = [info, yg, *yg_halo, x, *x_halo, vec, gain, *pays]
    specs = (
        [pl.BlockSpec(memory_space=pltpu.SMEM)]
        + rows3
        + rows3
        + [whole_block((2, C)), whole_block((1, C))]
        + [whole_block(pays[0].shape)] * ranks
    )
    if adds is not None:
        operands += adds
        specs += rows3
    operands += [kernel, in_x, in_vec, in_scale, in_shift]
    specs += [
        pl.BlockSpec((1, 3 * C, C), lambda i: (2 - i, 0, 0)),
        whole_block((px, C)),
        whole_block((2, C)),
        whole_block((1, C)),
        whole_block((1, C)),
    ]
    ext = px + 2 * WID
    shapes = [(px, C // 2)] * 2 if split else [(px, C)]
    shapes += [(px, C), (3, C)]
    return pl.pallas_call(
        functools.partial(
            conv_backward_kernel,
            px=px,
            ways=ways,
            ranks=ranks,
            has_add=adds is not None,
            split=split,
        ),
        grid=(3,),
        in_specs=specs,
        out_specs=[whole_block(shape) for shape in shapes],
        out_shape=[jax.ShapeDtypeStruct(shape, F32) for shape in shapes],
        scratch_shapes=[
            pltpu.VMEM((ext, 3 * C), BF),
            pltpu.VMEM((ext, 3 * C), BF),
            pltpu.VMEM((px, C), F32),
            pltpu.VMEM((1, C), F32),
        ],
        compiler_params=pltpu.CompilerParams(vmem_limit_bytes=VMEM_LIMIT),
        cost_estimate=cost(7e9),
        name="conv_backward",
    )(*operands)


def kernel_grad_kernel(info, *refs, ranks, seqs, grad_count):
    acts, grads = refs[:seqs], refs[seqs : seqs + grad_count]
    out_ref, taps, g_high, g_low = refs[seqs + grad_count :]
    tap = pl.program_id(0)
    parts, _, ext, quarter = acts[0].shape
    px = ext - 2 * WID
    block = quarter // ranks

    @pl.when(tap == 0)
    def _():
        for seq in range(seqs):
            for part in range(parts):
                at = seq * parts + part
                act = acts[seq][info[ROWS_SEQ + 3 + part], 0]
                for col in range(3):
                    high, low = hilo(shifted(act, col))
                    taps[at, :, col * quarter : (col + 1) * quarter] = high
                    taps[at, :, (3 + col) * quarter : (4 + col) * quarter] = low
                rows = slice(at * px, (at + 1) * px)
                high, low = hilo(grads[at][...] if grad_count > 1 else grads[0][rows, :])
                g_high[rows, :] = high
                g_low[rows, :] = low

    base = pl.multiple_of(tap * WID, WID)
    left = jnp.concatenate([taps[at, pl.ds(base, px), :] for at in range(seqs * parts)], axis=0)
    both = dot_tn(left, g_high[...])
    rest = dot_tn(left[:, : 3 * quarter], g_low[...])
    total = both[: 3 * quarter] + both[3 * quarter :] + rest
    for rank in range(ranks):
        for col in range(3):
            start = col * quarter + rank * block
            out_ref[rank, 0, col * block : (col + 1) * block, :] = total[start : start + block]


def kernel_grad(info, acts, which, grads, ranks):
    parts, _, ext, quarter = acts[0].shape
    px = ext - 2 * WID
    cols = grads[0].shape[1]
    block = 3 * quarter // ranks
    seqs = len(acts)
    return pl.pallas_call(
        functools.partial(kernel_grad_kernel, ranks=ranks, seqs=seqs, grad_count=len(grads)),
        grid=(3,),
        in_specs=[pl.BlockSpec(memory_space=pltpu.SMEM)]
        + [
            pl.BlockSpec(
                (parts, 1, ext, quarter),
                lambda i, at=at: (0, at, 0, 0),
                pipeline_mode=pl.Buffered(1),
            )
            for at in which
        ]
        + [whole_block(grad.shape) for grad in grads],
        out_specs=pl.BlockSpec((ranks, 1, block, cols), lambda i: (0, i, 0, 0)),
        out_shape=jax.ShapeDtypeStruct((ranks, 3, block, cols), F32),
        scratch_shapes=[
            pltpu.VMEM((seqs * parts, ext, 6 * quarter), BF),
            pltpu.VMEM((seqs * parts * px, cols), BF),
            pltpu.VMEM((seqs * parts * px, cols), BF),
        ],
        compiler_params=pltpu.CompilerParams(vmem_limit_bytes=VMEM_LIMIT),
        cost_estimate=cost(6e9),
        name="kernel_grad",
    )(info, *acts, *grads)


def final_kernel(info, yg_ref, x_ref, vec_ref, gain_ref, *refs, band_px, count):
    adds, pays, out_ref = refs[:count], refs[count:-1], refs[-1]
    add = adds[0][...]
    if count == 2:
        even = info[ROWS_SEQ + 2] == 0
        other = adds[1][...]
        add = jnp.concatenate([jnp.where(even, add, other), jnp.where(even, other, add)], axis=1)
    scal = scalars(info, len(pays), x_ref.shape[0] // WID)
    gain = gain_ref[...]
    mean, inverse = vec_ref[0:1, :], vec_ref[1:2, :]
    first, second = back_means(pays, scal, gain, band_px)
    hat = (x_ref[...] - mean) * inverse
    out_ref[...] = add + (yg_ref[...] * gain - first - hat * second) * inverse


def final_norm(info, yg, x, vec, gain, adds, pays, dims):
    px, ways, _ = dims
    return pl.pallas_call(
        functools.partial(
            final_kernel, band_px=float(px * (ways // len(pays))), count=len(adds)
        ),
        in_specs=[pl.BlockSpec(memory_space=pltpu.SMEM)]
        + [pl.BlockSpec(memory_space=pltpu.VMEM)] * (4 + len(adds) + len(pays)),
        out_specs=pl.BlockSpec(memory_space=pltpu.VMEM),
        out_shape=jax.ShapeDtypeStruct(x.shape, F32),
        compiler_params=pltpu.CompilerParams(vmem_limit_bytes=VMEM_LIMIT),
        cost_estimate=cost(2e9),
        name="final_norm",
    )(info, yg, x, vec, gain, *adds, *pays)


def split_halves(packed):
    return jnp.concatenate([packed[:, :HD], packed[:, HD:]], axis=0)


def join_halves(values):
    half = values.shape[0] // 2
    return jnp.concatenate([values[:half], values[half:]], axis=1)


def inner_weight_of(w_ref, shard, span):
    rows = C + 8
    weight = jnp.concatenate(
        [w_ref[shard, part * rows : part * rows + C, :].astype(BF) for part in range(3)], axis=1
    )
    bias = jnp.concatenate(
        [w_ref[shard, part * rows + C : part * rows + C + 1, :] for part in range(3)], axis=1
    )
    return weight, bias


def outer_weight_of(w_ref, span):
    return jnp.concatenate(
        [
            jnp.concatenate(
                [
                    w_ref[shard, part * span : (part + 1) * span, :].astype(BF)
                    for part in range(C // span)
                ],
                axis=1,
            )
            for shard in range(w_ref.shape[0])
        ],
        axis=0,
    )


def project_kernel(info, x_ref, scale_ref, shift_ref, w_ref, *refs, group, shard_heads, band_px):
    pays, (out_ref, vec_ref) = refs[:-2], refs[-2:]
    px = x_ref.shape[0]
    scal = scalars(info, len(pays), px // WID)
    mean, inverse = norm_stats(pays, scal, band_px)
    vec_ref[...] = jnp.concatenate([mean, inverse], axis=0)
    high, low = hilo((x_ref[...] - mean) * inverse * scale_ref[...] + shift_ref[...])
    both = jnp.concatenate([high, low], axis=0)
    portion = px // group
    span = shard_heads * HD
    for shard in range(w_ref.shape[0]):
        weight, bias = inner_weight_of(w_ref, shard, span)
        inner = dot(both, weight)
        inner = inner[:px] + inner[px:] + bias
        for head in range(shard_heads):
            at = head * HD
            query = inner[:, at : at + HD]
            pair = jnp.concatenate(
                [inner[:, span + at : span + at + HD], inner[:, 2 * span + at : 2 * span + at + HD]],
                axis=1,
            )
            for part in range(group):
                slot = (shard * shard_heads + head) * group + part
                rows = slice(part * portion, (part + 1) * portion)
                out_ref[slot, :portion, :] = pair[rows]
                out_ref[slot, portion:, :] = join_halves(query[rows])


def project(info, x, pays, scale, shift, weights, dims, group):
    px, ways, _ = dims
    portion = px // group
    return pl.pallas_call(
        functools.partial(
            project_kernel,
            group=group,
            shard_heads=NH // weights.shape[0],
            band_px=float(px * (ways // len(pays))),
        ),
        in_specs=[pl.BlockSpec(memory_space=pltpu.SMEM)]
        + [pl.BlockSpec(memory_space=pltpu.VMEM)] * (4 + len(pays)),
        out_specs=[pl.BlockSpec(memory_space=pltpu.VMEM)] * 2,
        out_shape=[
            jax.ShapeDtypeStruct((ways, portion + portion // 2, 2 * HD), F32),
            jax.ShapeDtypeStruct((2, C), F32),
        ],
        compiler_params=pltpu.CompilerParams(vmem_limit_bytes=VMEM_LIMIT),
        cost_estimate=cost(5e9),
        name="project",
    )(info, x, scale, shift, weights, *pays)


def project_back_kernel(
    grad_ref, x_ref, vec_ref, scale_ref, shift_ref, w_ref, cot_sum, ng_ref, sum_ref, wg_ref, *, group, shard_heads
):
    px = x_ref.shape[0]
    hat = (x_ref[...] - vec_ref[0:1, :]) * vec_ref[1:2, :]
    normed_high, normed_low = hilo(hat * scale_ref[...] + shift_ref[...])
    portion = px // group
    span = shard_heads * HD
    grad = jnp.zeros((px, C), F32)
    for shard in range(w_ref.shape[0]):
        columns = [[], [], []]
        for head in range(shard_heads):
            slots = [(shard * shard_heads + head) * group + part for part in range(group)]
            pair = jnp.concatenate([grad_ref[slot, :portion, :] for slot in slots], axis=0)
            query = jnp.concatenate(
                [split_halves(grad_ref[slot, portion:, :]) for slot in slots], axis=0
            )
            columns[0].append(query)
            columns[1].append(pair[:, :HD])
            columns[2].append(pair[:, HD:])
        inner = jnp.concatenate(columns[0] + columns[1] + columns[2], axis=1)
        high, low = hilo(inner)
        weight, _ = inner_weight_of(w_ref, shard, span)
        part = dot_nt(jnp.concatenate([high, low], axis=0), weight)
        grad = grad + part[:px] + part[px:]
        weight_grad = (
            dot_tn(normed_high, high) + dot_tn(normed_high, low) + dot_tn(normed_low, high)
        )
        bias_grad = jnp.broadcast_to(row_sum(inner), (GRAD_ROWS - C, inner.shape[1]))
        tall = jnp.concatenate([weight_grad, bias_grad], axis=0)
        wg_ref[shard] = jnp.concatenate(
            [tall[:, part * span : (part + 1) * span] for part in range(3)], axis=0
        )
    ng_ref[...] = grad
    sum_ref[...] = jnp.concatenate([row_sum(grad), row_sum(grad * hat), cot_sum[...]], axis=0)


def project_back(grad, x, vec, scale, shift, weights, cot_sum, dims, group):
    px, _, head_ways = dims
    shape = (head_ways, 3 * GRAD_ROWS, C // head_ways)
    return pl.pallas_call(
        functools.partial(project_back_kernel, group=group, shard_heads=NH // head_ways),
        in_specs=[pl.BlockSpec(memory_space=pltpu.VMEM)] * 7,
        out_specs=[pl.BlockSpec(memory_space=pltpu.VMEM)] * 3,
        out_shape=[
            jax.ShapeDtypeStruct((px, C), F32),
            jax.ShapeDtypeStruct((3, C), F32),
            jax.ShapeDtypeStruct(shape, F32),
        ],
        compiler_params=pltpu.CompilerParams(vmem_limit_bytes=VMEM_LIMIT),
        cost_estimate=cost(7e9),
        name="project_back",
    )(grad, x, vec, scale, shift, weights, cot_sum)


def attended_grad_kernel(cot_ref, w_ref, out_ref, sum_ref, *, group):
    cot = cot_ref[...]
    px = cot.shape[0]
    weight = outer_weight_of(w_ref, C // w_ref.shape[0])
    grad = dot_nt(jnp.concatenate(hilo(cot), axis=0), weight)
    grad = grad[:px] + grad[px:]
    portion = px // group
    for head in range(NH):
        for part in range(group):
            rows = slice(part * portion, (part + 1) * portion)
            out_ref[head * group + part] = join_halves(grad[rows, head * HD : (head + 1) * HD])
    sum_ref[...] = row_sum(cot)


def attended_gradient(cot, weights, ways, group):
    px = cot.shape[0]
    return pl.pallas_call(
        functools.partial(attended_grad_kernel, group=group),
        out_shape=[
            jax.ShapeDtypeStruct((ways, px // group // 2, 2 * HD), F32),
            jax.ShapeDtypeStruct((1, C), F32),
        ],
        compiler_params=pltpu.CompilerParams(vmem_limit_bytes=VMEM_LIMIT),
        cost_estimate=cost(3e9),
        name="attended_gradient",
    )(cot, weights)


def output_kernel(att_ref, res_ref, cot_ref, w_ref, bias_ref, out_ref, wg_ref, *, group):
    att = jnp.concatenate(
        [
            jnp.concatenate(
                [split_halves(att_ref[head * group + part]) for part in range(group)], axis=0
            )
            for head in range(NH)
        ],
        axis=1,
    )
    px = att.shape[0]
    high, low = hilo(att)
    weight = outer_weight_of(w_ref, C // w_ref.shape[0])
    out = dot(jnp.concatenate([high, low], axis=0), weight)
    out_ref[...] = res_ref[...] + out[:px] + out[px:] + bias_ref[...]
    cot_high, cot_low = hilo(cot_ref[...])
    grad = dot_tn(high, cot_high) + dot_tn(high, cot_low) + dot_tn(low, cot_high)
    shards, _, span = wg_ref.shape
    for shard in range(shards):
        mine = grad[shard * span : (shard + 1) * span]
        wg_ref[shard] = jnp.concatenate(
            [mine[:, part * span : (part + 1) * span] for part in range(C // span)], axis=0
        )


def output_step(att, residual, cot, weights, bias, dims, group):
    head_ways = dims[2]
    return pl.pallas_call(
        functools.partial(output_kernel, group=group),
        out_shape=[
            jax.ShapeDtypeStruct(residual.shape, F32),
            jax.ShapeDtypeStruct((head_ways, C, C // head_ways), F32),
        ],
        compiler_params=pltpu.CompilerParams(vmem_limit_bytes=VMEM_LIMIT),
        cost_estimate=cost(4e9),
        name="output_step",
    )(att, residual, cot, weights, bias)


def attention_kernel(*refs, group, sources, portion):
    info, q_ref, do_ref = refs[:3]
    kv_refs = refs[3 : 3 + group]
    ctx_ref, o_ref, dq_ref = refs[3 + group : 6 + group]
    dkv_refs = refs[6 + group : 6 + 2 * group]
    dctx_ref = refs[6 + 2 * group]
    k4, v4, kt, vt, ck4, cv4, ckt, cvt, s_sc, dk_acc, dv_acc, cdk, cdv = refs[7 + 2 * group :]
    step = pl.program_id(0)
    own = sources * portion
    chunk = own // GRAN
    piece = 512 if own % 512 == 0 else own

    def prepare(kv, k4_at, v4_at):
        kh, kl = hilo(kv[:, :HD])
        vh, vl = hilo(kv[:, HD:])
        k4_at[...] = jnp.concatenate([kh, kl, kh, kl], axis=1)
        v4_at[...] = jnp.concatenate([vh, vl, vh, vl], axis=1)
        high, low = hilo(kv.T)
        return (
            jnp.concatenate([high[:HD], low[:HD]], axis=0),
            jnp.concatenate([high[HD:], low[HD:]], axis=0),
        )

    @pl.when(step == 0)
    def _():
        for way in range(group):
            for start in range(0, own, piece):
                kv = kv_refs[way][start // portion : (start + piece) // portion]
                at = slice(way * own + start, way * own + start + piece)
                kt[:, at], vt[:, at] = prepare(kv.reshape(piece, 2 * HD), k4.at[at], v4.at[at])
        for slot in range(SLOTS):
            ckt[slot], cvt[slot] = prepare(ctx_ref[slot], ck4.at[slot], cv4.at[slot])
        dk_acc[...] = jnp.zeros_like(dk_acc)
        dv_acc[...] = jnp.zeros_like(dv_acc)
        cdk[...] = jnp.zeros_like(cdk)
        cdv[...] = jnp.zeros_like(cdv)

    boundary = GRAN - sum(info[part * (ROWS_SEQ // GRAN)] for part in range(GRAN))
    gran = step // (pl.num_programs(0) // GRAN)
    slot = (gran >= boundary).astype(jnp.int32)
    first = jnp.where(slot == 0, 0, boundary)
    last = jnp.where(slot == 0, boundary, GRAN)
    packed = q_ref[...].reshape(2 * HD, 2 * HD)
    turned = packed.T
    turned = jnp.concatenate([turned[:HD], turned[HD:]], axis=1)
    high, low = hilo(turned * (HD**-0.5 * LOG2E))
    q4 = jnp.concatenate([high, high, low, low], axis=0)
    q2 = jnp.concatenate(hilo(split_halves(packed) * HD**-0.5), axis=1)
    do_turned = do_ref[...].reshape(2 * HD, 2 * HD).T
    do_turned = jnp.concatenate([do_turned[:HD], do_turned[HD:]], axis=1)

    def pack_back(values):
        half = values.shape[1] // 2
        return jnp.concatenate([values[:, :half], values[:, half:]], axis=0).T

    def take(high, low, turned_pair):
        both = dot(turned_pair, high)
        return both[:HD] + both[HD:] + dot(turned_pair[:HD], low)

    def places(g):
        return [
            pl.ds(pl.multiple_of(way * own + g * chunk, chunk), chunk) for way in range(group)
        ]

    ctx_scores = dot(ck4[slot], q4)
    token = lax.broadcasted_iota(jnp.int32, ctx_scores.shape, 0)
    ctx_scores = jnp.where(token < CTX_TOK, ctx_scores, -1e30)

    def score_pass(g, top):
        for at in places(g):
            scores = dot(k4[at, :], q4)
            s_sc[at, :] = scores
            top = jnp.maximum(top, jnp.max(scores, axis=0, keepdims=True))
        return top

    top = lax.fori_loop(first, last, score_pass, jnp.max(ctx_scores, axis=0, keepdims=True))
    ctx_p = jnp.exp2(ctx_scores - top)

    def value_pass(g, carry):
        total, out = carry
        for at in places(g):
            p = jnp.exp2(s_sc[at, :] - top)
            s_sc[at, :] = p
            total = total + row_sum(p)
            out = out + take(*hilo(p), vt[:, at])
        return total, out

    total, out = lax.fori_loop(
        first, last, value_pass, (row_sum(ctx_p), take(*hilo(ctx_p), cvt[slot]))
    )
    inverse = 1.0 / total
    out = out * inverse
    o_ref[...] = pack_back(out).reshape(o_ref.shape)
    do_scaled = do_turned * inverse
    diagonal = row_sum(do_scaled * out)
    high, low = hilo(do_scaled)
    d4 = jnp.concatenate([high, high, low, low], axis=0)
    d2 = jnp.concatenate(hilo(split_halves(pack_back(do_scaled))), axis=1)

    def back(p, values, keys_turned):
        ds = p * (dot(values, d4) - diagonal)
        ds_high, ds_low = hilo(ds)
        p_high, p_low = hilo(p)
        dv = dot(p_high, d2) + dot(p_low, d2)
        dk = dot(ds_high, q2) + dot(ds_low, q2)
        return dk, dv, take(ds_high, ds_low, keys_turned)

    dk, dv, dq = back(ctx_p, cv4[slot], ckt[slot])
    cdk[slot] += dk
    cdv[slot] += dv

    def gradient_pass(g, dq):
        for at in places(g):
            dk, dv, part = back(s_sc[at, :], v4[at, :], kt[:, at])
            dk_acc[at, :] += dk
            dv_acc[at, :] += dv
            dq = dq + part
        return dq

    dq = lax.fori_loop(first, last, gradient_pass, dq) * HD**-0.5
    dq_ref[...] = pack_back(dq).reshape(dq_ref.shape)

    def fold(pair):
        return pair[:, :HD] + pair[:, HD:]

    @pl.when(step == pl.num_programs(0) - 1)
    def _():
        for way in range(group):
            for start in range(0, own, piece):
                at = slice(way * own + start, way * own + start + piece)
                joined = jnp.concatenate([fold(dk_acc[at, :]), fold(dv_acc[at, :])], axis=1)
                dkv_refs[way][start // portion : (start + piece) // portion] = joined.reshape(
                    piece // portion, portion, 2 * HD
                )
        for slot in range(SLOTS):
            dctx_ref[slot] = jnp.concatenate([fold(cdk[slot]), fold(cdv[slot])], axis=1)


def attention(info, traded, do, others, ctx, group):
    sources = traded.shape[0]
    half = do.shape[1]
    portion = 2 * half
    own = sources * portion
    keys = group * own
    per_step = 2 * HD // half
    steps = sources // per_step
    q_block = pl.BlockSpec((per_step, half, 2 * HD), lambda i: (i, 2, 0))
    side_block = pl.BlockSpec((per_step, half, 2 * HD), lambda i: (i, 0, 0))
    kv_shape = (sources, portion, 2 * HD)
    pair_shape = (SLOTS, CTX_PAD, 2 * HD)
    return pl.pallas_call(
        functools.partial(attention_kernel, group=group, sources=sources, portion=portion),
        grid=(steps,),
        in_specs=[pl.BlockSpec(memory_space=pltpu.SMEM), q_block, side_block]
        + [whole_block(kv_shape)] * group
        + [whole_block(pair_shape)],
        out_specs=[side_block, side_block] + [whole_block(kv_shape)] * group + [whole_block(pair_shape)],
        out_shape=[jax.ShapeDtypeStruct((sources, half, 2 * HD), F32)] * 2
        + [jax.ShapeDtypeStruct(kv_shape, F32)] * group
        + [jax.ShapeDtypeStruct(pair_shape, F32)],
        scratch_shapes=[
            pltpu.VMEM((keys, 4 * HD), BF),
            pltpu.VMEM((keys, 4 * HD), BF),
            pltpu.VMEM((2 * HD, keys), BF),
            pltpu.VMEM((2 * HD, keys), BF),
            pltpu.VMEM((SLOTS, CTX_PAD, 4 * HD), BF),
            pltpu.VMEM((SLOTS, CTX_PAD, 4 * HD), BF),
            pltpu.VMEM((SLOTS, 2 * HD, CTX_PAD), BF),
            pltpu.VMEM((SLOTS, 2 * HD, CTX_PAD), BF),
            pltpu.VMEM((keys, 4 * HD), F32),
            pltpu.VMEM((keys, 2 * HD), F32),
            pltpu.VMEM((keys, 2 * HD), F32),
            pltpu.VMEM(pair_shape, F32),
            pltpu.VMEM(pair_shape, F32),
        ],
        compiler_params=pltpu.CompilerParams(vmem_limit_bytes=VMEM_LIMIT),
        cost_estimate=cost(6e10),
        name="attention",
    )(info, traded, do, traded, *others, ctx)


def rotated(values, axis):
    size = lax.axis_size(axis)
    return [values] + [
        lax.ppermute(values, axis, [(i, (i + d) % size) for i in range(size)])
        for d in range(1, size)
    ]


def gathered(values, axis):
    size = lax.axis_size(axis)
    pieces = rotated(values, axis)[::-1]
    stacked = jnp.stack(pieces + pieces[:-1])
    return lax.dynamic_slice_in_dim(stacked, size - 1 - lax.axis_index(axis), size, 0)


def band_stats(stat, px):
    parts = rotated(stat, "heads")
    mean = sum(part[0] for part in parts) / len(parts)
    spread = sum(part[1] + px * jnp.square(part[0] - mean) for part in parts)
    return jnp.stack([mean, spread])


def band_sums(sums):
    return sum(rotated(sums, "heads"))


def turned(values):
    size = lax.axis_size("heads")
    return lax.ppermute(
        values, SEQ, [(r * size + h, h * size + r) for r in range(size) for h in range(size)]
    )


def after(values, *others):
    return lax.optimization_barrier((values, *others))[0]


def halo(edge_low, edge_high):
    size = lax.axis_size("rows") * lax.axis_size("heads")
    forward = [(i, i + 1) for i in range(size - 1)]
    backward = [(i + 1, i) for i in range(size - 1)]
    return lax.ppermute(edge_high, SEQ, forward), lax.ppermute(edge_low, SEQ, backward)


def edges(values):
    return halo(values[:WID], values[-WID:])


def trade(values):
    return lax.all_to_all(values, SEQ, split_axis=0, concat_axis=0, tiled=True)


def per_device(
    pixels,
    crop_slot,
    embedding,
    context,
    first_gain,
    first_offset,
    first_kernel,
    first_bias,
    embed_weight,
    embed_bias,
    second_gain,
    second_offset,
    second_kernel,
    second_bias,
    attend_gain,
    attend_offset,
    inner_weight,
    inner_bias,
    context_weight,
    context_bias,
    outer_weight,
    outer_bias,
    cotangent,
):
    row_count = pixels.shape[0]
    assert pixels.shape[1] == 1
    ranks = lax.axis_size("rows")
    head_ways = lax.axis_size("heads")
    halves = lax.axis_size("dp")
    ways = ranks * head_ways
    group = ways // NH
    px = row_count * WID
    dims = (px, ways, head_ways)
    rank = lax.axis_index("rows")
    head_rank = lax.axis_index("heads")
    joint = rank * head_ways + head_rank
    shard_heads = NH // head_ways
    span = shard_heads * HD
    square = ranks == head_ways and NH // ranks == shard_heads

    slots = crop_slot[:, 0]
    hier = head_ways == 4
    part_order = [head_rank ^ d if hier else d for d in range(head_ways)]
    info = jnp.concatenate(
        [slots, jnp.stack([rank, joint, lax.axis_index("dp")] + part_order).astype(jnp.int32)]
    )
    split = halves == 2 and hier

    x = pixels.reshape(px, C)
    cot = cotangent.reshape(px, C)

    def row(vector):
        return vector.reshape(1, C)

    bias_rows = jnp.stack(
        [inner_bias[0].reshape(span), jnp.zeros((span,), F32), inner_bias[1].reshape(span)]
    )
    own_inner = jnp.concatenate(
        [
            inner_weight.astype(F32).transpose(1, 0, 2, 3).reshape(3, C, span),
            jnp.pad(bias_rows[:, None], ((0, 0), (0, 7), (0, 0))),
        ],
        axis=1,
    ).reshape(3 * (C + 8), span)
    own_outer = (
        outer_weight.astype(F32)
        .reshape(span, C // span, span)
        .transpose(1, 0, 2)
        .reshape(C, span)
    )
    outer_w = lax.all_gather(own_outer, "heads", axis=0, tiled=False)

    mean = jnp.mean(x, axis=0)
    x_stat = jnp.stack([mean, jnp.sum(jnp.square(x - mean), axis=0)])
    band_stat = band_stats(x_stat, px)
    pays0 = rotated(band_stat, "rows")
    x_halo = edges(x)
    inner_w = lax.all_gather(own_inner, "heads", axis=0, tiled=False)
    first_k = first_kernel.reshape(3, 3 * C, C)
    second_k = second_kernel.reshape(3, 3 * C, C)
    conv1, act1, stat1, x_vec = conv_forward(
        info, x, x_halo, pays0, row(first_gain), row(first_offset), first_k, row(first_bias), None, dims
    )

    ctx_flat = context[0].reshape(SLOTS * CTX_TOK, context.shape[-1])
    ctx_pair = jnp.dot(
        after(ctx_flat, conv1),
        context_weight.reshape(context.shape[-1], 2 * span),
        preferred_element_type=F32,
    ).reshape(SLOTS * CTX_TOK, 2, shard_heads, HD)
    ctx_pair = ctx_pair + jnp.stack([jnp.zeros_like(context_bias), context_bias])
    ctx_pair = ctx_pair.transpose(2, 0, 1, 3).reshape(shard_heads, SLOTS * CTX_TOK, 2 * HD)
    own_head = joint // group
    if square:
        ctx_all, at = turned(ctx_pair), own_head % shard_heads
    else:
        ctx_all, at = lax.all_gather(ctx_pair, "heads", axis=0, tiled=True), own_head
    ctx_own = lax.dynamic_index_in_dim(ctx_all, at, 0, keepdims=False)
    ctx_own = jnp.pad(
        ctx_own.reshape(SLOTS, CTX_TOK, 2 * HD), ((0, 0), (0, CTX_PAD - CTX_TOK), (0, 0))
    )

    embed_act = jax.nn.silu(embedding[0])
    modulation = jnp.dot(after(embed_act, conv1), embed_weight.astype(F32), precision=HIGH) + embed_bias
    own_slot = slots[joint * row_count]
    own_mod = lax.dynamic_index_in_dim(modulation, own_slot, 0, keepdims=True)
    lift = 1.0 + own_mod[:, :C]
    second_scale = row(second_gain) * lift
    second_shift = row(second_offset) * lift + own_mod[:, C:]
    def swapped(values):
        return lax.ppermute(values, "dp", [(0, 1), (1, 0)])

    conv1_halo = edges(conv1)
    pays1 = rotated(band_stats(stat1, px), "rows")
    do_blocks, cot_sum = attended_gradient(cot, outer_w, ways, group)
    pays1[0] = after(pays1[0], do_blocks)
    residual, act2, stat2, vec1 = conv_forward(
        info, conv1, conv1_halo, pays1, second_scale, second_shift, second_k, row(second_bias), x, dims
    )
    do_own = trade(do_blocks)
    acts = [act1, act2]
    band_stat = band_stats(stat2, px)
    band_stat = after(band_stat, ctx_own)
    if split:
        acts += [swapped(act) for act in acts]
        band_stat = after(band_stat, acts[2])

    pays2 = rotated(band_stat, "rows")
    pays2[0] = after(pays2[0], do_own)
    blocks, vec2 = project(
        info, residual, pays2, row(attend_gain), row(attend_offset), inner_w, dims, group
    )
    traded = trade(blocks)
    res_halo = edges(after(residual, blocks))
    cot_halo = edges(after(cot, blocks))
    act_seqs = rotated(after(embed_act, blocks), "dp")
    acts = jnp.stack(acts, axis=1)
    traded, acts, res_halo, cot_halo, act_seqs = lax.optimization_barrier(
        (traded, acts, res_halo, cot_halo, act_seqs)
    )
    ctx_seqs = rotated(after(ctx_flat.astype(F32), traded), "dp")
    portion = px // group
    own_kv = traded[:, :portion]

    def mates(d):
        return [(i, i // group * group + (i % group + d) % group) for i in range(ways)]

    others = [lax.ppermute(own_kv, SEQ, mates(group - d)) for d in range(1, group)]
    acts = lax.all_to_all(after(acts, *others), "heads", split_axis=0, concat_axis=0, tiled=True)
    results = attention(info, traded, do_own, others, ctx_own, group)
    att_own, dq_own = results[:2]
    dkv_parts = list(results[2 : 2 + group])
    ctx_grad = results[2 + group]
    dkv = dkv_parts[0]
    for d in range(1, group):
        dkv = dkv + lax.ppermute(dkv_parts[d], SEQ, mates(d))
    dkv = after(dkv, acts, tuple(ctx_seqs))
    grads = trade(jnp.concatenate([dkv, dq_own], axis=1))

    ctx_grad = after(ctx_grad, dkv)[:, :CTX_TOK].reshape(SLOTS * CTX_TOK, 2 * HD)
    if square:
        ctx_grads = jnp.stack(rotated(ctx_grad, "heads"))
        ctx_order = (head_rank - jnp.arange(head_ways)) % head_ways // group
        ctx_row = jnp.stack(
            [
                jnp.sum(jnp.where((ctx_order == head)[:, None, None], ctx_grads, 0.0), axis=0)
                for head in range(shard_heads)
            ]
        )
        ctx_mine = turned(after(ctx_row, grads))
    else:
        ctx_grads = lax.all_gather(ctx_grad, SEQ, axis=0, tiled=False)
        ctx_grads = jnp.sum(ctx_grads.reshape(NH, group, SLOTS * CTX_TOK, 2 * HD), axis=1)
        ctx_mine = lax.dynamic_slice_in_dim(ctx_grads, head_rank * shard_heads, shard_heads, 0)

    normed_grad, sums2, inner_part = project_back(
        grads, residual, vec2, row(attend_gain), row(attend_offset), inner_w, cot_sum, dims, group
    )

    def far_of(grad):
        if not split:
            return grad
        return [grad[0], swapped(grad[1]), flip(grad[0], 2)]

    def band_of(hops, *waiting):
        if not split:
            return [lax.all_gather(hops[0], "heads", axis=0, tiled=True)]
        mine, other, far = (after(hop, *waiting) if waiting else hop for hop in hops)
        other_far = flip(other, 2)
        return [
            mine,
            flip(mine, 1),
            far,
            flip(far, 1),
            other,
            flip(other, 1),
            other_far,
            flip(other_far, 1),
        ]

    def flip(values, bit):
        return lax.ppermute(values, "heads", [(i, i ^ bit) for i in range(head_ways)])

    ng_halo = edges(normed_grad)
    band_sum = band_sums(sums2)
    pays3 = rotated(band_sum, "rows")
    attended = trade(after(att_own, grads, pays3[-1]))

    def shard_sum(parts):
        return lax.psum_scatter(parts, "heads", scatter_dimension=0, tiled=False)

    inner_sum = shard_sum(inner_part)
    *residual_grad, hidden_grad, sums1 = conv_backward(
        info,
        normed_grad,
        ng_halo,
        residual,
        res_halo,
        vec2,
        row(attend_gain),
        pays3,
        [cot, *cot_halo],
        second_k,
        (conv1, vec1, second_scale, second_shift),
        dims,
        split,
    )
    hg_halo = edges(hidden_grad)
    band_sum = after(band_sums(sums1), attended)
    pays4 = rotated(band_sum, "rows")
    second_hops = far_of([after(grad, band_sum) for grad in residual_grad])
    output, outer_part = output_step(
        after(attended, band_sum, inner_sum), residual, cot, outer_w, row(outer_bias), dims, group
    )
    inner_sum = lax.psum_scatter(inner_sum, "rows", scatter_dimension=0, tiled=True)
    outer_part, pays4[0] = lax.optimization_barrier((outer_part, pays4[0]))
    outer_sum = lax.psum_scatter(
        shard_sum(outer_part), "rows", scatter_dimension=0, tiled=True
    )
    *conv1_grad, pre_grad, sums0 = conv_backward(
        info,
        hidden_grad,
        hg_halo,
        conv1,
        conv1_halo,
        vec1,
        second_scale,
        pays4,
        None,
        first_k,
        (x, x_vec, row(first_gain), row(first_offset)),
        dims,
        split,
    )
    second_band = band_of(second_hops, pre_grad)
    first_hops = far_of(conv1_grad)
    first_band = band_of(first_hops)
    if split:
        second_band[0] = after(second_band[0], tuple(first_hops), first_band[1])

    def kernel_sum(at, band, *waits):
        seqs = [acts, acts] if split else [acts]
        part = kernel_grad(info, seqs, (at, at + 2)[: len(seqs)], band, ranks)
        if not split:
            part = lax.psum_scatter(part, "dp", scatter_dimension=3, tiled=True)
        parts = lax.all_to_all(part, "rows", split_axis=0, concat_axis=0)
        return jnp.sum(after(parts, *waits), axis=0).reshape(3, 3, C // ways, C // halves), part

    second_kernel_grad, second_part = kernel_sum(1, second_band)
    first_kernel_grad, first_part = kernel_sum(0, first_band)
    inner_sum = gathered(sum(rotated(after(inner_sum, second_part), "dp")), "rows")
    outer_sum = gathered(sum(rotated(after(outer_sum, first_part), "dp")), "rows")
    pays5 = rotated(band_sums(after(sums0, first_part)), "rows")
    pixels_grad = final_norm(
        info, pre_grad, x, x_vec, row(first_gain), residual_grad, pays5, dims
    )
    inner_sum = inner_sum.reshape(3, GRAD_ROWS, span)
    inner_weight_grad = inner_sum[:, :C].reshape(3, C, shard_heads, HD).transpose(1, 0, 2, 3)
    bias_sum = inner_sum[:, C].reshape(3, shard_heads, HD)
    inner_bias_grad = jnp.stack([bias_sum[0], bias_sum[2]])
    outer_weight_grad = (
        outer_sum
        .reshape(C // span, span, span)
        .transpose(1, 0, 2)
        .reshape(shard_heads, HD, C)
    )

    ctx_mine = (
        ctx_mine.reshape(shard_heads, SLOTS * CTX_TOK, 2, HD)
        .transpose(1, 2, 0, 3)
        .reshape(SLOTS * CTX_TOK, 2 * span)
    )
    mine_seqs = rotated(after(ctx_mine, first_part), "dp")
    context_weight_grad = jnp.dot(
        after(jnp.concatenate(ctx_seqs, axis=0).T, first_part), jnp.concatenate(mine_seqs, axis=0), precision=HIGH
    ).reshape(context.shape[-1], 2, shard_heads, HD)
    context_bias_grad = jnp.sum(sum(mine_seqs), axis=0).reshape(2, shard_heads, HD)[1]

    attend_sums = sum(after(tuple(pays3), first_part))
    band_slots = slots[:: row_count * head_ways]
    band_slots = jnp.stack([band_slots[(rank - d) % ranks] for d in range(ranks)])
    slot_rows = (band_slots[None, :] == jnp.arange(SLOTS)[:, None]).astype(F32)
    late4 = after(tuple(pays4), first_part)
    by_slot = sum(slot_rows[:, d, None, None] * late4[d] for d in range(ranks))
    shift_grad, hat_grad = by_slot[:, 0], by_slot[:, 1]
    mod_lift = 1.0 + modulation[:, :C]
    scale_grad = hat_grad * second_gain + shift_grad * second_offset
    pack = jnp.concatenate(
        [
            attend_sums,
            jnp.stack(
                [
                    jnp.sum(hat_grad * mod_lift, axis=0),
                    jnp.sum(shift_grad * mod_lift, axis=0),
                    jnp.sum(by_slot[:, 2], axis=0),
                ]
            ),
            scale_grad,
            shift_grad,
        ],
        axis=0,
    )
    packs = rotated(pack, "dp")
    vectors = sum(packs)
    mod_grads = jnp.concatenate(
        [jnp.concatenate([p[6 : 6 + SLOTS], p[6 + SLOTS :]], axis=1) for p in packs], axis=0
    )
    embed_bias_grad = jnp.sum(mod_grads, axis=0)
    embed_rows = embed_weight.shape[0] // ways
    embed_cols = 2 * C // halves
    embed_weight_grad = jnp.einsum(
        "ke,kc->ec",
        lax.dynamic_slice_in_dim(jnp.concatenate(act_seqs, axis=0), joint * embed_rows, embed_rows, 1),
        lax.dynamic_slice_in_dim(mod_grads, lax.axis_index("dp") * embed_cols, embed_cols, 1),
        precision=HIGH,
    )
    first_sums = sum(rotated(sum(pays5), "dp"))

    shape = pixels.shape
    return (
        output.reshape(shape),
        pixels_grad.reshape(shape),
        first_sums[1],
        first_sums[0],
        first_kernel_grad,
        first_sums[2],
        embed_weight_grad,
        embed_bias_grad,
        vectors[3],
        vectors[4],
        second_kernel_grad,
        vectors[5],
        vectors[1],
        vectors[0],
        inner_weight_grad,
        inner_bias_grad,
        context_weight_grad,
        context_bias_grad,
        outer_weight_grad,
        vectors[2],
    )


def solution(mesh):
    band = P(SEQ, "dp", None, None)
    kernel_out = P(None, None, SEQ, "dp")
    return jax.shard_map(
        per_device,
        mesh=mesh,
        in_specs=(
            band,
            P(None, "dp"),
            P("dp", None, None),
            P("dp", None, None, None),
            P(),
            P(),
            P(),
            P(),
            P(),
            P(),
            P(),
            P(),
            P(),
            P(),
            P(),
            P(),
            P(None, None, "heads", None),
            P(None, "heads", None),
            P(None, None, "heads", None),
            P("heads", None),
            P("heads", None, None),
            P(),
            band,
        ),
        out_specs=(
            band,
            band,
            P(),
            P(),
            kernel_out,
            P(),
            P(SEQ, "dp"),
            P(),
            P(),
            P(),
            kernel_out,
            P(),
            P(),
            P(),
            P(None, None, "heads", None),
            P(None, "heads", None),
            P(None, None, "heads", None),
            P("heads", None),
            P("heads", None, None),
            P(),
        ),
        check_vma=False,
    )
```

```python
import functools

import jax
import jax.numpy as jnp
from jax import lax
from jax.experimental import pallas as pl
from jax.experimental.pallas import tpu as pltpu
from jax.sharding import PartitionSpec as P

C = 512
NH = 8
HD = 64
GROUPS = 32
GROUP_C = C // GROUPS
CTX_TOK = 81
CTX_PAD = 128
GRAD_ROWS = 576
QUERIES = 512
WID = 64
SLOTS = 2
ROWS_SEQ = 64
GRAN = 4
EPS = 1e-05
LOG2E = 1.4426950408889634
F32 = jnp.float32
BF = jnp.bfloat16
SEQ = ("rows", "heads")
HIGH = lax.Precision.HIGHEST
VMEM_LIMIT = 56 << 20


def hilo(values):
    high = values.astype(BF)
    return high, (values - high.astype(F32)).astype(BF)


def dot(left, right):
    return jnp.dot(left, right, preferred_element_type=F32)


def dot_nt(left, right):
    return lax.dot_general(left, right, (((1,), (1,)), ((), ())), preferred_element_type=F32)


def dot_tn(left, right):
    return lax.dot_general(left, right, (((0,), (0,)), ((), ())), preferred_element_type=F32)


def group_mean(values):
    lane = lax.broadcasted_iota(jnp.int32, values.shape, 1)
    for step in (1, 2, 4, 8):
        up = pltpu.roll(values, step, 1)
        down = pltpu.roll(values, C - step, 1)
        values = values + jnp.where((lane & step) != 0, up, down)
    return values * (1.0 / GROUP_C)


def wide(row):
    return jnp.broadcast_to(row, (8, C))


def scalars(info, ranks, rows):
    rank, joint = info[ROWS_SEQ], info[ROWS_SEQ + 1]
    band = ROWS_SEQ // ranks
    own = info[joint * rows]
    found = []
    for step in range(ranks):
        other = rank - step
        other = jnp.where(other < 0, other + ranks, other)
        found.append(info[other * band] == own)
    first, last = joint * rows, joint * rows + rows
    found.append((first > 0) & (info[jnp.maximum(first - 1, 0)] == own))
    found.append((last < ROWS_SEQ) & (info[jnp.minimum(last, ROWS_SEQ - 1)] == own))
    return [jnp.where(item, 1.0, 0.0).astype(F32) for item in found]


def norm_stats(pays, scal, px):
    count = sum(scal[i] for i in range(len(pays)))
    mean = sum(scal[i] * wide(pay[0:1, :]) for i, pay in enumerate(pays)) / count
    spread = sum(
        scal[i] * (wide(pay[1:2, :]) + px * jnp.square(wide(pay[0:1, :]) - mean))
        for i, pay in enumerate(pays)
    )
    total = count * px
    center = group_mean(mean)
    variance = group_mean(spread + total * jnp.square(mean - center)) / total
    return center[0:1], (1.0 / jnp.sqrt(variance + EPS))[0:1]


def back_means(pays, scal, gain, px):
    count = sum(scal[i] for i in range(len(pays))) * px
    first = sum(scal[i] * wide(pay[0:1, :]) for i, pay in enumerate(pays))
    second = sum(scal[i] * wide(pay[1:2, :]) for i, pay in enumerate(pays))
    return (group_mean(first * gain) / count)[0:1], (group_mean(second * gain) / count)[0:1]


def local_stats(values):
    mean = jnp.mean(values, axis=0, keepdims=True)
    return mean, jnp.sum(jnp.square(values - mean), axis=0, keepdims=True)


def row_sum(values):
    return jnp.sum(values, axis=0, keepdims=True)


def shifted(values, tap):
    if tap == 1:
        return values
    column = lax.broadcasted_iota(jnp.int32, values.shape, 0) % WID
    rows = values.shape[0]
    if tap == 0:
        return jnp.where(column == 0, 0.0, pltpu.roll(values, 1, 0))
    return jnp.where(column == WID - 1, 0.0, pltpu.roll(values, rows - 1, 0))


def fill_taps(values, high_ref, low_ref, row, width):
    for tap in range(3):
        high, low = hilo(shifted(values, tap))
        high_ref[row : row + values.shape[0], tap * width : (tap + 1) * width] = high
        low_ref[row : row + values.shape[0], tap * width : (tap + 1) * width] = low


def conv_forward_kernel(*refs, px, ways, ranks, has_skip):
    info, x_ref, top_ref, low_ref = refs[:4]
    pays = refs[4 : 4 + ranks]
    scale_ref, shift_ref, w_ref, bias_ref = refs[4 + ranks : 8 + ranks]
    rest = refs[8 + ranks :]
    band_px = float(px * (ways // ranks))
    if has_skip:
        skip_ref, rest = rest[0], rest[1:]
    out_ref, act_ref, stat_ref, vec_ref, high_sc, low_sc, acc = rest
    tap = pl.program_id(0)
    block = C // ways

    @pl.when(tap == 0)
    def _():
        scal = scalars(info, ranks, px // WID)
        mean, inverse = norm_stats(pays, scal, band_px)
        vec_ref[...] = jnp.concatenate([mean, inverse], axis=0)
        scale = scale_ref[...]
        shift = shift_ref[...]
        heads_count = act_ref.shape[0]

        def activate(values, weight, row):
            pre = (values - mean) * inverse * scale + shift
            act = pre / (1.0 + jnp.exp(-pre))
            if weight is not None:
                act = act * weight
            size = values.shape[0]
            fill_taps(act, high_sc, low_sc, row, C)
            for head in range(heads_count):
                act_ref[head, row : row + size, :] = jnp.concatenate(
                    [
                        act[:, (r * heads_count + head) * block : (r * heads_count + head + 1) * block]
                        for r in range(ways // heads_count)
                    ],
                    axis=1,
                )

        activate(top_ref[...], scal[ranks], 0)
        for row in range(px // WID):
            activate(x_ref[row * WID : (row + 1) * WID, :], None, (row + 1) * WID)
        activate(low_ref[...], scal[ranks + 1], px + WID)

    base = pl.multiple_of(tap * WID, WID)
    part = dot(
        jnp.concatenate([high_sc[pl.ds(base, px), :], low_sc[pl.ds(base, px), :]], axis=0), w_ref[0]
    )
    part = part[:px] + part[px:]

    @pl.when(tap == 0)
    def _():
        acc[...] = part

    @pl.when(tap == 1)
    def _():
        acc[...] += part

    @pl.when(tap == 2)
    def _():
        out = acc[...] + part + bias_ref[...]
        if has_skip:
            out = out + skip_ref[...]
        out_ref[...] = out
        stat_ref[...] = jnp.concatenate(local_stats(out), axis=0)


def cost(flops):
    return pl.CostEstimate(flops=int(flops), transcendentals=0, bytes_accessed=0)


def whole_block(shape):
    return pl.BlockSpec(shape, lambda *_: (0,) * len(shape), pipeline_mode=pl.Buffered(1))


def conv_forward(info, x, halo, pays, scale, shift, kernel, bias, skip, dims):
    px, ways, head_ways = dims
    ranks = len(pays)
    quarter = C // head_ways
    operands = [info, x, halo[0], halo[1], *pays, scale, shift, kernel, bias]
    specs = (
        [pl.BlockSpec(memory_space=pltpu.SMEM), whole_block((px, C))]
        + [whole_block((WID, C))] * 2
        + [whole_block(pays[0].shape)] * ranks
        + [whole_block((1, C))] * 2
        + [pl.BlockSpec((1, 3 * C, C), lambda i: (i, 0, 0)), whole_block((1, C))]
    )
    if skip is not None:
        operands.append(skip)
        specs.append(whole_block((px, C)))
    ext = px + 2 * WID
    return pl.pallas_call(
        functools.partial(
            conv_forward_kernel,
            px=px,
            ways=ways,
            ranks=ranks,
            has_skip=skip is not None,
        ),
        grid=(3,),
        in_specs=specs,
        out_specs=[
            whole_block((px, C)),
            whole_block((head_ways, ext, quarter)),
            whole_block((2, C)),
            whole_block((2, C)),
        ],
        out_shape=[
            jax.ShapeDtypeStruct((px, C), F32),
            jax.ShapeDtypeStruct((head_ways, ext, quarter), F32),
            jax.ShapeDtypeStruct((2, C), F32),
            jax.ShapeDtypeStruct((2, C), F32),
        ],
        scratch_shapes=[
            pltpu.VMEM((ext, 3 * C), BF),
            pltpu.VMEM((ext, 3 * C), BF),
            pltpu.VMEM((px, C), F32),
        ],
        compiler_params=pltpu.CompilerParams(vmem_limit_bytes=VMEM_LIMIT),
        cost_estimate=cost(7e9),
        name="conv_forward",
    )(*operands)


def halves_of(info, values, split):
    if not split:
        return [values]
    even = info[ROWS_SEQ + 2] == 0
    left, right = values[:, : C // 2], values[:, C // 2 :]
    return [jnp.where(even, left, right), jnp.where(even, right, left)]


def conv_backward_kernel(*refs, px, ways, ranks, has_add, split):
    info, yg_ref, yg_top, yg_low, x_ref, x_top, x_low, vec_ref, gain_ref = refs[:9]
    pays = refs[9 : 9 + ranks]
    rest = refs[9 + ranks :]
    band_px = float(px * (ways // ranks))
    if has_add:
        adds, rest = rest[:3], rest[3:]
    w_ref, in_ref, in_vec, in_scale, in_shift = rest[:5]
    g_refs = rest[5 : 7 if split else 6]
    h_ref, sum_ref, high_sc, low_sc, acc, bias_sum = rest[7 if split else 6 :]
    tap = pl.program_id(0)

    @pl.when(tap == 0)
    def _():
        scal = scalars(info, ranks, px // WID)
        gain = gain_ref[...]
        mean, inverse = vec_ref[0:1, :], vec_ref[1:2, :]
        first, second = back_means(pays, scal, gain, band_px)

        def gradient(yg, x, extra, weight, row):
            grad = (yg * gain - first - (x - mean) * inverse * second) * inverse
            if extra is not None:
                grad = grad + extra
            if weight is not None:
                grad = grad * weight
            fill_taps(grad, high_sc, low_sc, row, C)
            return grad

        gradient(yg_top[...], x_top[...], adds[1][...] if has_add else None, scal[ranks], 0)
        total = jnp.zeros((1, C), F32)
        for row in range(px // WID):
            at = slice(row * WID, (row + 1) * WID)
            grad = gradient(
                yg_ref[at, :],
                x_ref[at, :],
                adds[0][at, :] if has_add else None,
                None,
                (row + 1) * WID,
            )
            for ref, piece in zip(g_refs, halves_of(info, grad, split)):
                ref[at, :] = piece
            total = total + row_sum(grad)
        gradient(
            yg_low[...], x_low[...], adds[2][...] if has_add else None, scal[ranks + 1], px + WID
        )
        bias_sum[...] = total
        acc[...] = jnp.zeros_like(acc)

    base = pl.multiple_of(tap * WID, WID)
    part = acc[...]
    for col in range(3):
        weight = w_ref[0, (2 - col) * C : (3 - col) * C, :]
        at = (pl.ds(base, px), slice(col * C, (col + 1) * C))
        both = dot_nt(jnp.concatenate([high_sc[at], low_sc[at]], axis=0), weight)
        part = part + both[:px] + both[px:]
    acc[...] = part

    @pl.when(tap == 2)
    def _():
        hat = (in_ref[...] - in_vec[0:1, :]) * in_vec[1:2, :]
        pre = hat * in_scale[...] + in_shift[...]
        sigmoid = 1.0 / (1.0 + jnp.exp(-pre))
        h = acc[...] * (sigmoid * (1.0 + pre * (1.0 - sigmoid)))
        h_ref[...] = h
        sum_ref[...] = jnp.concatenate([row_sum(h), row_sum(h * hat), bias_sum[...]], axis=0)


def conv_backward(info, yg, yg_halo, x, x_halo, vec, gain, pays, adds, kernel, inner, dims, split):
    px, ways, _ = dims
    ranks = len(pays)
    in_x, in_vec, in_scale, in_shift = inner
    rows3 = [whole_block((px, C)), whole_block((WID, C)), whole_block((WID, C))]
    operands = [info, yg, *yg_halo, x, *x_halo, vec, gain, *pays]
    specs = (
        [pl.BlockSpec(memory_space=pltpu.SMEM)]
        + rows3
        + rows3
        + [whole_block((2, C)), whole_block((1, C))]
        + [whole_block(pays[0].shape)] * ranks
    )
    if adds is not None:
        operands += adds
        specs += rows3
    operands += [kernel, in_x, in_vec, in_scale, in_shift]
    specs += [
        pl.BlockSpec((1, 3 * C, C), lambda i: (2 - i, 0, 0)),
        whole_block((px, C)),
        whole_block((2, C)),
        whole_block((1, C)),
        whole_block((1, C)),
    ]
    ext = px + 2 * WID
    shapes = [(px, C // 2)] * 2 if split else [(px, C)]
    shapes += [(px, C), (3, C)]
    return pl.pallas_call(
        functools.partial(
            conv_backward_kernel,
            px=px,
            ways=ways,
            ranks=ranks,
            has_add=adds is not None,
            split=split,
        ),
        grid=(3,),
        in_specs=specs,
        out_specs=[whole_block(shape) for shape in shapes],
        out_shape=[jax.ShapeDtypeStruct(shape, F32) for shape in shapes],
        scratch_shapes=[
            pltpu.VMEM((ext, 3 * C), BF),
            pltpu.VMEM((ext, 3 * C), BF),
            pltpu.VMEM((px, C), F32),
            pltpu.VMEM((1, C), F32),
        ],
        compiler_params=pltpu.CompilerParams(vmem_limit_bytes=VMEM_LIMIT),
        cost_estimate=cost(7e9),
        name="conv_backward",
    )(*operands)


def kernel_grad_kernel(info, *refs, ranks, seqs, grad_count):
    acts, grads = refs[:seqs], refs[seqs : seqs + grad_count]
    out_ref, taps, g_high, g_low = refs[seqs + grad_count :]
    tap = pl.program_id(0)
    parts, _, ext, quarter = acts[0].shape
    px = ext - 2 * WID
    block = quarter // ranks

    @pl.when(tap == 0)
    def _():
        for seq in range(seqs):
            for part in range(parts):
                at = seq * parts + part
                act = acts[seq][info[ROWS_SEQ + 3 + part], 0]
                for col in range(3):
                    high, low = hilo(shifted(act, col))
                    taps[at, :, col * quarter : (col + 1) * quarter] = high
                    taps[at, :, (3 + col) * quarter : (4 + col) * quarter] = low
                rows = slice(at * px, (at + 1) * px)
                high, low = hilo(grads[at][...] if grad_count > 1 else grads[0][rows, :])
                g_high[rows, :] = high
                g_low[rows, :] = low

    base = pl.multiple_of(tap * WID, WID)
    left = jnp.concatenate([taps[at, pl.ds(base, px), :] for at in range(seqs * parts)], axis=0)
    both = dot_tn(left, g_high[...])
    rest = dot_tn(left[:, : 3 * quarter], g_low[...])
    total = both[: 3 * quarter] + both[3 * quarter :] + rest
    for rank in range(ranks):
        for col in range(3):
            start = col * quarter + rank * block
            out_ref[rank, 0, col * block : (col + 1) * block, :] = total[start : start + block]


def kernel_grad(info, acts, which, grads, ranks):
    parts, _, ext, quarter = acts[0].shape
    px = ext - 2 * WID
    cols = grads[0].shape[1]
    block = 3 * quarter // ranks
    seqs = len(acts)
    return pl.pallas_call(
        functools.partial(kernel_grad_kernel, ranks=ranks, seqs=seqs, grad_count=len(grads)),
        grid=(3,),
        in_specs=[pl.BlockSpec(memory_space=pltpu.SMEM)]
        + [
            pl.BlockSpec(
                (parts, 1, ext, quarter),
                lambda i, at=at: (0, at, 0, 0),
                pipeline_mode=pl.Buffered(1),
            )
            for at in which
        ]
        + [whole_block(grad.shape) for grad in grads],
        out_specs=pl.BlockSpec((ranks, 1, block, cols), lambda i: (0, i, 0, 0)),
        out_shape=jax.ShapeDtypeStruct((ranks, 3, block, cols), F32),
        scratch_shapes=[
            pltpu.VMEM((seqs * parts, ext, 6 * quarter), BF),
            pltpu.VMEM((seqs * parts * px, cols), BF),
            pltpu.VMEM((seqs * parts * px, cols), BF),
        ],
        compiler_params=pltpu.CompilerParams(vmem_limit_bytes=VMEM_LIMIT),
        cost_estimate=cost(6e9),
        name="kernel_grad",
    )(info, *acts, *grads)


def final_kernel(info, yg_ref, x_ref, vec_ref, gain_ref, *refs, band_px, count):
    adds, pays, out_ref = refs[:count], refs[count:-1], refs[-1]
    add = adds[0][...]
    if count == 2:
        even = info[ROWS_SEQ + 2] == 0
        other = adds[1][...]
        add = jnp.concatenate([jnp.where(even, add, other), jnp.where(even, other, add)], axis=1)
    scal = scalars(info, len(pays), x_ref.shape[0] // WID)
    gain = gain_ref[...]
    mean, inverse = vec_ref[0:1, :], vec_ref[1:2, :]
    first, second = back_means(pays, scal, gain, band_px)
    hat = (x_ref[...] - mean) * inverse
    out_ref[...] = add + (yg_ref[...] * gain - first - hat * second) * inverse


def final_norm(info, yg, x, vec, gain, adds, pays, dims):
    px, ways, _ = dims
    return pl.pallas_call(
        functools.partial(
            final_kernel, band_px=float(px * (ways // len(pays))), count=len(adds)
        ),
        in_specs=[pl.BlockSpec(memory_space=pltpu.SMEM)]
        + [pl.BlockSpec(memory_space=pltpu.VMEM)] * (4 + len(adds) + len(pays)),
        out_specs=pl.BlockSpec(memory_space=pltpu.VMEM),
        out_shape=jax.ShapeDtypeStruct(x.shape, F32),
        compiler_params=pltpu.CompilerParams(vmem_limit_bytes=VMEM_LIMIT),
        cost_estimate=cost(2e9),
        name="final_norm",
    )(info, yg, x, vec, gain, *adds, *pays)


def split_halves(packed):
    return jnp.concatenate([packed[:, :HD], packed[:, HD:]], axis=0)


def join_halves(values):
    half = values.shape[0] // 2
    return jnp.concatenate([values[:half], values[half:]], axis=1)


def inner_weight_of(w_ref, shard, span):
    rows = C + 8
    weight = jnp.concatenate(
        [w_ref[shard, part * rows : part * rows + C, :].astype(BF) for part in range(3)], axis=1
    )
    bias = jnp.concatenate(
        [w_ref[shard, part * rows + C : part * rows + C + 1, :] for part in range(3)], axis=1
    )
    return weight, bias


def outer_weight_of(w_ref, span):
    return jnp.concatenate(
        [
            jnp.concatenate(
                [
                    w_ref[shard, part * span : (part + 1) * span, :].astype(BF)
                    for part in range(C // span)
                ],
                axis=1,
            )
            for shard in range(w_ref.shape[0])
        ],
        axis=0,
    )


def project_kernel(info, x_ref, scale_ref, shift_ref, w_ref, *refs, group, shard_heads, band_px):
    pays, (out_ref, vec_ref) = refs[:-2], refs[-2:]
    px = x_ref.shape[0]
    scal = scalars(info, len(pays), px // WID)
    mean, inverse = norm_stats(pays, scal, band_px)
    vec_ref[...] = jnp.concatenate([mean, inverse], axis=0)
    high, low = hilo((x_ref[...] - mean) * inverse * scale_ref[...] + shift_ref[...])
    both = jnp.concatenate([high, low], axis=0)
    portion = px // group
    span = shard_heads * HD
    for shard in range(w_ref.shape[0]):
        weight, bias = inner_weight_of(w_ref, shard, span)
        inner = dot(both, weight)
        inner = inner[:px] + inner[px:] + bias
        for head in range(shard_heads):
            at = head * HD
            query = inner[:, at : at + HD]
            pair = jnp.concatenate(
                [inner[:, span + at : span + at + HD], inner[:, 2 * span + at : 2 * span + at + HD]],
                axis=1,
            )
            for part in range(group):
                slot = (shard * shard_heads + head) * group + part
                rows = slice(part * portion, (part + 1) * portion)
                out_ref[slot, :portion, :] = pair[rows]
                out_ref[slot, portion:, :] = join_halves(query[rows])


def project(info, x, pays, scale, shift, weights, dims, group):
    px, ways, _ = dims
    portion = px // group
    return pl.pallas_call(
        functools.partial(
            project_kernel,
            group=group,
            shard_heads=NH // weights.shape[0],
            band_px=float(px * (ways // len(pays))),
        ),
        in_specs=[pl.BlockSpec(memory_space=pltpu.SMEM)]
        + [pl.BlockSpec(memory_space=pltpu.VMEM)] * (4 + len(pays)),
        out_specs=[pl.BlockSpec(memory_space=pltpu.VMEM)] * 2,
        out_shape=[
            jax.ShapeDtypeStruct((ways, portion + portion // 2, 2 * HD), F32),
            jax.ShapeDtypeStruct((2, C), F32),
        ],
        compiler_params=pltpu.CompilerParams(vmem_limit_bytes=VMEM_LIMIT),
        cost_estimate=cost(5e9),
        name="project",
    )(info, x, scale, shift, weights, *pays)


def project_back_kernel(
    grad_ref, x_ref, vec_ref, scale_ref, shift_ref, w_ref, cot_sum, ng_ref, sum_ref, wg_ref, *, group, shard_heads
):
    px = x_ref.shape[0]
    hat = (x_ref[...] - vec_ref[0:1, :]) * vec_ref[1:2, :]
    normed_high, normed_low = hilo(hat * scale_ref[...] + shift_ref[...])
    portion = px // group
    span = shard_heads * HD
    grad = jnp.zeros((px, C), F32)
    for shard in range(w_ref.shape[0]):
        columns = [[], [], []]
        for head in range(shard_heads):
            slots = [(shard * shard_heads + head) * group + part for part in range(group)]
            pair = jnp.concatenate([grad_ref[slot, :portion, :] for slot in slots], axis=0)
            query = jnp.concatenate(
                [split_halves(grad_ref[slot, portion:, :]) for slot in slots], axis=0
            )
            columns[0].append(query)
            columns[1].append(pair[:, :HD])
            columns[2].append(pair[:, HD:])
        inner = jnp.concatenate(columns[0] + columns[1] + columns[2], axis=1)
        high, low = hilo(inner)
        weight, _ = inner_weight_of(w_ref, shard, span)
        part = dot_nt(jnp.concatenate([high, low], axis=0), weight)
        grad = grad + part[:px] + part[px:]
        weight_grad = (
            dot_tn(normed_high, high) + dot_tn(normed_high, low) + dot_tn(normed_low, high)
        )
        bias_grad = jnp.broadcast_to(row_sum(inner), (GRAD_ROWS - C, inner.shape[1]))
        tall = jnp.concatenate([weight_grad, bias_grad], axis=0)
        wg_ref[shard] = jnp.concatenate(
            [tall[:, part * span : (part + 1) * span] for part in range(3)], axis=0
        )
    ng_ref[...] = grad
    sum_ref[...] = jnp.concatenate([row_sum(grad), row_sum(grad * hat), cot_sum[...]], axis=0)


def project_back(grad, x, vec, scale, shift, weights, cot_sum, dims, group):
    px, _, head_ways = dims
    shape = (head_ways, 3 * GRAD_ROWS, C // head_ways)
    return pl.pallas_call(
        functools.partial(project_back_kernel, group=group, shard_heads=NH // head_ways),
        in_specs=[pl.BlockSpec(memory_space=pltpu.VMEM)] * 7,
        out_specs=[pl.BlockSpec(memory_space=pltpu.VMEM)] * 3,
        out_shape=[
            jax.ShapeDtypeStruct((px, C), F32),
            jax.ShapeDtypeStruct((3, C), F32),
            jax.ShapeDtypeStruct(shape, F32),
        ],
        compiler_params=pltpu.CompilerParams(vmem_limit_bytes=VMEM_LIMIT),
        cost_estimate=cost(7e9),
        name="project_back",
    )(grad, x, vec, scale, shift, weights, cot_sum)


def attended_grad_kernel(cot_ref, w_ref, out_ref, sum_ref, *, group):
    cot = cot_ref[...]
    px = cot.shape[0]
    weight = outer_weight_of(w_ref, C // w_ref.shape[0])
    grad = dot_nt(jnp.concatenate(hilo(cot), axis=0), weight)
    grad = grad[:px] + grad[px:]
    portion = px // group
    for head in range(NH):
        for part in range(group):
            rows = slice(part * portion, (part + 1) * portion)
            out_ref[head * group + part] = join_halves(grad[rows, head * HD : (head + 1) * HD])
    sum_ref[...] = row_sum(cot)


def attended_gradient(cot, weights, ways, group):
    px = cot.shape[0]
    return pl.pallas_call(
        functools.partial(attended_grad_kernel, group=group),
        out_shape=[
            jax.ShapeDtypeStruct((ways, px // group // 2, 2 * HD), F32),
            jax.ShapeDtypeStruct((1, C), F32),
        ],
        compiler_params=pltpu.CompilerParams(vmem_limit_bytes=VMEM_LIMIT),
        cost_estimate=cost(3e9),
        name="attended_gradient",
    )(cot, weights)


def output_kernel(att_ref, res_ref, cot_ref, w_ref, bias_ref, out_ref, wg_ref, *, group):
    att = jnp.concatenate(
        [
            jnp.concatenate(
                [split_halves(att_ref[head * group + part]) for part in range(group)], axis=0
            )
            for head in range(NH)
        ],
        axis=1,
    )
    px = att.shape[0]
    high, low = hilo(att)
    weight = outer_weight_of(w_ref, C // w_ref.shape[0])
    out = dot(jnp.concatenate([high, low], axis=0), weight)
    out_ref[...] = res_ref[...] + out[:px] + out[px:] + bias_ref[...]
    cot_high, cot_low = hilo(cot_ref[...])
    grad = dot_tn(high, cot_high) + dot_tn(high, cot_low) + dot_tn(low, cot_high)
    shards, _, span = wg_ref.shape
    for shard in range(shards):
        mine = grad[shard * span : (shard + 1) * span]
        wg_ref[shard] = jnp.concatenate(
            [mine[:, part * span : (part + 1) * span] for part in range(C // span)], axis=0
        )


def output_step(att, residual, cot, weights, bias, dims, group):
    head_ways = dims[2]
    return pl.pallas_call(
        functools.partial(output_kernel, group=group),
        out_shape=[
            jax.ShapeDtypeStruct(residual.shape, F32),
            jax.ShapeDtypeStruct((head_ways, C, C // head_ways), F32),
        ],
        compiler_params=pltpu.CompilerParams(vmem_limit_bytes=VMEM_LIMIT),
        cost_estimate=cost(4e9),
        name="output_step",
    )(att, residual, cot, weights, bias)


def attention_kernel(*refs, group, sources, portion):
    info, q_ref, do_ref = refs[:3]
    kv_refs = refs[3 : 3 + group]
    ctx_ref, o_ref, dq_ref = refs[3 + group : 6 + group]
    dkv_refs = refs[6 + group : 6 + 2 * group]
    dctx_ref = refs[6 + 2 * group]
    k4, v4, kt, vt, ck4, cv4, ckt, cvt, s_sc, dk_acc, dv_acc, cdk, cdv = refs[7 + 2 * group :]
    step = pl.program_id(0)
    own = sources * portion
    chunk = own // GRAN
    piece = 512 if own % 512 == 0 else own

    def prepare(kv, k4_at, v4_at):
        kh, kl = hilo(kv[:, :HD])
        vh, vl = hilo(kv[:, HD:])
        k4_at[...] = jnp.concatenate([kh, kl, kh, kl], axis=1)
        v4_at[...] = jnp.concatenate([vh, vl, vh, vl], axis=1)
        high, low = hilo(kv.T)
        return (
            jnp.concatenate([high[:HD], low[:HD]], axis=0),
            jnp.concatenate([high[HD:], low[HD:]], axis=0),
        )

    @pl.when(step == 0)
    def _():
        for way in range(group):
            for start in range(0, own, piece):
                kv = kv_refs[way][start // portion : (start + piece) // portion]
                at = slice(way * own + start, way * own + start + piece)
                kt[:, at], vt[:, at] = prepare(kv.reshape(piece, 2 * HD), k4.at[at], v4.at[at])
        for slot in range(SLOTS):
            ckt[slot], cvt[slot] = prepare(ctx_ref[slot], ck4.at[slot], cv4.at[slot])
        dk_acc[...] = jnp.zeros_like(dk_acc)
        dv_acc[...] = jnp.zeros_like(dv_acc)
        cdk[...] = jnp.zeros_like(cdk)
        cdv[...] = jnp.zeros_like(cdv)

    boundary = GRAN - sum(info[part * (ROWS_SEQ // GRAN)] for part in range(GRAN))
    gran = step // (pl.num_programs(0) // GRAN)
    slot = (gran >= boundary).astype(jnp.int32)
    first = jnp.where(slot == 0, 0, boundary)
    last = jnp.where(slot == 0, boundary, GRAN)
    packed = q_ref[...].reshape(-1, 2 * HD)
    turned = packed.T
    turned = jnp.concatenate([turned[:HD], turned[HD:]], axis=1)
    high, low = hilo(turned * (HD**-0.5 * LOG2E))
    q4 = jnp.concatenate([high, high, low, low], axis=0)
    q2 = jnp.concatenate(hilo(split_halves(packed) * HD**-0.5), axis=1)
    do_turned = do_ref[...].reshape(-1, 2 * HD).T
    do_turned = jnp.concatenate([do_turned[:HD], do_turned[HD:]], axis=1)

    def pack_back(values):
        half = values.shape[1] // 2
        return jnp.concatenate([values[:, :half], values[:, half:]], axis=0).T

    def take(high, low, turned_pair):
        both = dot(turned_pair, high)
        return both[:HD] + both[HD:] + dot(turned_pair[:HD], low)

    def places(g):
        return [
            pl.ds(pl.multiple_of(way * own + g * chunk, chunk), chunk) for way in range(group)
        ]

    ctx_scores = dot(ck4[slot], q4)
    token = lax.broadcasted_iota(jnp.int32, ctx_scores.shape, 0)
    ctx_scores = jnp.where(token < CTX_TOK, ctx_scores, -1e30)

    def score_pass(g, top):
        for at in places(g):
            scores = dot(k4[at, :], q4)
            s_sc[at, :] = scores
            top = jnp.maximum(top, jnp.max(scores, axis=0, keepdims=True))
        return top

    top = lax.fori_loop(first, last, score_pass, jnp.max(ctx_scores, axis=0, keepdims=True))
    ctx_p = jnp.exp2(ctx_scores - top)

    def value_pass(g, carry):
        total, out = carry
        for at in places(g):
            p = jnp.exp2(s_sc[at, :] - top)
            s_sc[at, :] = p
            total = total + row_sum(p)
            out = out + take(*hilo(p), vt[:, at])
        return total, out

    total, out = lax.fori_loop(
        first, last, value_pass, (row_sum(ctx_p), take(*hilo(ctx_p), cvt[slot]))
    )
    inverse = 1.0 / total
    out = out * inverse
    o_ref[...] = pack_back(out).reshape(o_ref.shape)
    do_scaled = do_turned * inverse
    diagonal = row_sum(do_scaled * out)
    high, low = hilo(do_scaled)
    d4 = jnp.concatenate([high, high, low, low], axis=0)
    d2 = jnp.concatenate(hilo(split_halves(pack_back(do_scaled))), axis=1)
    d22 = jnp.concatenate([d2, d2], axis=0)
    q22 = jnp.concatenate([q2, q2], axis=0)

    def back(p, values, keys_turned):
        ds = p * (dot(values, d4) - diagonal)
        ds_high, ds_low = hilo(ds)
        p_high, p_low = hilo(p)
        dv = dot(jnp.concatenate([p_high, p_low], axis=1), d22)
        dk = dot(jnp.concatenate([ds_high, ds_low], axis=1), q22)
        return dk, dv, take(ds_high, ds_low, keys_turned)

    dk, dv, dq = back(ctx_p, cv4[slot], ckt[slot])
    cdk[slot] += dk
    cdv[slot] += dv

    def gradient_pass(g, dq):
        for at in places(g):
            dk, dv, part = back(s_sc[at, :], v4[at, :], kt[:, at])
            dk_acc[at, :] += dk
            dv_acc[at, :] += dv
            dq = dq + part
        return dq

    dq = lax.fori_loop(first, last, gradient_pass, dq) * HD**-0.5
    dq_ref[...] = pack_back(dq).reshape(dq_ref.shape)

    def fold(pair):
        return pair[:, :HD] + pair[:, HD:]

    @pl.when(step == pl.num_programs(0) - 1)
    def _():
        for way in range(group):
            for start in range(0, own, piece):
                at = slice(way * own + start, way * own + start + piece)
                joined = jnp.concatenate([fold(dk_acc[at, :]), fold(dv_acc[at, :])], axis=1)
                dkv_refs[way][start // portion : (start + piece) // portion] = joined.reshape(
                    piece // portion, portion, 2 * HD
                )
        for slot in range(SLOTS):
            dctx_ref[slot] = jnp.concatenate([fold(cdk[slot]), fold(cdv[slot])], axis=1)


def attention(info, traded, do, others, ctx, group):
    sources = traded.shape[0]
    half = do.shape[1]
    portion = 2 * half
    own = sources * portion
    keys = group * own
    per_step = min(own // GRAN, QUERIES) // portion
    steps = sources // per_step
    q_block = pl.BlockSpec((per_step, half, 2 * HD), lambda i: (i, 2, 0))
    side_block = pl.BlockSpec((per_step, half, 2 * HD), lambda i: (i, 0, 0))
    kv_shape = (sources, portion, 2 * HD)
    pair_shape = (SLOTS, CTX_PAD, 2 * HD)
    return pl.pallas_call(
        functools.partial(attention_kernel, group=group, sources=sources, portion=portion),
        grid=(steps,),
        in_specs=[pl.BlockSpec(memory_space=pltpu.SMEM), q_block, side_block]
        + [whole_block(kv_shape)] * group
        + [whole_block(pair_shape)],
        out_specs=[side_block, side_block] + [whole_block(kv_shape)] * group + [whole_block(pair_shape)],
        out_shape=[jax.ShapeDtypeStruct((sources, half, 2 * HD), F32)] * 2
        + [jax.ShapeDtypeStruct(kv_shape, F32)] * group
        + [jax.ShapeDtypeStruct(pair_shape, F32)],
        scratch_shapes=[
            pltpu.VMEM((keys, 4 * HD), BF),
            pltpu.VMEM((keys, 4 * HD), BF),
            pltpu.VMEM((2 * HD, keys), BF),
            pltpu.VMEM((2 * HD, keys), BF),
            pltpu.VMEM((SLOTS, CTX_PAD, 4 * HD), BF),
            pltpu.VMEM((SLOTS, CTX_PAD, 4 * HD), BF),
            pltpu.VMEM((SLOTS, 2 * HD, CTX_PAD), BF),
            pltpu.VMEM((SLOTS, 2 * HD, CTX_PAD), BF),
            pltpu.VMEM((keys, per_step * portion), F32),
            pltpu.VMEM((keys, 2 * HD), F32),
            pltpu.VMEM((keys, 2 * HD), F32),
            pltpu.VMEM(pair_shape, F32),
            pltpu.VMEM(pair_shape, F32),
        ],
        compiler_params=pltpu.CompilerParams(vmem_limit_bytes=VMEM_LIMIT),
        cost_estimate=cost(6e10),
        name="attention",
    )(info, traded, do, traded, *others, ctx)


def rotated(values, axis):
    size = lax.axis_size(axis)
    return [values] + [
        lax.ppermute(values, axis, [(i, (i + d) % size) for i in range(size)])
        for d in range(1, size)
    ]


def gathered(values, axis):
    size = lax.axis_size(axis)
    pieces = rotated(values, axis)[::-1]
    stacked = jnp.stack(pieces + pieces[:-1])
    return lax.dynamic_slice_in_dim(stacked, size - 1 - lax.axis_index(axis), size, 0)


def band_stats(stat, px):
    parts = rotated(stat, "heads")
    mean = sum(part[0] for part in parts) / len(parts)
    spread = sum(part[1] + px * jnp.square(part[0] - mean) for part in parts)
    return jnp.stack([mean, spread])


def band_sums(sums):
    return sum(rotated(sums, "heads"))


def turned(values):
    size = lax.axis_size("heads")
    return lax.ppermute(
        values, SEQ, [(r * size + h, h * size + r) for r in range(size) for h in range(size)]
    )


def after(values, *others):
    return lax.optimization_barrier((values, *others))[0]


def halo(edge_low, edge_high):
    size = lax.axis_size("rows") * lax.axis_size("heads")
    forward = [(i, i + 1) for i in range(size - 1)]
    backward = [(i + 1, i) for i in range(size - 1)]
    return lax.ppermute(edge_high, SEQ, forward), lax.ppermute(edge_low, SEQ, backward)


def edges(values):
    return halo(values[:WID], values[-WID:])


def trade(values):
    return lax.all_to_all(values, SEQ, split_axis=0, concat_axis=0, tiled=True)


def per_device(
    pixels,
    crop_slot,
    embedding,
    context,
    first_gain,
    first_offset,
    first_kernel,
    first_bias,
    embed_weight,
    embed_bias,
    second_gain,
    second_offset,
    second_kernel,
    second_bias,
    attend_gain,
    attend_offset,
    inner_weight,
    inner_bias,
    context_weight,
    context_bias,
    outer_weight,
    outer_bias,
    cotangent,
):
    row_count = pixels.shape[0]
    assert pixels.shape[1] == 1
    ranks = lax.axis_size("rows")
    head_ways = lax.axis_size("heads")
    halves = lax.axis_size("dp")
    ways = ranks * head_ways
    group = ways // NH
    px = row_count * WID
    dims = (px, ways, head_ways)
    rank = lax.axis_index("rows")
    head_rank = lax.axis_index("heads")
    joint = rank * head_ways + head_rank
    shard_heads = NH // head_ways
    span = shard_heads * HD
    square = ranks == head_ways and NH // ranks == shard_heads

    slots = crop_slot[:, 0]
    hier = head_ways == 4
    part_order = [head_rank ^ d if hier else d for d in range(head_ways)]
    info = jnp.concatenate(
        [slots, jnp.stack([rank, joint, lax.axis_index("dp")] + part_order).astype(jnp.int32)]
    )
    split = halves == 2 and hier

    x = pixels.reshape(px, C)
    cot = cotangent.reshape(px, C)

    def row(vector):
        return vector.reshape(1, C)

    bias_rows = jnp.stack(
        [inner_bias[0].reshape(span), jnp.zeros((span,), F32), inner_bias[1].reshape(span)]
    )
    own_inner = jnp.concatenate(
        [
            inner_weight.astype(F32).transpose(1, 0, 2, 3).reshape(3, C, span),
            jnp.pad(bias_rows[:, None], ((0, 0), (0, 7), (0, 0))),
        ],
        axis=1,
    ).reshape(3 * (C + 8), span)
    own_outer = (
        outer_weight.astype(F32)
        .reshape(span, C // span, span)
        .transpose(1, 0, 2)
        .reshape(C, span)
    )
    outer_w = lax.all_gather(own_outer, "heads", axis=0, tiled=False)

    mean = jnp.mean(x, axis=0)
    x_stat = jnp.stack([mean, jnp.sum(jnp.square(x - mean), axis=0)])
    band_stat = band_stats(x_stat, px)
    pays0 = rotated(band_stat, "rows")
    x_halo = edges(x)
    inner_w = lax.all_gather(own_inner, "heads", axis=0, tiled=False)
    first_k = first_kernel.reshape(3, 3 * C, C)
    second_k = second_kernel.reshape(3, 3 * C, C)
    conv1, act1, stat1, x_vec = conv_forward(
        info, x, x_halo, pays0, row(first_gain), row(first_offset), first_k, row(first_bias), None, dims
    )

    ctx_flat = context[0].reshape(SLOTS * CTX_TOK, context.shape[-1])
    ctx_pair = jnp.dot(
        after(ctx_flat, conv1),
        context_weight.reshape(context.shape[-1], 2 * span),
        preferred_element_type=F32,
    ).reshape(SLOTS * CTX_TOK, 2, shard_heads, HD)
    ctx_pair = ctx_pair + jnp.stack([jnp.zeros_like(context_bias), context_bias])
    ctx_pair = ctx_pair.transpose(2, 0, 1, 3).reshape(shard_heads, SLOTS * CTX_TOK, 2 * HD)
    own_head = joint // group
    if square:
        ctx_all, at = turned(ctx_pair), own_head % shard_heads
    else:
        ctx_all, at = lax.all_gather(ctx_pair, "heads", axis=0, tiled=True), own_head
    ctx_own = lax.dynamic_index_in_dim(ctx_all, at, 0, keepdims=False)
    ctx_own = jnp.pad(
        ctx_own.reshape(SLOTS, CTX_TOK, 2 * HD), ((0, 0), (0, CTX_PAD - CTX_TOK), (0, 0))
    )

    embed_act = jax.nn.silu(embedding[0])
    modulation = jnp.dot(after(embed_act, conv1), embed_weight.astype(F32), precision=HIGH) + embed_bias
    own_slot = slots[joint * row_count]
    own_mod = lax.dynamic_index_in_dim(modulation, own_slot, 0, keepdims=True)
    lift = 1.0 + own_mod[:, :C]
    second_scale = row(second_gain) * lift
    second_shift = row(second_offset) * lift + own_mod[:, C:]
    def swapped(values):
        return lax.ppermute(values, "dp", [(0, 1), (1, 0)])

    conv1_halo = edges(conv1)
    pays1 = rotated(band_stats(stat1, px), "rows")
    do_blocks, cot_sum = attended_gradient(cot, outer_w, ways, group)
    pays1[0] = after(pays1[0], do_blocks)
    residual, act2, stat2, vec1 = conv_forward(
        info, conv1, conv1_halo, pays1, second_scale, second_shift, second_k, row(second_bias), x, dims
    )
    do_own = trade(do_blocks)
    acts = [act1, act2]
    band_stat = band_stats(stat2, px)
    band_stat = after(band_stat, ctx_own)
    if split:
        acts += [swapped(act) for act in acts]
        band_stat = after(band_stat, acts[2])

    pays2 = rotated(band_stat, "rows")
    pays2[0] = after(pays2[0], do_own)
    blocks, vec2 = project(
        info, residual, pays2, row(attend_gain), row(attend_offset), inner_w, dims, group
    )
    traded = trade(blocks)
    res_halo = edges(after(residual, blocks))
    cot_halo = edges(after(cot, blocks))
    act_seqs = rotated(after(embed_act, blocks), "dp")
    acts = jnp.stack(acts, axis=1)
    traded, acts, res_halo, cot_halo, act_seqs = lax.optimization_barrier(
        (traded, acts, res_halo, cot_halo, act_seqs)
    )
    ctx_seqs = rotated(after(ctx_flat.astype(F32), traded), "dp")
    portion = px // group
    own_kv = traded[:, :portion]

    def mates(d):
        return [(i, i // group * group + (i % group + d) % group) for i in range(ways)]

    others = [lax.ppermute(own_kv, SEQ, mates(group - d)) for d in range(1, group)]
    acts = lax.all_to_all(after(acts, *others), "heads", split_axis=0, concat_axis=0, tiled=True)
    results = attention(info, traded, do_own, others, ctx_own, group)
    att_own, dq_own = results[:2]
    dkv_parts = list(results[2 : 2 + group])
    ctx_grad = results[2 + group]
    dkv = dkv_parts[0]
    for d in range(1, group):
        dkv = dkv + lax.ppermute(dkv_parts[d], SEQ, mates(d))
    dkv = after(dkv, acts, tuple(ctx_seqs))
    grads = trade(jnp.concatenate([dkv, dq_own], axis=1))

    ctx_grad = after(ctx_grad, dkv)[:, :CTX_TOK].reshape(SLOTS * CTX_TOK, 2 * HD)
    if square:
        ctx_grads = jnp.stack(rotated(ctx_grad, "heads"))
        ctx_order = (head_rank - jnp.arange(head_ways)) % head_ways // group
        ctx_row = jnp.stack(
            [
                jnp.sum(jnp.where((ctx_order == head)[:, None, None], ctx_grads, 0.0), axis=0)
                for head in range(shard_heads)
            ]
        )
        ctx_mine = turned(after(ctx_row, grads))
    else:
        ctx_grads = lax.all_gather(ctx_grad, SEQ, axis=0, tiled=False)
        ctx_grads = jnp.sum(ctx_grads.reshape(NH, group, SLOTS * CTX_TOK, 2 * HD), axis=1)
        ctx_mine = lax.dynamic_slice_in_dim(ctx_grads, head_rank * shard_heads, shard_heads, 0)

    normed_grad, sums2, inner_part = project_back(
        grads, residual, vec2, row(attend_gain), row(attend_offset), inner_w, cot_sum, dims, group
    )

    def far_of(grad):
        if not split:
            return grad
        return [grad[0], swapped(grad[1]), flip(grad[0], 2)]

    def band_of(hops, *waiting):
        if not split:
            return [lax.all_gather(hops[0], "heads", axis=0, tiled=True)]
        mine, other, far = (after(hop, *waiting) if waiting else hop for hop in hops)
        other_far = flip(other, 2)
        return [
            mine,
            flip(mine, 1),
            far,
            flip(far, 1),
            other,
            flip(other, 1),
            other_far,
            flip(other_far, 1),
        ]

    def flip(values, bit):
        return lax.ppermute(values, "heads", [(i, i ^ bit) for i in range(head_ways)])

    ng_halo = edges(normed_grad)
    band_sum = band_sums(sums2)
    pays3 = rotated(band_sum, "rows")
    attended = trade(after(att_own, grads, pays3[-1]))

    def shard_sum(parts):
        return lax.psum_scatter(parts, "heads", scatter_dimension=0, tiled=False)

    inner_sum = shard_sum(inner_part)
    *residual_grad, hidden_grad, sums1 = conv_backward(
        info,
        normed_grad,
        ng_halo,
        residual,
        res_halo,
        vec2,
        row(attend_gain),
        pays3,
        [cot, *cot_halo],
        second_k,
        (conv1, vec1, second_scale, second_shift),
        dims,
        split,
    )
    hg_halo = edges(hidden_grad)
    band_sum = after(band_sums(sums1), attended)
    pays4 = rotated(band_sum, "rows")
    second_hops = far_of([after(grad, band_sum) for grad in residual_grad])
    output, outer_part = output_step(
        after(attended, band_sum, inner_sum), residual, cot, outer_w, row(outer_bias), dims, group
    )
    inner_sum = lax.psum_scatter(inner_sum, "rows", scatter_dimension=0, tiled=True)
    outer_part, pays4[0] = lax.optimization_barrier((outer_part, pays4[0]))
    outer_sum = lax.psum_scatter(
        shard_sum(outer_part), "rows", scatter_dimension=0, tiled=True
    )
    *conv1_grad, pre_grad, sums0 = conv_backward(
        info,
        hidden_grad,
        hg_halo,
        conv1,
        conv1_halo,
        vec1,
        second_scale,
        pays4,
        None,
        first_k,
        (x, x_vec, row(first_gain), row(first_offset)),
        dims,
        split,
    )
    second_band = band_of(second_hops, pre_grad)
    first_hops = far_of(conv1_grad)
    first_band = band_of(first_hops)
    if split:
        second_band[0] = after(second_band[0], tuple(first_hops), first_band[1])

    def kernel_sum(at, band, *waits):
        seqs = [acts, acts] if split else [acts]
        part = kernel_grad(info, seqs, (at, at + 2)[: len(seqs)], band, ranks)
        if not split:
            part = lax.psum_scatter(part, "dp", scatter_dimension=3, tiled=True)
        parts = lax.all_to_all(part, "rows", split_axis=0, concat_axis=0)
        return jnp.sum(after(parts, *waits), axis=0).reshape(3, 3, C // ways, C // halves), part

    second_kernel_grad, second_part = kernel_sum(1, second_band)
    first_kernel_grad, first_part = kernel_sum(0, first_band)
    inner_sum = gathered(sum(rotated(after(inner_sum, second_part), "dp")), "rows")
    outer_sum = gathered(sum(rotated(after(outer_sum, first_part), "dp")), "rows")
    pays5 = rotated(band_sums(after(sums0, first_kernel_grad)), "rows")
    pixels_grad = final_norm(
        info, pre_grad, x, x_vec, row(first_gain), residual_grad, pays5, dims
    )
    inner_sum = inner_sum.reshape(3, GRAD_ROWS, span)
    inner_weight_grad = inner_sum[:, :C].reshape(3, C, shard_heads, HD).transpose(1, 0, 2, 3)
    bias_sum = inner_sum[:, C].reshape(3, shard_heads, HD)
    inner_bias_grad = jnp.stack([bias_sum[0], bias_sum[2]])
    outer_weight_grad = (
        outer_sum
        .reshape(C // span, span, span)
        .transpose(1, 0, 2)
        .reshape(shard_heads, HD, C)
    )

    ctx_mine = (
        ctx_mine.reshape(shard_heads, SLOTS * CTX_TOK, 2, HD)
        .transpose(1, 2, 0, 3)
        .reshape(SLOTS * CTX_TOK, 2 * span)
    )
    mine_seqs = rotated(after(ctx_mine, first_part), "dp")
    context_weight_grad = jnp.dot(
        after(jnp.concatenate(ctx_seqs, axis=0).T, first_part), jnp.concatenate(mine_seqs, axis=0), precision=HIGH
    ).reshape(context.shape[-1], 2, shard_heads, HD)
    context_bias_grad = jnp.sum(sum(mine_seqs), axis=0).reshape(2, shard_heads, HD)[1]

    attend_sums = sum(after(tuple(pays3), first_part))
    band_slots = slots[:: row_count * head_ways]
    band_slots = jnp.stack([band_slots[(rank - d) % ranks] for d in range(ranks)])
    slot_rows = (band_slots[None, :] == jnp.arange(SLOTS)[:, None]).astype(F32)
    late4 = after(tuple(pays4), first_part)
    by_slot = sum(slot_rows[:, d, None, None] * late4[d] for d in range(ranks))
    shift_grad, hat_grad = by_slot[:, 0], by_slot[:, 1]
    mod_lift = 1.0 + modulation[:, :C]
    scale_grad = hat_grad * second_gain + shift_grad * second_offset
    pack = jnp.concatenate(
        [
            attend_sums,
            jnp.stack(
                [
                    jnp.sum(hat_grad * mod_lift, axis=0),
                    jnp.sum(shift_grad * mod_lift, axis=0),
                    jnp.sum(by_slot[:, 2], axis=0),
                ]
            ),
            scale_grad,
            shift_grad,
        ],
        axis=0,
    )
    packs = rotated(pack, "dp")
    vectors = sum(packs)
    mod_grads = jnp.concatenate(
        [jnp.concatenate([p[6 : 6 + SLOTS], p[6 + SLOTS :]], axis=1) for p in packs], axis=0
    )
    embed_bias_grad = jnp.sum(mod_grads, axis=0)
    embed_rows = embed_weight.shape[0] // ways
    embed_cols = 2 * C // halves
    embed_weight_grad = jnp.einsum(
        "ke,kc->ec",
        lax.dynamic_slice_in_dim(jnp.concatenate(act_seqs, axis=0), joint * embed_rows, embed_rows, 1),
        lax.dynamic_slice_in_dim(mod_grads, lax.axis_index("dp") * embed_cols, embed_cols, 1),
        precision=HIGH,
    )
    first_sums = sum(rotated(sum(pays5), "dp"))

    shape = pixels.shape
    return (
        output.reshape(shape),
        pixels_grad.reshape(shape),
        first_sums[1],
        first_sums[0],
        first_kernel_grad,
        first_sums[2],
        embed_weight_grad,
        embed_bias_grad,
        vectors[3],
        vectors[4],
        second_kernel_grad,
        vectors[5],
        vectors[1],
        vectors[0],
        inner_weight_grad,
        inner_bias_grad,
        context_weight_grad,
        context_bias_grad,
        outer_weight_grad,
        vectors[2],
    )


def solution(mesh):
    band = P(SEQ, "dp", None, None)
    kernel_out = P(None, None, SEQ, "dp")
    return jax.shard_map(
        per_device,
        mesh=mesh,
        in_specs=(
            band,
            P(None, "dp"),
            P("dp", None, None),
            P("dp", None, None, None),
            P(),
            P(),
            P(),
            P(),
            P(),
            P(),
            P(),
            P(),
            P(),
            P(),
            P(),
            P(),
            P(None, None, "heads", None),
            P(None, "heads", None),
            P(None, None, "heads", None),
            P("heads", None),
            P("heads", None, None),
            P(),
            band,
        ),
        out_specs=(
            band,
            band,
            P(),
            P(),
            kernel_out,
            P(),
            P(SEQ, "dp"),
            P(),
            P(),
            P(),
            kernel_out,
            P(),
            P(),
            P(),
            P(None, None, "heads", None),
            P(None, "heads", None),
            P(None, None, "heads", None),
            P("heads", None),
            P("heads", None, None),
            P(),
        ),
        check_vma=False,
    )
```

```python
import functools

import jax
import jax.numpy as jnp
from jax import lax
from jax.experimental import pallas as pl
from jax.experimental.pallas import tpu as pltpu
from jax.sharding import PartitionSpec as P

C = 512
NH = 8
HD = 64
GROUPS = 32
GROUP_C = C // GROUPS
CTX_TOK = 81
CTX_PAD = 128
GRAD_ROWS = 576
QUERIES = 512
WID = 64
SLOTS = 2
ROWS_SEQ = 64
GRAN = 4
EPS = 1e-05
LOG2E = 1.4426950408889634
F32 = jnp.float32
BF = jnp.bfloat16
SEQ = ("rows", "heads")
HIGH = lax.Precision.HIGHEST
VMEM_LIMIT = 56 << 20


def hilo(values):
    high = values.astype(BF)
    return high, (values - high.astype(F32)).astype(BF)


def dot(left, right):
    return jnp.dot(left, right, preferred_element_type=F32)


def dot_nt(left, right):
    return lax.dot_general(left, right, (((1,), (1,)), ((), ())), preferred_element_type=F32)


def dot_tn(left, right):
    return lax.dot_general(left, right, (((0,), (0,)), ((), ())), preferred_element_type=F32)


def group_mean(values):
    lane = lax.broadcasted_iota(jnp.int32, values.shape, 1)
    for step in (1, 2, 4, 8):
        up = pltpu.roll(values, step, 1)
        down = pltpu.roll(values, C - step, 1)
        values = values + jnp.where((lane & step) != 0, up, down)
    return values * (1.0 / GROUP_C)


def wide(row):
    return jnp.broadcast_to(row, (8, C))


def scalars(info, ranks, rows):
    rank, joint = info[ROWS_SEQ], info[ROWS_SEQ + 1]
    band = ROWS_SEQ // ranks
    own = info[joint * rows]
    found = []
    for step in range(ranks):
        other = rank - step
        other = jnp.where(other < 0, other + ranks, other)
        found.append(info[other * band] == own)
    first, last = joint * rows, joint * rows + rows
    found.append((first > 0) & (info[jnp.maximum(first - 1, 0)] == own))
    found.append((last < ROWS_SEQ) & (info[jnp.minimum(last, ROWS_SEQ - 1)] == own))
    return [jnp.where(item, 1.0, 0.0).astype(F32) for item in found]


def norm_stats(pays, scal, px):
    count = sum(scal[i] for i in range(len(pays)))
    mean = sum(scal[i] * wide(pay[0:1, :]) for i, pay in enumerate(pays)) / count
    spread = sum(
        scal[i] * (wide(pay[1:2, :]) + px * jnp.square(wide(pay[0:1, :]) - mean))
        for i, pay in enumerate(pays)
    )
    total = count * px
    center = group_mean(mean)
    variance = group_mean(spread + total * jnp.square(mean - center)) / total
    return center[0:1], (1.0 / jnp.sqrt(variance + EPS))[0:1]


def back_means(pays, scal, gain, px):
    count = sum(scal[i] for i in range(len(pays))) * px
    first = sum(scal[i] * wide(pay[0:1, :]) for i, pay in enumerate(pays))
    second = sum(scal[i] * wide(pay[1:2, :]) for i, pay in enumerate(pays))
    return (group_mean(first * gain) / count)[0:1], (group_mean(second * gain) / count)[0:1]


def local_stats(values):
    mean = jnp.mean(values, axis=0, keepdims=True)
    return mean, jnp.sum(jnp.square(values - mean), axis=0, keepdims=True)


def row_sum(values):
    return jnp.sum(values, axis=0, keepdims=True)


def shifted(values, tap):
    if tap == 1:
        return values
    column = lax.broadcasted_iota(jnp.int32, values.shape, 0) % WID
    rows = values.shape[0]
    if tap == 0:
        return jnp.where(column == 0, 0.0, pltpu.roll(values, 1, 0))
    return jnp.where(column == WID - 1, 0.0, pltpu.roll(values, rows - 1, 0))


def fill_taps(values, high_ref, low_ref, row, width):
    for tap in range(3):
        high, low = hilo(shifted(values, tap))
        high_ref[row : row + values.shape[0], tap * width : (tap + 1) * width] = high
        low_ref[row : row + values.shape[0], tap * width : (tap + 1) * width] = low


def conv_forward_kernel(*refs, px, ways, ranks, has_skip):
    info, x_ref, top_ref, low_ref = refs[:4]
    pays = refs[4 : 4 + ranks]
    scale_ref, shift_ref, w_ref, bias_ref = refs[4 + ranks : 8 + ranks]
    rest = refs[8 + ranks :]
    band_px = float(px * (ways // ranks))
    if has_skip:
        skip_ref, rest = rest[0], rest[1:]
    out_ref, act_ref, stat_ref, vec_ref, high_sc, low_sc, acc = rest
    tap = pl.program_id(0)
    block = C // ways

    @pl.when(tap == 0)
    def _():
        scal = scalars(info, ranks, px // WID)
        mean, inverse = norm_stats(pays, scal, band_px)
        vec_ref[...] = jnp.concatenate([mean, inverse], axis=0)
        scale = scale_ref[...]
        shift = shift_ref[...]
        heads_count = act_ref.shape[0]

        def activate(values, weight, row):
            pre = (values - mean) * inverse * scale + shift
            act = pre / (1.0 + jnp.exp(-pre))
            if weight is not None:
                act = act * weight
            size = values.shape[0]
            fill_taps(act, high_sc, low_sc, row, C)
            for head in range(heads_count):
                act_ref[head, row : row + size, :] = jnp.concatenate(
                    [
                        act[:, (r * heads_count + head) * block : (r * heads_count + head + 1) * block]
                        for r in range(ways // heads_count)
                    ],
                    axis=1,
                )

        activate(top_ref[...], scal[ranks], 0)
        for row in range(px // WID):
            activate(x_ref[row * WID : (row + 1) * WID, :], None, (row + 1) * WID)
        activate(low_ref[...], scal[ranks + 1], px + WID)

    base = pl.multiple_of(tap * WID, WID)
    part = dot(
        jnp.concatenate([high_sc[pl.ds(base, px), :], low_sc[pl.ds(base, px), :]], axis=0), w_ref[0]
    )
    part = part[:px] + part[px:]

    @pl.when(tap == 0)
    def _():
        acc[...] = part

    @pl.when(tap == 1)
    def _():
        acc[...] += part

    @pl.when(tap == 2)
    def _():
        out = acc[...] + part + bias_ref[...]
        if has_skip:
            out = out + skip_ref[...]
        out_ref[...] = out
        stat_ref[...] = jnp.concatenate(local_stats(out), axis=0)


def cost(flops):
    return pl.CostEstimate(flops=int(flops), transcendentals=0, bytes_accessed=0)


def whole_block(shape):
    return pl.BlockSpec(shape, lambda *_: (0,) * len(shape), pipeline_mode=pl.Buffered(1))


def conv_forward(info, x, halo, pays, scale, shift, kernel, bias, skip, dims):
    px, ways, head_ways = dims
    ranks = len(pays)
    quarter = C // head_ways
    operands = [info, x, halo[0], halo[1], *pays, scale, shift, kernel, bias]
    specs = (
        [pl.BlockSpec(memory_space=pltpu.SMEM), whole_block((px, C))]
        + [whole_block((WID, C))] * 2
        + [whole_block(pays[0].shape)] * ranks
        + [whole_block((1, C))] * 2
        + [pl.BlockSpec((1, 3 * C, C), lambda i: (i, 0, 0)), whole_block((1, C))]
    )
    if skip is not None:
        operands.append(skip)
        specs.append(whole_block((px, C)))
    ext = px + 2 * WID
    return pl.pallas_call(
        functools.partial(
            conv_forward_kernel,
            px=px,
            ways=ways,
            ranks=ranks,
            has_skip=skip is not None,
        ),
        grid=(3,),
        in_specs=specs,
        out_specs=[
            whole_block((px, C)),
            whole_block((head_ways, ext, quarter)),
            whole_block((2, C)),
            whole_block((2, C)),
        ],
        out_shape=[
            jax.ShapeDtypeStruct((px, C), F32),
            jax.ShapeDtypeStruct((head_ways, ext, quarter), F32),
            jax.ShapeDtypeStruct((2, C), F32),
            jax.ShapeDtypeStruct((2, C), F32),
        ],
        scratch_shapes=[
            pltpu.VMEM((ext, 3 * C), BF),
            pltpu.VMEM((ext, 3 * C), BF),
            pltpu.VMEM((px, C), F32),
        ],
        compiler_params=pltpu.CompilerParams(vmem_limit_bytes=VMEM_LIMIT),
        cost_estimate=cost(7e9),
        name="conv_forward",
    )(*operands)


def halves_of(info, values, split):
    if not split:
        return [values]
    even = info[ROWS_SEQ + 2] == 0
    left, right = values[:, : C // 2], values[:, C // 2 :]
    return [jnp.where(even, left, right), jnp.where(even, right, left)]


def conv_backward_kernel(*refs, px, ways, ranks, has_add, split):
    info, yg_ref, yg_top, yg_low, x_ref, x_top, x_low, vec_ref, gain_ref = refs[:9]
    pays = refs[9 : 9 + ranks]
    rest = refs[9 + ranks :]
    band_px = float(px * (ways // ranks))
    if has_add:
        adds, rest = rest[:3], rest[3:]
    w_ref, in_ref, in_vec, in_scale, in_shift = rest[:5]
    g_refs = rest[5 : 7 if split else 6]
    h_ref, sum_ref, high_sc, low_sc, acc, bias_sum = rest[7 if split else 6 :]
    tap = pl.program_id(0)

    @pl.when(tap == 0)
    def _():
        scal = scalars(info, ranks, px // WID)
        gain = gain_ref[...]
        mean, inverse = vec_ref[0:1, :], vec_ref[1:2, :]
        first, second = back_means(pays, scal, gain, band_px)

        def gradient(yg, x, extra, weight, row):
            grad = (yg * gain - first - (x - mean) * inverse * second) * inverse
            if extra is not None:
                grad = grad + extra
            if weight is not None:
                grad = grad * weight
            fill_taps(grad, high_sc, low_sc, row, C)
            return grad

        gradient(yg_top[...], x_top[...], adds[1][...] if has_add else None, scal[ranks], 0)
        total = jnp.zeros((1, C), F32)
        for row in range(px // WID):
            at = slice(row * WID, (row + 1) * WID)
            grad = gradient(
                yg_ref[at, :],
                x_ref[at, :],
                adds[0][at, :] if has_add else None,
                None,
                (row + 1) * WID,
            )
            for ref, piece in zip(g_refs, halves_of(info, grad, split)):
                ref[at, :] = piece
            total = total + row_sum(grad)
        gradient(
            yg_low[...], x_low[...], adds[2][...] if has_add else None, scal[ranks + 1], px + WID
        )
        bias_sum[...] = total
        acc[...] = jnp.zeros_like(acc)

    base = pl.multiple_of(tap * WID, WID)
    part = acc[...]
    for col in range(3):
        weight = w_ref[0, (2 - col) * C : (3 - col) * C, :]
        at = (pl.ds(base, px), slice(col * C, (col + 1) * C))
        both = dot_nt(jnp.concatenate([high_sc[at], low_sc[at]], axis=0), weight)
        part = part + both[:px] + both[px:]
    acc[...] = part

    @pl.when(tap == 2)
    def _():
        hat = (in_ref[...] - in_vec[0:1, :]) * in_vec[1:2, :]
        pre = hat * in_scale[...] + in_shift[...]
        sigmoid = 1.0 / (1.0 + jnp.exp(-pre))
        h = acc[...] * (sigmoid * (1.0 + pre * (1.0 - sigmoid)))
        h_ref[...] = h
        sum_ref[...] = jnp.concatenate([row_sum(h), row_sum(h * hat), bias_sum[...]], axis=0)


def conv_backward(info, yg, yg_halo, x, x_halo, vec, gain, pays, adds, kernel, inner, dims, split):
    px, ways, _ = dims
    ranks = len(pays)
    in_x, in_vec, in_scale, in_shift = inner
    rows3 = [whole_block((px, C)), whole_block((WID, C)), whole_block((WID, C))]
    operands = [info, yg, *yg_halo, x, *x_halo, vec, gain, *pays]
    specs = (
        [pl.BlockSpec(memory_space=pltpu.SMEM)]
        + rows3
        + rows3
        + [whole_block((2, C)), whole_block((1, C))]
        + [whole_block(pays[0].shape)] * ranks
    )
    if adds is not None:
        operands += adds
        specs += rows3
    operands += [kernel, in_x, in_vec, in_scale, in_shift]
    specs += [
        pl.BlockSpec((1, 3 * C, C), lambda i: (2 - i, 0, 0)),
        whole_block((px, C)),
        whole_block((2, C)),
        whole_block((1, C)),
        whole_block((1, C)),
    ]
    ext = px + 2 * WID
    shapes = [(px, C // 2)] * 2 if split else [(px, C)]
    shapes += [(px, C), (3, C)]
    return pl.pallas_call(
        functools.partial(
            conv_backward_kernel,
            px=px,
            ways=ways,
            ranks=ranks,
            has_add=adds is not None,
            split=split,
        ),
        grid=(3,),
        in_specs=specs,
        out_specs=[whole_block(shape) for shape in shapes],
        out_shape=[jax.ShapeDtypeStruct(shape, F32) for shape in shapes],
        scratch_shapes=[
            pltpu.VMEM((ext, 3 * C), BF),
            pltpu.VMEM((ext, 3 * C), BF),
            pltpu.VMEM((px, C), F32),
            pltpu.VMEM((1, C), F32),
        ],
        compiler_params=pltpu.CompilerParams(vmem_limit_bytes=VMEM_LIMIT),
        cost_estimate=cost(7e9),
        name="conv_backward",
    )(*operands)


def kernel_grad_kernel(info, *refs, ranks, seqs, grad_count):
    acts, grads = refs[:seqs], refs[seqs : seqs + grad_count]
    out_ref, taps, g_high, g_low = refs[seqs + grad_count :]
    tap = pl.program_id(0)
    parts, _, ext, quarter = acts[0].shape
    px = ext - 2 * WID
    block = quarter // ranks

    @pl.when(tap == 0)
    def _():
        for seq in range(seqs):
            for part in range(parts):
                at = seq * parts + part
                act = acts[seq][info[ROWS_SEQ + 3 + part], 0]
                for col in range(3):
                    high, low = hilo(shifted(act, col))
                    taps[at, :, col * quarter : (col + 1) * quarter] = high
                    taps[at, :, (3 + col) * quarter : (4 + col) * quarter] = low
                rows = slice(at * px, (at + 1) * px)
                high, low = hilo(grads[at][...] if grad_count > 1 else grads[0][rows, :])
                g_high[rows, :] = high
                g_low[rows, :] = low

    base = pl.multiple_of(tap * WID, WID)
    left = jnp.concatenate([taps[at, pl.ds(base, px), :] for at in range(seqs * parts)], axis=0)
    both = dot_tn(left, g_high[...])
    rest = dot_tn(left[:, : 3 * quarter], g_low[...])
    total = both[: 3 * quarter] + both[3 * quarter :] + rest
    for rank in range(ranks):
        for col in range(3):
            start = col * quarter + rank * block
            out_ref[rank, 0, col * block : (col + 1) * block, :] = total[start : start + block]


def kernel_grad(info, acts, which, grads, ranks):
    parts, _, ext, quarter = acts[0].shape
    px = ext - 2 * WID
    cols = grads[0].shape[1]
    block = 3 * quarter // ranks
    seqs = len(acts)
    return pl.pallas_call(
        functools.partial(kernel_grad_kernel, ranks=ranks, seqs=seqs, grad_count=len(grads)),
        grid=(3,),
        in_specs=[pl.BlockSpec(memory_space=pltpu.SMEM)]
        + [
            pl.BlockSpec(
                (parts, 1, ext, quarter),
                lambda i, at=at: (0, at, 0, 0),
                pipeline_mode=pl.Buffered(1),
            )
            for at in which
        ]
        + [whole_block(grad.shape) for grad in grads],
        out_specs=pl.BlockSpec((ranks, 1, block, cols), lambda i: (0, i, 0, 0)),
        out_shape=jax.ShapeDtypeStruct((ranks, 3, block, cols), F32),
        scratch_shapes=[
            pltpu.VMEM((seqs * parts, ext, 6 * quarter), BF),
            pltpu.VMEM((seqs * parts * px, cols), BF),
            pltpu.VMEM((seqs * parts * px, cols), BF),
        ],
        compiler_params=pltpu.CompilerParams(vmem_limit_bytes=VMEM_LIMIT),
        cost_estimate=cost(6e9),
        name="kernel_grad",
    )(info, *acts, *grads)


def final_kernel(info, yg_ref, x_ref, vec_ref, gain_ref, *refs, band_px, count):
    adds, pays, out_ref = refs[:count], refs[count:-1], refs[-1]
    add = adds[0][...]
    if count == 2:
        even = info[ROWS_SEQ + 2] == 0
        other = adds[1][...]
        add = jnp.concatenate([jnp.where(even, add, other), jnp.where(even, other, add)], axis=1)
    scal = scalars(info, len(pays), x_ref.shape[0] // WID)
    gain = gain_ref[...]
    mean, inverse = vec_ref[0:1, :], vec_ref[1:2, :]
    first, second = back_means(pays, scal, gain, band_px)
    hat = (x_ref[...] - mean) * inverse
    out_ref[...] = add + (yg_ref[...] * gain - first - hat * second) * inverse


def final_norm(info, yg, x, vec, gain, adds, pays, dims):
    px, ways, _ = dims
    return pl.pallas_call(
        functools.partial(
            final_kernel, band_px=float(px * (ways // len(pays))), count=len(adds)
        ),
        in_specs=[pl.BlockSpec(memory_space=pltpu.SMEM)]
        + [pl.BlockSpec(memory_space=pltpu.VMEM)] * (4 + len(adds) + len(pays)),
        out_specs=pl.BlockSpec(memory_space=pltpu.VMEM),
        out_shape=jax.ShapeDtypeStruct(x.shape, F32),
        compiler_params=pltpu.CompilerParams(vmem_limit_bytes=VMEM_LIMIT),
        cost_estimate=cost(2e9),
        name="final_norm",
    )(info, yg, x, vec, gain, *adds, *pays)


def split_halves(packed):
    return jnp.concatenate([packed[:, :HD], packed[:, HD:]], axis=0)


def join_halves(values):
    half = values.shape[0] // 2
    return jnp.concatenate([values[:half], values[half:]], axis=1)


def inner_weight_of(w_ref, shard, span):
    rows = C + 8
    weight = jnp.concatenate(
        [w_ref[shard, part * rows : part * rows + C, :].astype(BF) for part in range(3)], axis=1
    )
    bias = jnp.concatenate(
        [w_ref[shard, part * rows + C : part * rows + C + 1, :] for part in range(3)], axis=1
    )
    return weight, bias


def outer_weight_of(w_ref, span):
    return jnp.concatenate(
        [
            jnp.concatenate(
                [
                    w_ref[shard, part * span : (part + 1) * span, :].astype(BF)
                    for part in range(C // span)
                ],
                axis=1,
            )
            for shard in range(w_ref.shape[0])
        ],
        axis=0,
    )


def project_kernel(info, x_ref, scale_ref, shift_ref, w_ref, *refs, group, shard_heads, band_px):
    pays, (out_ref, vec_ref) = refs[:-2], refs[-2:]
    px = x_ref.shape[0]
    scal = scalars(info, len(pays), px // WID)
    mean, inverse = norm_stats(pays, scal, band_px)
    vec_ref[...] = jnp.concatenate([mean, inverse], axis=0)
    high, low = hilo((x_ref[...] - mean) * inverse * scale_ref[...] + shift_ref[...])
    both = jnp.concatenate([high, low], axis=0)
    portion = px // group
    span = shard_heads * HD
    for shard in range(w_ref.shape[0]):
        weight, bias = inner_weight_of(w_ref, shard, span)
        inner = dot(both, weight)
        inner = inner[:px] + inner[px:] + bias
        for head in range(shard_heads):
            at = head * HD
            query = inner[:, at : at + HD]
            pair = jnp.concatenate(
                [inner[:, span + at : span + at + HD], inner[:, 2 * span + at : 2 * span + at + HD]],
                axis=1,
            )
            for part in range(group):
                slot = (shard * shard_heads + head) * group + part
                rows = slice(part * portion, (part + 1) * portion)
                out_ref[slot, :portion, :] = pair[rows]
                out_ref[slot, portion:, :] = join_halves(query[rows])


def project(info, x, pays, scale, shift, weights, dims, group):
    px, ways, _ = dims
    portion = px // group
    return pl.pallas_call(
        functools.partial(
            project_kernel,
            group=group,
            shard_heads=NH // weights.shape[0],
            band_px=float(px * (ways // len(pays))),
        ),
        in_specs=[pl.BlockSpec(memory_space=pltpu.SMEM)]
        + [pl.BlockSpec(memory_space=pltpu.VMEM)] * (4 + len(pays)),
        out_specs=[pl.BlockSpec(memory_space=pltpu.VMEM)] * 2,
        out_shape=[
            jax.ShapeDtypeStruct((ways, portion + portion // 2, 2 * HD), F32),
            jax.ShapeDtypeStruct((2, C), F32),
        ],
        compiler_params=pltpu.CompilerParams(vmem_limit_bytes=VMEM_LIMIT),
        cost_estimate=cost(5e9),
        name="project",
    )(info, x, scale, shift, weights, *pays)


def project_back_kernel(
    grad_ref, x_ref, vec_ref, scale_ref, shift_ref, w_ref, cot_sum, ng_ref, sum_ref, wg_ref, *, group, shard_heads
):
    px = x_ref.shape[0]
    hat = (x_ref[...] - vec_ref[0:1, :]) * vec_ref[1:2, :]
    normed_high, normed_low = hilo(hat * scale_ref[...] + shift_ref[...])
    portion = px // group
    span = shard_heads * HD
    grad = jnp.zeros((px, C), F32)
    for shard in range(w_ref.shape[0]):
        columns = [[], [], []]
        for head in range(shard_heads):
            slots = [(shard * shard_heads + head) * group + part for part in range(group)]
            pair = jnp.concatenate([grad_ref[slot, :portion, :] for slot in slots], axis=0)
            query = jnp.concatenate(
                [split_halves(grad_ref[slot, portion:, :]) for slot in slots], axis=0
            )
            columns[0].append(query)
            columns[1].append(pair[:, :HD])
            columns[2].append(pair[:, HD:])
        inner = jnp.concatenate(columns[0] + columns[1] + columns[2], axis=1)
        high, low = hilo(inner)
        weight, _ = inner_weight_of(w_ref, shard, span)
        part = dot_nt(jnp.concatenate([high, low], axis=0), weight)
        grad = grad + part[:px] + part[px:]
        weight_grad = (
            dot_tn(normed_high, high) + dot_tn(normed_high, low) + dot_tn(normed_low, high)
        )
        bias_grad = jnp.broadcast_to(row_sum(inner), (GRAD_ROWS - C, inner.shape[1]))
        tall = jnp.concatenate([weight_grad, bias_grad], axis=0)
        wg_ref[shard] = jnp.concatenate(
            [tall[:, part * span : (part + 1) * span] for part in range(3)], axis=0
        )
    ng_ref[...] = grad
    sum_ref[...] = jnp.concatenate([row_sum(grad), row_sum(grad * hat), cot_sum[...]], axis=0)


def project_back(grad, x, vec, scale, shift, weights, cot_sum, dims, group):
    px, _, head_ways = dims
    shape = (head_ways, 3 * GRAD_ROWS, C // head_ways)
    return pl.pallas_call(
        functools.partial(project_back_kernel, group=group, shard_heads=NH // head_ways),
        in_specs=[pl.BlockSpec(memory_space=pltpu.VMEM)] * 7,
        out_specs=[pl.BlockSpec(memory_space=pltpu.VMEM)] * 3,
        out_shape=[
            jax.ShapeDtypeStruct((px, C), F32),
            jax.ShapeDtypeStruct((3, C), F32),
            jax.ShapeDtypeStruct(shape, F32),
        ],
        compiler_params=pltpu.CompilerParams(vmem_limit_bytes=VMEM_LIMIT),
        cost_estimate=cost(7e9),
        name="project_back",
    )(grad, x, vec, scale, shift, weights, cot_sum)


def attended_grad_kernel(cot_ref, w_ref, out_ref, sum_ref, *, group):
    cot = cot_ref[...]
    px = cot.shape[0]
    weight = outer_weight_of(w_ref, C // w_ref.shape[0])
    grad = dot_nt(jnp.concatenate(hilo(cot), axis=0), weight)
    grad = grad[:px] + grad[px:]
    portion = px // group
    for head in range(NH):
        for part in range(group):
            rows = slice(part * portion, (part + 1) * portion)
            out_ref[head * group + part] = join_halves(grad[rows, head * HD : (head + 1) * HD])
    sum_ref[...] = row_sum(cot)


def attended_gradient(cot, weights, ways, group):
    px = cot.shape[0]
    return pl.pallas_call(
        functools.partial(attended_grad_kernel, group=group),
        out_shape=[
            jax.ShapeDtypeStruct((ways, px // group // 2, 2 * HD), F32),
            jax.ShapeDtypeStruct((1, C), F32),
        ],
        compiler_params=pltpu.CompilerParams(vmem_limit_bytes=VMEM_LIMIT),
        cost_estimate=cost(3e9),
        name="attended_gradient",
    )(cot, weights)


def output_kernel(att_ref, res_ref, cot_ref, w_ref, bias_ref, out_ref, wg_ref, *, group):
    att = jnp.concatenate(
        [
            jnp.concatenate(
                [split_halves(att_ref[head * group + part]) for part in range(group)], axis=0
            )
            for head in range(NH)
        ],
        axis=1,
    )
    px = att.shape[0]
    high, low = hilo(att)
    weight = outer_weight_of(w_ref, C // w_ref.shape[0])
    out = dot(jnp.concatenate([high, low], axis=0), weight)
    out_ref[...] = res_ref[...] + out[:px] + out[px:] + bias_ref[...]
    cot_high, cot_low = hilo(cot_ref[...])
    grad = dot_tn(high, cot_high) + dot_tn(high, cot_low) + dot_tn(low, cot_high)
    shards, _, span = wg_ref.shape
    for shard in range(shards):
        mine = grad[shard * span : (shard + 1) * span]
        wg_ref[shard] = jnp.concatenate(
            [mine[:, part * span : (part + 1) * span] for part in range(C // span)], axis=0
        )


def output_step(att, residual, cot, weights, bias, dims, group):
    head_ways = dims[2]
    return pl.pallas_call(
        functools.partial(output_kernel, group=group),
        out_shape=[
            jax.ShapeDtypeStruct(residual.shape, F32),
            jax.ShapeDtypeStruct((head_ways, C, C // head_ways), F32),
        ],
        compiler_params=pltpu.CompilerParams(vmem_limit_bytes=VMEM_LIMIT),
        cost_estimate=cost(4e9),
        name="output_step",
    )(att, residual, cot, weights, bias)


def attention_kernel(*refs, group, sources, portion):
    info, q_ref, do_ref = refs[:3]
    kv_refs = refs[3 : 3 + group]
    ctx_ref, o_ref, dq_ref = refs[3 + group : 6 + group]
    dkv_refs = refs[6 + group : 6 + 2 * group]
    dctx_ref = refs[6 + 2 * group]
    k4, v4, kt, vt, ck4, cv4, ckt, cvt, s_sc, dk_acc, dv_acc, cdk, cdv = refs[7 + 2 * group :]
    step = pl.program_id(0)
    own = sources * portion
    chunk = own // GRAN
    piece = 512 if own % 512 == 0 else own

    def prepare(kv, k4_at, v4_at):
        kh, kl = hilo(kv[:, :HD])
        vh, vl = hilo(kv[:, HD:])
        k4_at[...] = jnp.concatenate([kh, kl, kh, kl], axis=1)
        v4_at[...] = jnp.concatenate([vh, vl, vh, vl], axis=1)
        high, low = hilo(kv.T)
        return (
            jnp.concatenate([high[:HD], low[:HD]], axis=0),
            jnp.concatenate([high[HD:], low[HD:]], axis=0),
        )

    @pl.when(step == 0)
    def _():
        for way in range(group):
            for start in range(0, own, piece):
                kv = kv_refs[way][start // portion : (start + piece) // portion]
                at = slice(way * own + start, way * own + start + piece)
                kt[:, at], vt[:, at] = prepare(kv.reshape(piece, 2 * HD), k4.at[at], v4.at[at])
        for slot in range(SLOTS):
            ckt[slot], cvt[slot] = prepare(ctx_ref[slot], ck4.at[slot], cv4.at[slot])
        dk_acc[...] = jnp.zeros_like(dk_acc)
        dv_acc[...] = jnp.zeros_like(dv_acc)
        cdk[...] = jnp.zeros_like(cdk)
        cdv[...] = jnp.zeros_like(cdv)

    boundary = GRAN - sum(info[part * (ROWS_SEQ // GRAN)] for part in range(GRAN))
    gran = step // (pl.num_programs(0) // GRAN)
    slot = (gran >= boundary).astype(jnp.int32)
    first = jnp.where(slot == 0, 0, boundary)
    last = jnp.where(slot == 0, boundary, GRAN)
    packed = q_ref[...].reshape(-1, 2 * HD)
    turned = packed.T
    turned = jnp.concatenate([turned[:HD], turned[HD:]], axis=1)
    high, low = hilo(turned * (HD**-0.5 * LOG2E))
    q4 = jnp.concatenate([high, high, low, low], axis=0)
    q2 = jnp.concatenate(hilo(split_halves(packed) * HD**-0.5), axis=1)
    do_turned = do_ref[...].reshape(-1, 2 * HD).T
    do_turned = jnp.concatenate([do_turned[:HD], do_turned[HD:]], axis=1)

    def pack_back(values):
        half = values.shape[1] // 2
        return jnp.concatenate([values[:, :half], values[:, half:]], axis=0).T

    def take(high, low, turned_pair):
        both = dot(turned_pair, high)
        return both[:HD] + both[HD:] + dot(turned_pair[:HD], low)

    def places(g):
        return [
            pl.ds(pl.multiple_of(way * own + g * chunk, chunk), chunk) for way in range(group)
        ]

    ctx_scores = dot(ck4[slot], q4)
    token = lax.broadcasted_iota(jnp.int32, ctx_scores.shape, 0)
    ctx_scores = jnp.where(token < CTX_TOK, ctx_scores, -1e30)

    def score_pass(g, top):
        for at in places(g):
            scores = dot(k4[at, :], q4)
            s_sc[at, :] = scores
            top = jnp.maximum(top, jnp.max(scores, axis=0, keepdims=True))
        return top

    top = lax.fori_loop(first, last, score_pass, jnp.max(ctx_scores, axis=0, keepdims=True))
    ctx_p = jnp.exp2(ctx_scores - top)

    def value_pass(g, carry):
        total, out = carry
        for at in places(g):
            p = jnp.exp2(s_sc[at, :] - top)
            s_sc[at, :] = p
            high, low = hilo(p)
            ones = jnp.ones((16, chunk), BF)
            values = vt[:, at]
            both = dot(jnp.concatenate([values, ones], axis=0), high)
            rest = dot(jnp.concatenate([values[:HD], ones], axis=0), low)
            total = total + both[2 * HD : 2 * HD + 1] + rest[HD : HD + 1]
            out = out + both[:HD] + both[HD : 2 * HD] + rest[:HD]
        return total, out

    total, out = lax.fori_loop(
        first, last, value_pass, (row_sum(ctx_p), take(*hilo(ctx_p), cvt[slot]))
    )
    inverse = 1.0 / total
    out = out * inverse
    o_ref[...] = pack_back(out).reshape(o_ref.shape)
    do_scaled = do_turned * inverse
    diagonal = row_sum(do_scaled * out)
    high, low = hilo(do_scaled)
    d4 = jnp.concatenate([high, high, low, low], axis=0)
    d2 = jnp.concatenate(hilo(split_halves(pack_back(do_scaled))), axis=1)
    d22 = jnp.concatenate([d2, d2], axis=0)
    q22 = jnp.concatenate([q2, q2], axis=0)

    def back(p, values, keys_turned):
        ds = p * (dot(values, d4) - diagonal)
        ds_high, ds_low = hilo(ds)
        p_high, p_low = hilo(p)
        dv = dot(jnp.concatenate([p_high, p_low], axis=1), d22)
        dk = dot(jnp.concatenate([ds_high, ds_low], axis=1), q22)
        return dk, dv, take(ds_high, ds_low, keys_turned)

    dk, dv, dq = back(ctx_p, cv4[slot], ckt[slot])
    cdk[slot] += dk
    cdv[slot] += dv

    def gradient_pass(g, dq):
        for at in places(g):
            dk, dv, part = back(s_sc[at, :], v4[at, :], kt[:, at])
            dk_acc[at, :] += dk
            dv_acc[at, :] += dv
            dq = dq + part
        return dq

    dq = lax.fori_loop(first, last, gradient_pass, dq) * HD**-0.5
    dq_ref[...] = pack_back(dq).reshape(dq_ref.shape)

    def fold(pair):
        return pair[:, :HD] + pair[:, HD:]

    @pl.when(step == pl.num_programs(0) - 1)
    def _():
        for way in range(group):
            for start in range(0, own, piece):
                at = slice(way * own + start, way * own + start + piece)
                joined = jnp.concatenate([fold(dk_acc[at, :]), fold(dv_acc[at, :])], axis=1)
                dkv_refs[way][start // portion : (start + piece) // portion] = joined.reshape(
                    piece // portion, portion, 2 * HD
                )
        for slot in range(SLOTS):
            dctx_ref[slot] = jnp.concatenate([fold(cdk[slot]), fold(cdv[slot])], axis=1)


def attention(info, traded, do, others, ctx, group):
    sources = traded.shape[0]
    half = do.shape[1]
    portion = 2 * half
    own = sources * portion
    keys = group * own
    per_step = min(own // GRAN, QUERIES) // portion
    steps = sources // per_step
    q_block = pl.BlockSpec((per_step, half, 2 * HD), lambda i: (i, 2, 0))
    side_block = pl.BlockSpec((per_step, half, 2 * HD), lambda i: (i, 0, 0))
    kv_shape = (sources, portion, 2 * HD)
    pair_shape = (SLOTS, CTX_PAD, 2 * HD)
    return pl.pallas_call(
        functools.partial(attention_kernel, group=group, sources=sources, portion=portion),
        grid=(steps,),
        in_specs=[pl.BlockSpec(memory_space=pltpu.SMEM), q_block, side_block]
        + [whole_block(kv_shape)] * group
        + [whole_block(pair_shape)],
        out_specs=[side_block, side_block] + [whole_block(kv_shape)] * group + [whole_block(pair_shape)],
        out_shape=[jax.ShapeDtypeStruct((sources, half, 2 * HD), F32)] * 2
        + [jax.ShapeDtypeStruct(kv_shape, F32)] * group
        + [jax.ShapeDtypeStruct(pair_shape, F32)],
        scratch_shapes=[
            pltpu.VMEM((keys, 4 * HD), BF),
            pltpu.VMEM((keys, 4 * HD), BF),
            pltpu.VMEM((2 * HD, keys), BF),
            pltpu.VMEM((2 * HD, keys), BF),
            pltpu.VMEM((SLOTS, CTX_PAD, 4 * HD), BF),
            pltpu.VMEM((SLOTS, CTX_PAD, 4 * HD), BF),
            pltpu.VMEM((SLOTS, 2 * HD, CTX_PAD), BF),
            pltpu.VMEM((SLOTS, 2 * HD, CTX_PAD), BF),
            pltpu.VMEM((keys, per_step * portion), F32),
            pltpu.VMEM((keys, 2 * HD), F32),
            pltpu.VMEM((keys, 2 * HD), F32),
            pltpu.VMEM(pair_shape, F32),
            pltpu.VMEM(pair_shape, F32),
        ],
        compiler_params=pltpu.CompilerParams(vmem_limit_bytes=VMEM_LIMIT),
        cost_estimate=cost(6e10),
        name="attention",
    )(info, traded, do, traded, *others, ctx)


def rotated(values, axis):
    size = lax.axis_size(axis)
    return [values] + [
        lax.ppermute(values, axis, [(i, (i + d) % size) for i in range(size)])
        for d in range(1, size)
    ]


def gathered(values, axis):
    size = lax.axis_size(axis)
    pieces = rotated(values, axis)[::-1]
    stacked = jnp.stack(pieces + pieces[:-1])
    return lax.dynamic_slice_in_dim(stacked, size - 1 - lax.axis_index(axis), size, 0)


def band_stats(stat, px):
    parts = rotated(stat, "heads")
    mean = sum(part[0] for part in parts) / len(parts)
    spread = sum(part[1] + px * jnp.square(part[0] - mean) for part in parts)
    return jnp.stack([mean, spread])


def band_sums(sums):
    return sum(rotated(sums, "heads"))


def turned(values):
    size = lax.axis_size("heads")
    return lax.ppermute(
        values, SEQ, [(r * size + h, h * size + r) for r in range(size) for h in range(size)]
    )


def after(values, *others):
    return lax.optimization_barrier((values, *others))[0]


def halo(edge_low, edge_high):
    size = lax.axis_size("rows") * lax.axis_size("heads")
    forward = [(i, i + 1) for i in range(size - 1)]
    backward = [(i + 1, i) for i in range(size - 1)]
    return lax.ppermute(edge_high, SEQ, forward), lax.ppermute(edge_low, SEQ, backward)


def edges(values):
    return halo(values[:WID], values[-WID:])


def trade(values):
    return lax.all_to_all(values, SEQ, split_axis=0, concat_axis=0, tiled=True)


def per_device(
    pixels,
    crop_slot,
    embedding,
    context,
    first_gain,
    first_offset,
    first_kernel,
    first_bias,
    embed_weight,
    embed_bias,
    second_gain,
    second_offset,
    second_kernel,
    second_bias,
    attend_gain,
    attend_offset,
    inner_weight,
    inner_bias,
    context_weight,
    context_bias,
    outer_weight,
    outer_bias,
    cotangent,
):
    row_count = pixels.shape[0]
    assert pixels.shape[1] == 1
    ranks = lax.axis_size("rows")
    head_ways = lax.axis_size("heads")
    halves = lax.axis_size("dp")
    ways = ranks * head_ways
    group = ways // NH
    px = row_count * WID
    dims = (px, ways, head_ways)
    rank = lax.axis_index("rows")
    head_rank = lax.axis_index("heads")
    joint = rank * head_ways + head_rank
    shard_heads = NH // head_ways
    span = shard_heads * HD
    square = ranks == head_ways and NH // ranks == shard_heads

    slots = crop_slot[:, 0]
    hier = head_ways == 4
    part_order = [head_rank ^ d if hier else d for d in range(head_ways)]
    info = jnp.concatenate(
        [slots, jnp.stack([rank, joint, lax.axis_index("dp")] + part_order).astype(jnp.int32)]
    )
    split = halves == 2 and hier

    x = pixels.reshape(px, C)
    cot = cotangent.reshape(px, C)

    def row(vector):
        return vector.reshape(1, C)

    bias_rows = jnp.stack(
        [inner_bias[0].reshape(span), jnp.zeros((span,), F32), inner_bias[1].reshape(span)]
    )
    own_inner = jnp.concatenate(
        [
            inner_weight.astype(F32).transpose(1, 0, 2, 3).reshape(3, C, span),
            jnp.pad(bias_rows[:, None], ((0, 0), (0, 7), (0, 0))),
        ],
        axis=1,
    ).reshape(3 * (C + 8), span)
    own_outer = (
        outer_weight.astype(F32)
        .reshape(span, C // span, span)
        .transpose(1, 0, 2)
        .reshape(C, span)
    )
    outer_w = lax.all_gather(own_outer, "heads", axis=0, tiled=False)

    mean = jnp.mean(x, axis=0)
    x_stat = jnp.stack([mean, jnp.sum(jnp.square(x - mean), axis=0)])
    band_stat = band_stats(x_stat, px)
    pays0 = rotated(band_stat, "rows")
    x_halo = edges(x)
    inner_w = lax.all_gather(own_inner, "heads", axis=0, tiled=False)
    first_k = first_kernel.reshape(3, 3 * C, C)
    second_k = second_kernel.reshape(3, 3 * C, C)
    conv1, act1, stat1, x_vec = conv_forward(
        info, x, x_halo, pays0, row(first_gain), row(first_offset), first_k, row(first_bias), None, dims
    )

    ctx_flat = context[0].reshape(SLOTS * CTX_TOK, context.shape[-1])
    ctx_pair = jnp.dot(
        after(ctx_flat, conv1),
        context_weight.reshape(context.shape[-1], 2 * span),
        preferred_element_type=F32,
    ).reshape(SLOTS * CTX_TOK, 2, shard_heads, HD)
    ctx_pair = ctx_pair + jnp.stack([jnp.zeros_like(context_bias), context_bias])
    ctx_pair = ctx_pair.transpose(2, 0, 1, 3).reshape(shard_heads, SLOTS * CTX_TOK, 2 * HD)
    own_head = joint // group
    if square:
        ctx_all, at = turned(ctx_pair), own_head % shard_heads
    else:
        ctx_all, at = lax.all_gather(ctx_pair, "heads", axis=0, tiled=True), own_head
    ctx_own = lax.dynamic_index_in_dim(ctx_all, at, 0, keepdims=False)
    ctx_own = jnp.pad(
        ctx_own.reshape(SLOTS, CTX_TOK, 2 * HD), ((0, 0), (0, CTX_PAD - CTX_TOK), (0, 0))
    )

    embed_act = jax.nn.silu(embedding[0])
    modulation = jnp.dot(after(embed_act, conv1), embed_weight.astype(F32), precision=HIGH) + embed_bias
    own_slot = slots[joint * row_count]
    own_mod = lax.dynamic_index_in_dim(modulation, own_slot, 0, keepdims=True)
    lift = 1.0 + own_mod[:, :C]
    second_scale = row(second_gain) * lift
    second_shift = row(second_offset) * lift + own_mod[:, C:]
    def swapped(values):
        return lax.ppermute(values, "dp", [(0, 1), (1, 0)])

    conv1_halo = edges(conv1)
    pays1 = rotated(band_stats(stat1, px), "rows")
    do_blocks, cot_sum = attended_gradient(cot, outer_w, ways, group)
    pays1[0] = after(pays1[0], do_blocks)
    residual, act2, stat2, vec1 = conv_forward(
        info, conv1, conv1_halo, pays1, second_scale, second_shift, second_k, row(second_bias), x, dims
    )
    do_own = trade(do_blocks)
    acts = [act1, act2]
    band_stat = band_stats(stat2, px)
    band_stat = after(band_stat, ctx_own)
    if split:
        acts += [swapped(act) for act in acts]
        band_stat = after(band_stat, acts[2])

    pays2 = rotated(band_stat, "rows")
    pays2[0] = after(pays2[0], do_own)
    blocks, vec2 = project(
        info, residual, pays2, row(attend_gain), row(attend_offset), inner_w, dims, group
    )
    traded = trade(blocks)
    res_halo = edges(after(residual, blocks))
    cot_halo = edges(after(cot, blocks))
    act_seqs = rotated(after(embed_act, blocks), "dp")
    acts = jnp.stack(acts, axis=1)
    traded, acts, res_halo, cot_halo, act_seqs = lax.optimization_barrier(
        (traded, acts, res_halo, cot_halo, act_seqs)
    )
    ctx_seqs = rotated(after(ctx_flat.astype(F32), traded), "dp")
    portion = px // group
    own_kv = traded[:, :portion]

    def mates(d):
        return [(i, i // group * group + (i % group + d) % group) for i in range(ways)]

    others = [lax.ppermute(own_kv, SEQ, mates(group - d)) for d in range(1, group)]
    acts = lax.all_to_all(after(acts, *others), "heads", split_axis=0, concat_axis=0, tiled=True)
    results = attention(info, traded, do_own, others, ctx_own, group)
    att_own, dq_own = results[:2]
    dkv_parts = list(results[2 : 2 + group])
    ctx_grad = results[2 + group]
    dkv = dkv_parts[0]
    for d in range(1, group):
        dkv = dkv + lax.ppermute(dkv_parts[d], SEQ, mates(d))
    dkv = after(dkv, acts, tuple(ctx_seqs))
    grads = trade(jnp.concatenate([dkv, dq_own], axis=1))

    ctx_grad = after(ctx_grad, dkv)[:, :CTX_TOK].reshape(SLOTS * CTX_TOK, 2 * HD)
    if square:
        ctx_grads = jnp.stack(rotated(ctx_grad, "heads"))
        ctx_order = (head_rank - jnp.arange(head_ways)) % head_ways // group
        ctx_row = jnp.stack(
            [
                jnp.sum(jnp.where((ctx_order == head)[:, None, None], ctx_grads, 0.0), axis=0)
                for head in range(shard_heads)
            ]
        )
        ctx_mine = turned(after(ctx_row, grads))
    else:
        ctx_grads = lax.all_gather(ctx_grad, SEQ, axis=0, tiled=False)
        ctx_grads = jnp.sum(ctx_grads.reshape(NH, group, SLOTS * CTX_TOK, 2 * HD), axis=1)
        ctx_mine = lax.dynamic_slice_in_dim(ctx_grads, head_rank * shard_heads, shard_heads, 0)

    normed_grad, sums2, inner_part = project_back(
        grads, residual, vec2, row(attend_gain), row(attend_offset), inner_w, cot_sum, dims, group
    )

    def far_of(grad):
        if not split:
            return grad
        return [grad[0], swapped(grad[1]), flip(grad[0], 2)]

    def band_of(hops, *waiting):
        if not split:
            return [lax.all_gather(hops[0], "heads", axis=0, tiled=True)]
        mine, other, far = (after(hop, *waiting) if waiting else hop for hop in hops)
        other_far = flip(other, 2)
        return [
            mine,
            flip(mine, 1),
            far,
            flip(far, 1),
            other,
            flip(other, 1),
            other_far,
            flip(other_far, 1),
        ]

    def flip(values, bit):
        return lax.ppermute(values, "heads", [(i, i ^ bit) for i in range(head_ways)])

    ng_halo = edges(normed_grad)
    band_sum = band_sums(sums2)
    pays3 = rotated(band_sum, "rows")
    attended = trade(after(att_own, grads, pays3[-1]))

    def shard_sum(parts):
        return lax.psum_scatter(parts, "heads", scatter_dimension=0, tiled=False)

    inner_sum = shard_sum(inner_part)
    *residual_grad, hidden_grad, sums1 = conv_backward(
        info,
        normed_grad,
        ng_halo,
        residual,
        res_halo,
        vec2,
        row(attend_gain),
        pays3,
        [cot, *cot_halo],
        second_k,
        (conv1, vec1, second_scale, second_shift),
        dims,
        split,
    )
    hg_halo = edges(hidden_grad)
    band_sum = after(band_sums(sums1), attended)
    pays4 = rotated(band_sum, "rows")
    second_hops = far_of([after(grad, band_sum) for grad in residual_grad])
    output, outer_part = output_step(
        after(attended, band_sum, inner_sum), residual, cot, outer_w, row(outer_bias), dims, group
    )
    inner_sum = lax.psum_scatter(inner_sum, "rows", scatter_dimension=0, tiled=True)
    outer_part, pays4[0] = lax.optimization_barrier((outer_part, pays4[0]))
    outer_sum = lax.psum_scatter(
        shard_sum(outer_part), "rows", scatter_dimension=0, tiled=True
    )
    *conv1_grad, pre_grad, sums0 = conv_backward(
        info,
        hidden_grad,
        hg_halo,
        conv1,
        conv1_halo,
        vec1,
        second_scale,
        pays4,
        None,
        first_k,
        (x, x_vec, row(first_gain), row(first_offset)),
        dims,
        split,
    )
    second_band = band_of(second_hops, pre_grad)
    first_hops = far_of(conv1_grad)
    first_band = band_of(first_hops)
    if split:
        second_band[0] = after(second_band[0], tuple(first_hops), first_band[1])

    def kernel_sum(at, band, *waits):
        seqs = [acts, acts] if split else [acts]
        part = kernel_grad(info, seqs, (at, at + 2)[: len(seqs)], band, ranks)
        if not split:
            part = lax.psum_scatter(part, "dp", scatter_dimension=3, tiled=True)
        parts = lax.all_to_all(part, "rows", split_axis=0, concat_axis=0)
        return jnp.sum(after(parts, *waits), axis=0).reshape(3, 3, C // ways, C // halves), part

    second_kernel_grad, second_part = kernel_sum(1, second_band)
    first_kernel_grad, first_part = kernel_sum(0, first_band)
    inner_sum = gathered(sum(rotated(after(inner_sum, second_part), "dp")), "rows")
    outer_sum = gathered(sum(rotated(after(outer_sum, first_part), "dp")), "rows")
    pays5 = rotated(band_sums(after(sums0, first_kernel_grad)), "rows")
    pixels_grad = final_norm(
        info, pre_grad, x, x_vec, row(first_gain), residual_grad, pays5, dims
    )
    inner_sum = inner_sum.reshape(3, GRAD_ROWS, span)
    inner_weight_grad = inner_sum[:, :C].reshape(3, C, shard_heads, HD).transpose(1, 0, 2, 3)
    bias_sum = inner_sum[:, C].reshape(3, shard_heads, HD)
    inner_bias_grad = jnp.stack([bias_sum[0], bias_sum[2]])
    outer_weight_grad = (
        outer_sum
        .reshape(C // span, span, span)
        .transpose(1, 0, 2)
        .reshape(shard_heads, HD, C)
    )

    ctx_mine = (
        ctx_mine.reshape(shard_heads, SLOTS * CTX_TOK, 2, HD)
        .transpose(1, 2, 0, 3)
        .reshape(SLOTS * CTX_TOK, 2 * span)
    )
    mine_seqs = rotated(after(ctx_mine, first_part), "dp")
    context_weight_grad = jnp.dot(
        after(jnp.concatenate(ctx_seqs, axis=0).T, first_part), jnp.concatenate(mine_seqs, axis=0), precision=HIGH
    ).reshape(context.shape[-1], 2, shard_heads, HD)
    context_bias_grad = jnp.sum(sum(mine_seqs), axis=0).reshape(2, shard_heads, HD)[1]

    attend_sums = sum(after(tuple(pays3), first_part))
    band_slots = slots[:: row_count * head_ways]
    band_slots = jnp.stack([band_slots[(rank - d) % ranks] for d in range(ranks)])
    slot_rows = (band_slots[None, :] == jnp.arange(SLOTS)[:, None]).astype(F32)
    late4 = after(tuple(pays4), first_part)
    by_slot = sum(slot_rows[:, d, None, None] * late4[d] for d in range(ranks))
    shift_grad, hat_grad = by_slot[:, 0], by_slot[:, 1]
    mod_lift = 1.0 + modulation[:, :C]
    scale_grad = hat_grad * second_gain + shift_grad * second_offset
    pack = jnp.concatenate(
        [
            attend_sums,
            jnp.stack(
                [
                    jnp.sum(hat_grad * mod_lift, axis=0),
                    jnp.sum(shift_grad * mod_lift, axis=0),
                    jnp.sum(by_slot[:, 2], axis=0),
                ]
            ),
            scale_grad,
            shift_grad,
        ],
        axis=0,
    )
    packs = rotated(pack, "dp")
    vectors = sum(packs)
    mod_grads = jnp.concatenate(
        [jnp.concatenate([p[6 : 6 + SLOTS], p[6 + SLOTS :]], axis=1) for p in packs], axis=0
    )
    embed_bias_grad = jnp.sum(mod_grads, axis=0)
    embed_rows = embed_weight.shape[0] // ways
    embed_cols = 2 * C // halves
    embed_weight_grad = jnp.einsum(
        "ke,kc->ec",
        lax.dynamic_slice_in_dim(jnp.concatenate(act_seqs, axis=0), joint * embed_rows, embed_rows, 1),
        lax.dynamic_slice_in_dim(mod_grads, lax.axis_index("dp") * embed_cols, embed_cols, 1),
        precision=HIGH,
    )
    first_sums = sum(rotated(sum(pays5), "dp"))

    shape = pixels.shape
    return (
        output.reshape(shape),
        pixels_grad.reshape(shape),
        first_sums[1],
        first_sums[0],
        first_kernel_grad,
        first_sums[2],
        embed_weight_grad,
        embed_bias_grad,
        vectors[3],
        vectors[4],
        second_kernel_grad,
        vectors[5],
        vectors[1],
        vectors[0],
        inner_weight_grad,
        inner_bias_grad,
        context_weight_grad,
        context_bias_grad,
        outer_weight_grad,
        vectors[2],
    )


def solution(mesh):
    band = P(SEQ, "dp", None, None)
    kernel_out = P(None, None, SEQ, "dp")
    return jax.shard_map(
        per_device,
        mesh=mesh,
        in_specs=(
            band,
            P(None, "dp"),
            P("dp", None, None),
            P("dp", None, None, None),
            P(),
            P(),
            P(),
            P(),
            P(),
            P(),
            P(),
            P(),
            P(),
            P(),
            P(),
            P(),
            P(None, None, "heads", None),
            P(None, "heads", None),
            P(None, None, "heads", None),
            P("heads", None),
            P("heads", None, None),
            P(),
            band,
        ),
        out_specs=(
            band,
            band,
            P(),
            P(),
            kernel_out,
            P(),
            P(SEQ, "dp"),
            P(),
            P(),
            P(),
            kernel_out,
            P(),
            P(),
            P(),
            P(None, None, "heads", None),
            P(None, "heads", None),
            P(None, None, "heads", None),
            P("heads", None),
            P("heads", None, None),
            P(),
        ),
        check_vma=False,
    )
```
